32 devices in a mesh: req: 8 (over z, y), ctx: 4 (over x, core).
Axes of the slice: x: 2, y: 2, z: 4, core: 2. Of those that a mesh axis runs over, the one named last changes fastest.
Arguments:
- history: bfloat16 [24576, 1024], P(('req', 'ctx')), may hold values from -6 to 6
- block_owner: int32 [1536, 1], P(('req', 'ctx')), may hold values from 0 to 7; in each aligned block of 48 rows (0 to 47, 48 to 95, ...) at most 12 rows name the same one
- candidates: bfloat16 [4096, 1024], P(('req', 'ctx')), may hold values from -6 to 6
- w_kv: bfloat16 [1024, 2048], replicated, may hold values from -0.1875 to 0.1875
- w_qu: bfloat16 [1024, 2048], replicated, may hold values from -0.1875 to 0.1875
- w_out: bfloat16 [1024, 1024], replicated, may hold values from -0.1875 to 0.1875
Outputs:
- scored: bfloat16 [4096, 1024], P(('req', 'ctx'))
The draws below stay inside these ranges and needn't reach their ends.
Inputs may be any that keep to these rules, and one draw needn't show every extreme that they name: `block_owner`: each packed block belongs to one request; among the 48 blocks of one device at most 12 belong to the same request, and that most is reached on some device; every request owns at least one block.
All inputs are finite; a program needn't handle non-finite values.
Results may differ from the reference program's by a relative error of at most 0.0052.
Values may be sent and summed in bfloat16 or wider, within the bound.
No kernel may reach another device: no remote copies, remote signals or barrier semaphores. Data moves between devices by JAX's collectives and lax.ppermute only.
A program may use at most 128 MiB of HBM per device.

```python
import math
import jax
import jax.numpy as jnp
import numpy as np
from jax import lax

D = 1024
HEAD = 128
BLK = 16
NB = 48
CAP = 12
CANDS = 512
REQUESTS = 8
NBLOCKS = 1536
HIST = 24576
N_REQ = 8
N_CTX = 4


def block_levels(stream_key, shape, split, least, largest):
    def one(axis_at, shards_of):
        steps = jax.random.uniform(jax.random.fold_in(jax.random.fold_in(stream_key, 6), axis_at), (shards_of,), jnp.float32, least / len(split), largest / len(split))
        return jnp.repeat(jnp.exp(steps), shape[axis_at] // shards_of).reshape((-1,) + (1,) * (len(shape) - axis_at - 1))

    loudness = one(*split[0])
    for cut in split[1:]:
        loudness = loudness * one(*cut)
    return loudness


def shared_out(own_key, own, number, rows, number_of, top, reach, slope):
    order = jax.random.permutation(own_key, number_of)
    crowded, ordinary = load_shares(number_of, rows * top, reach, slope, True), load_shares(number_of, rows * top, reach, slope, False)
    places = jnp.arange(number_of)

    def named(lengths, rotation):
        used = int((lengths > 0).sum())
        fixed = max(1, used // 4)
        passed = fixed + (places - fixed + rotation * (used - fixed)) % max(1, number_of - fixed)
        return jnp.zeros((number_of,), jnp.int32).at[order[jnp.where(places < fixed, places, passed)]].set(jnp.asarray(lengths, jnp.int32))

    lengths = jnp.where(number % 4 == 0, named(crowded, number // 4), named(ordinary, number - number // 4 - 1))
    mixed = jax.random.permutation(jax.random.fold_in(own, 3), number_of)
    donor, receiver = mixed[0:number_of // 2 * 2:2], mixed[1:number_of // 2 * 2:2]
    room = jnp.minimum(lengths[donor] - 1, reach - lengths[receiver]) // 2
    room = jnp.where((donor == order[0]) | (receiver == order[0]) | (lengths[receiver] == 0), 0, jnp.maximum(room, 0))
    passed = jax.random.randint(jax.random.fold_in(own, 4), (number_of // 2,), 0, 1 << 20) % (room + 1)
    lengths = lengths.at[donor].add(-passed).at[receiver].add(passed)
    items = jnp.searchsorted(jnp.cumsum(lengths), jnp.arange(rows * top), side="right").astype(jnp.int32)
    listing = items.reshape(top, rows).T
    listing = listing[jax.random.permutation(jax.random.fold_in(own, 1), rows)]
    rotation = jax.random.randint(jax.random.fold_in(own, 2), (rows, 1), 0, top)
    return jnp.take_along_axis(listing, (jnp.arange(top)[None, :] + rotation) % top, axis=1)


def load_shares(number_of, total, bound, lean, full):
    portions = [(1 << 20) // math.isqrt(standing ** lean) + 1 for standing in range(1, number_of + 1)]
    largest = bound if full else min(bound, max(-(-total // number_of), total * portions[0] // sum(portions)))
    least = 1 if total - largest >= number_of - 1 else 0
    counts, surplus = [largest] + [least] * (number_of - 1), total - largest - least * (number_of - 1)
    while surplus > 0:
        free = [i for i in range(1, number_of) if counts[i] < largest] or [i for i in range(1, number_of) if counts[i] < bound]
        mass, remaining = sum([portions[i] for i in free]), surplus
        for i in free:
            more = min(bound - counts[i], max(1, remaining * portions[i] // mass), surplus)
            counts[i] = counts[i] + more
            surplus = surplus - more
    return np.array(counts)


def normal_values(own_key, shape, scale, limit, cuts=(), kind=jnp.bfloat16):
    values = jax.random.normal(own_key, shape, jnp.float32) * scale
    if len(cuts) > 0:
        values = block_levels(own_key, shape, cuts, -0.22, 0.18) * values
    return jnp.clip(values, min=-limit, max=limit).astype(kind)


def setup_inputs(seed: int = 0) -> dict:
    seeds = jax.random.split(jax.random.key(seed), 7)
    history = normal_values(seeds[0], (HIST, D), 1.0, 6.0, ((0, 32),))
    block_owner_keys = jax.random.split(jax.random.fold_in(seeds[1], 1), NBLOCKS // NB)
    block_owner_turns = jax.random.permutation(jax.random.fold_in(seeds[1], 3), NBLOCKS // NB)
    block_owner = jax.vmap(lambda own, number: shared_out(jax.random.fold_in(seeds[1], 2), own, number, NB, N_REQ, 1, CAP, 2))(block_owner_keys, block_owner_turns).reshape((NBLOCKS, 1))
    candidates = normal_values(seeds[2], (REQUESTS * CANDS, D), 1.0, 6.0, ((0, 32),))
    w_kv = normal_values(seeds[3], (D, 2 * D), D ** -0.5, 0.1875)
    w_qu = normal_values(seeds[4], (D, 2 * D), D ** -0.5, 0.1875)
    w_out = normal_values(seeds[5], (D, D), D ** -0.5, 0.1875)
    return {"history": history, "block_owner": block_owner, "candidates": candidates, "w_kv": w_kv, "w_qu": w_qu, "w_out": w_out}


key_span = 512

def attend(queries, keys_values):
    count, width = queries.shape
    heads = width // HEAD
    rows = keys_values.shape[0]
    span = key_span if rows % key_span == 0 else rows
    query = queries.astype(jnp.float32).reshape(count, heads, HEAD)
    pieces = keys_values.reshape(rows // span, span, 2, heads, HEAD)
    factor = HEAD ** (-0.5)

    def add_block(total, piece):
        keys = piece[:, 0].astype(jnp.float32)
        values = piece[:, 1].astype(jnp.float32)
        scores = jnp.einsum('qhd,khd->hqk', query, keys) * factor
        weights = jax.nn.silu(scores).astype(jnp.bfloat16).astype(jnp.float32)
        return (total + jnp.einsum('hqk,khd->qhd', weights, values), None)
    total, _ = lax.scan(add_block, jnp.zeros((count, heads, HEAD), jnp.float32), pieces)
    return total.reshape(count, width)

def reference(history, block_owner, candidates, w_kv, w_qu, w_out):
    devices = N_REQ * N_CTX
    raw = jnp.dot(history, w_kv, preferred_element_type=jnp.float32)
    keys_values = jnp.concatenate([jax.nn.silu(raw[:, :D]), raw[:, D:]], axis=1).astype(jnp.bfloat16)
    blocks = keys_values.reshape(devices, NB, BLK * 2 * D)
    owner = block_owner[:, 0].reshape(devices, NB)
    onehot = (owner[:, :, None] == jnp.arange(N_REQ, dtype=jnp.int32)[None, None, :]).astype(jnp.int32)
    rank = lax.optimization_barrier(jnp.sum((jnp.cumsum(onehot, axis=1) - onehot) * onehot, axis=2))
    slot = owner * CAP + rank
    projected = jnp.dot(candidates, w_qu, preferred_element_type=jnp.float32)
    queries = jax.nn.silu(projected[:, :D]).astype(jnp.bfloat16)
    gate = jax.nn.silu(projected[:, D:])

    def per_request(inputs):
        request, query = inputs
        wanted = request * CAP + jnp.arange(CAP, dtype=jnp.int32)
        hit = (slot[:, :, None] == wanted[None, None, :]).astype(jnp.int32)
        index = lax.optimization_barrier(jnp.sum(hit * jnp.arange(NB, dtype=jnp.int32)[None, :, None], axis=1)).astype(jnp.int32)
        valid = lax.optimization_barrier(jnp.sum(hit, axis=1))
        chosen = blocks[jnp.arange(devices, dtype=jnp.int32)[:, None], index]
        chosen = jnp.where(valid[:, :, None] > 0, chosen, jnp.zeros_like(chosen))
        return attend(query, chosen.reshape(devices * CAP * BLK, 2 * D))
    attended = lax.map(per_request, (jnp.arange(N_REQ, dtype=jnp.int32), queries.reshape(N_REQ, CANDS, D)))
    attended = attended.reshape(N_REQ * CANDS, D)
    mean = lax.optimization_barrier(jnp.mean(attended, axis=-1, keepdims=True))
    centred = attended - mean
    variance = lax.optimization_barrier(jnp.mean(centred * centred, axis=-1, keepdims=True))
    mixed = (centred * lax.rsqrt(variance + 1e-05) * gate).astype(jnp.bfloat16)
    result = candidates.astype(jnp.float32) + jnp.dot(mixed, w_out, preferred_element_type=jnp.float32)
    return result.astype(jnp.bfloat16)
```

```python
import functools

import jax
import jax.numpy as jnp
from jax import lax
from jax.experimental import pallas as pl
from jax.experimental.pallas import tpu as pltpu
from jax.sharding import PartitionSpec as P

HEAD = 128
TILE = 256
BF16 = jnp.bfloat16
F32 = jnp.float32


def silu(v):
    h = 0.5 * v
    return h + h * jnp.tanh(h)


def swap(value, axis, mask):
    count = lax.axis_size(axis)
    return lax.ppermute(value, axis, [(i, i ^ mask) for i in range(count)])


def scalar_grid(grid, in_specs, out_specs, scratch_shapes=()):
    return pltpu.PrefetchScalarGridSpec(
        num_scalar_prefetch=1,
        grid=grid,
        in_specs=in_specs,
        out_specs=out_specs,
        scratch_shapes=scratch_shapes,
    )


def cost(flops, moved, transcendentals=0):
    return pl.CostEstimate(
        flops=int(flops), bytes_accessed=int(moved), transcendentals=int(transcendentals)
    )


def query_kernel(_, cand_ref, w_ref, owner_ref, *outs):
    rows = cand_ref.shape[0]
    made = silu(jnp.dot(cand_ref[...], w_ref[...], preferred_element_type=F32)).astype(BF16)
    for k, out in enumerate(outs):

        @pl.when(pl.program_id(0) == k)
        def _(out=out):
            out[:rows, :] = made
            out[rows:, :] = owner_ref[...]


def project_queries(me, candidates, w_qu, owner_rows, parts):
    rows, width = candidates.shape
    cols = width // parts
    extra = owner_rows.shape[0]
    return pl.pallas_call(
        query_kernel,
        grid_spec=scalar_grid(
            (parts,),
            [
                pl.BlockSpec((rows, width), lambda k, m: (0, 0)),
                pl.BlockSpec((width, cols), lambda k, m: (0, k ^ m[0])),
                pl.BlockSpec((extra, cols), lambda k, m: (0, 0)),
            ],
            [pl.BlockSpec((rows + extra, cols), lambda k, m: (0, 0))] * parts,
        ),
        out_shape=[jax.ShapeDtypeStruct((rows + extra, cols), BF16)] * parts,
        cost_estimate=cost(2 * rows * width * width, 2 * width * width + 4 * rows * width),
        name="queries",
    )(me, candidates, w_qu, owner_rows)


def gate_kernel(_, cand_ref, w_ref, out_ref):
    out_ref[0] = silu(jnp.dot(cand_ref[...], w_ref[...], preferred_element_type=F32))


def project_gate(me, candidates, w_qu, parts):
    rows, width = candidates.shape
    cols = width // parts
    return pl.pallas_call(
        gate_kernel,
        grid_spec=scalar_grid(
            (parts,),
            [
                pl.BlockSpec((rows, width), lambda k, m: (0, 0)),
                pl.BlockSpec((width, cols), lambda k, m: (0, parts + (k ^ m[0]))),
            ],
            pl.BlockSpec((1, rows, cols), lambda k, m: (k, 0, 0)),
        ),
        out_shape=jax.ShapeDtypeStruct((parts, rows, cols), F32),
        cost_estimate=cost(2 * rows * width * width, 2 * width * width + 6 * rows * width),
        name="gate",
    )(me, candidates, w_qu)


def keys_values_kernel(first, _, hist_ref, wk_ref, wv_ref, *outs):
    rows = hist_ref.shape[0]
    step = min(rows, 256)
    for k, out in enumerate(outs):

        @pl.when(pl.program_id(0) == k)
        def _(out=out):
            for at in range(0, rows, step):
                part = hist_ref[at : at + step, :]
                keys = silu(jnp.dot(part, wk_ref[...], preferred_element_type=F32))
                out[at : at + step, :HEAD] = keys.astype(BF16)
                values = jnp.dot(part, wv_ref[...], preferred_element_type=F32)
                out[at : at + step, HEAD:] = values.astype(BF16)


def project_keys_values(me, history, w_kv, parts, each, which, ks):
    rows, width = history.shape
    first, count = ks[0], len(ks)
    heads = width // HEAD
    return pl.pallas_call(
        functools.partial(keys_values_kernel, first),
        grid_spec=scalar_grid(
            (count,),
            [
                pl.BlockSpec((rows, width), lambda k, m: (0, 0)),
                pl.BlockSpec(
                    (width, HEAD), lambda k, m: (0, ((k + first) ^ m[0]) * each + which)
                ),
                pl.BlockSpec(
                    (width, HEAD), lambda k, m: (0, heads + ((k + first) ^ m[0]) * each + which)
                ),
            ],
            [pl.BlockSpec((rows, 2 * HEAD), lambda k, m: (0, 0))] * count,
        ),
        out_shape=[jax.ShapeDtypeStruct((rows, 2 * HEAD), BF16)] * count,
        cost_estimate=cost(
            4 * rows * width * HEAD * count,
            2 * rows * width + 4 * width * HEAD * count + 4 * rows * HEAD * count,
        ),
        name=f"keys_values_{which}_{first}",
    )(me, history, w_kv, w_kv)


def attend_kernel(source, sink, events, room, pos_ref, count_ref, *refs):
    codes = len(source)
    n_q = 1 + max(a for a, _ in source)
    n_out = 1 + max(a for a, _ in sink)
    n_kv = len(refs) - n_q - n_out - 2
    kvs, queries = refs[:n_kv], refs[n_kv : n_kv + n_q]
    outs = refs[n_kv + n_q : n_kv + n_q + n_out]
    packed, total = refs[n_kv + n_q + n_out :]
    blocks = kvs[0].shape[0] // events
    cands = total.shape[0]
    half = 0.5 * HEAD ** (-0.5)
    packed[...] = jnp.zeros_like(packed)
    for s, kv in enumerate(kvs):

        def place(b, carry, s=s, kv=kv):
            at = pl.multiple_of(pos_ref[s * blocks + b] * events, events)
            packed[pl.ds(at, events), :] = kv[pl.ds(pl.multiple_of(b * events, events), events), :]
            return carry

        lax.fori_loop(0, blocks, place, 0, unroll=8)
    for code in range(codes):
        array, at = source[code]
        q_ref = queries[array]
        tiles = lax.div(count_ref[code] * events + (TILE - 1), TILE)
        total[...] = jnp.zeros_like(total)

        def add_tile(t, carry, code=code, q_ref=q_ref, at=at):
            row = pl.multiple_of(code * room + t * TILE, TILE)
            keys = packed[pl.ds(row, TILE), :HEAD]
            values = packed[pl.ds(row, TILE), HEAD:]
            scores = lax.dot_general(
                q_ref[at : at + cands, :], keys, (((1,), (1,)), ((), ())),
                preferred_element_type=F32,
            )
            h = scores * half
            weights = (h + h * jnp.tanh(h)).astype(BF16)
            total[...] += jnp.dot(weights, values, preferred_element_type=F32)
            return carry

        lax.fori_loop(0, tiles, add_tile, 0)
        array, at = sink[code]
        outs[array][at : at + cands, :] = total[...].astype(BF16)


def attend(pos, counts, kvs, queries, source, sink, cands, events, room, which):
    codes = len(source)
    sizes = [0] * (1 + max(a for a, _ in sink))
    for array, at in sink:
        sizes[array] = max(sizes[array], at + cands)
    rows = sum(kv.shape[0] for kv in kvs)
    vmem = pl.BlockSpec(memory_space=pltpu.VMEM)
    smem = pl.BlockSpec(memory_space=pltpu.SMEM)
    return pl.pallas_call(
        functools.partial(attend_kernel, source, sink, events, room),
        in_specs=[smem, smem] + [vmem] * (len(kvs) + len(queries)),
        out_specs=[vmem] * len(sizes),
        out_shape=[jax.ShapeDtypeStruct((size, HEAD), BF16) for size in sizes],
        scratch_shapes=[
            pltpu.VMEM((codes * room, 2 * HEAD), BF16),
            pltpu.VMEM((cands, HEAD), F32),
        ],
        cost_estimate=cost(
            8 * rows * cands * HEAD, 4 * rows * HEAD + 4 * codes * cands * HEAD, rows * cands
        ),
        name=f"attend_{which}",
    )(pos, counts, *kvs, *queries)


def finish_kernel(count, _, cand_ref, gate_ref, w_ref, *refs):
    parts, out_ref, stat, total = refs[:count], refs[count], refs[count + 1], refs[count + 2]
    k = pl.program_id(0)
    width = cand_ref.shape[1]

    @pl.when(k == 0)
    def _():
        mean = sum(jnp.sum(p[...].astype(F32), axis=1, keepdims=True) for p in parts) / width
        square = sum(
            jnp.sum(jnp.square(p[...].astype(F32) - mean), axis=1, keepdims=True) for p in parts
        )
        scale = lax.rsqrt(square / width + 1e-05)
        for j, p in enumerate(parts):
            stat[j] = (p[...].astype(F32) - mean) * scale
        total[...] = cand_ref[...].astype(F32)

    mixed = (stat[k] * gate_ref[0]).astype(BF16)
    total[...] += jnp.dot(mixed, w_ref[...], preferred_element_type=F32)

    @pl.when(k == count - 1)
    def _():
        out_ref[...] = total[...].astype(BF16)


def finish(me, candidates, gate, w_out, parts):
    rows, width = candidates.shape
    count = len(parts)
    cols = width // count
    return pl.pallas_call(
        functools.partial(finish_kernel, count),
        grid_spec=scalar_grid(
            (count,),
            [
                pl.BlockSpec((rows, width), lambda k, m: (0, 0)),
                pl.BlockSpec((1, rows, cols), lambda k, m: (k, 0, 0)),
                pl.BlockSpec((cols, width), lambda k, m: (k ^ m[0], 0)),
            ]
            + [pl.BlockSpec((rows, cols), lambda k, m: (0, 0))] * count,
            pl.BlockSpec((rows, width), lambda k, m: (0, 0)),
            [pltpu.VMEM((count, rows, cols), F32), pltpu.VMEM((rows, width), F32)],
        ),
        out_shape=jax.ShapeDtypeStruct((rows, width), BF16),
        cost_estimate=cost(2 * rows * width * width, 2 * width * width + 10 * rows * width),
        name="finish",
    )(me, candidates, gate, w_out, *parts)


def stages(count, inner_first):
    outer = []
    bit = count // 2
    while bit >= 2:
        outer.append(2 * bit - 2)
        bit //= 2
    inner = [1] if count > 1 else []
    held, plan = [0], []

    def step(mask, codes):
        plan.append((mask, tuple(codes)))
        held.extend(c ^ mask for c in codes)

    if inner_first:
        for mask in inner + outer:
            step(mask, list(held))
        return plan
    for mask in outer[:-1]:
        step(mask, list(held))
    early = list(held)
    if outer:
        if inner:
            plan.append((1, tuple(early)))
        step(outer[-1], early)
    late = [c for c in held if c not in early] or early
    if inner:
        plan.append((1, tuple(late)))
    return plan


def joined(pieces):
    return pieces[0] if len(pieces) == 1 else jnp.concatenate(pieces, axis=0)


def gather_queries(own, count, inner_first):
    cands = own.shape[0]
    arrays, where = [own], {0: (0, 0)}
    for mask, codes in stages(count, inner_first):
        pieces = [arrays[where[c][0]][where[c][1] : where[c][1] + cands] for c in codes]
        arrays.append(swap(joined(pieces), "req", mask))
        for j, c in enumerate(codes):
            where[c ^ mask] = (len(arrays) - 1, j * cands)
    return arrays, [where[c] for c in range(count)]


def scatter_layout(count, cands, inner_first):
    plan = stages(count, inner_first)
    sink, groups = {}, []
    for mask, codes in plan:
        groups.append([c ^ mask for c in codes])
        for j, c in enumerate(codes):
            sink[c ^ mask] = (len(groups), j * cands)
    sink[0] = (0, 0)
    return [sink[c] for c in range(count)]


def scatter_sums(arrays, sink, count, cands, inner_first):
    held = {c: arrays[sink[c][0]][sink[c][1] : sink[c][1] + cands] for c in range(count)}
    plan = stages(count, inner_first)
    untouched = set(range(count))
    for number in reversed(range(len(plan))):
        mask, codes = plan[number]
        away = [c ^ mask for c in codes]
        if all(c in untouched for c in away):
            sent = arrays[number + 1]
        else:
            sent = joined([held[c] for c in away])
        got = swap(sent, "req", mask)
        for j, c in enumerate(codes):
            total = held[c].astype(F32) + got[j * cands : (j + 1) * cands].astype(F32)
            held[c] = total.astype(BF16)
            untouched.discard(c)
    return held[0]


def on_device(history, block_owner, candidates, w_kv, w_qu, w_out):
    n_req, n_ctx = lax.axis_size("req"), lax.axis_size("ctx")
    rows, width = history.shape
    blocks = block_owner.shape[0]
    events = rows // blocks
    mine = candidates.shape[0]
    cands = mine * n_ctx
    each = width // HEAD // n_ctx
    cols = each * HEAD
    room = -(-n_ctx * (2 * blocks // n_req) * events // TILE) * TILE
    me_ctx = lax.axis_index("ctx").astype(jnp.int32).reshape(1)
    me_req = lax.axis_index("req").astype(jnp.int32)

    owner_rows = jnp.pad(
        block_owner.reshape(1, blocks).astype(BF16), ((0, 15), (0, cols - blocks))
    )
    made = project_queries(me_ctx, candidates, w_qu, owner_rows, n_ctx)
    arrived = [made[0]] + [swap(made[k], "ctx", k) for k in range(1, n_ctx)]

    far = range(n_ctx // 2, n_ctx)
    near = range(0, n_ctx // 2)
    kvs = []
    for h in range(each):
        sent = project_keys_values(me_ctx, history, w_kv, n_ctx, each, h, list(far))
        got_far = [swap(s, "ctx", k) for s, k in zip(sent, far)]
        kept = project_keys_values(me_ctx, history, w_kv, n_ctx, each, h, list(near))
        got_near = [kept[0]] + [swap(kept[k], "ctx", k) for k in near if k > 0]
        kvs.append(got_near + got_far)

    owners = jnp.concatenate([a[mine, :blocks] for a in arrived]).astype(jnp.int32)
    code = owners ^ me_req
    total_blocks = n_ctx * blocks
    order = jnp.arange(total_blocks, dtype=jnp.int32)
    same = code[:, None] == code[None, :]
    rank = jnp.sum((same & (order[None, :] < order[:, None])).astype(jnp.int32), axis=1)
    pos = code * (room // events) + rank
    counts = jnp.sum(
        (code[None, :] == jnp.arange(n_req, dtype=jnp.int32)[:, None]).astype(jnp.int32), axis=1
    )

    gate = project_gate(me_ctx, candidates, w_qu, n_ctx)

    summed = []
    for h in range(each):
        inner_first = h % 2 == 1
        own = jnp.concatenate([a[:mine, h * HEAD : (h + 1) * HEAD] for a in arrived], axis=0)
        queries, source = gather_queries(own, n_req, inner_first)
        sink = scatter_layout(n_req, cands, False)
        arrays = attend(
            pos, counts, kvs[h], queries, source, sink, cands, events, room, h
        )
        summed.append(scatter_sums(arrays, sink, n_req, cands, False))

    full = jnp.concatenate(summed, axis=1)
    parts = [full[:mine]] + [
        swap(full[k * mine : (k + 1) * mine], "ctx", k) for k in range(1, n_ctx)
    ]
    return finish(me_ctx, candidates, gate, w_out, parts)


def solution(mesh):
    placed = (
        P(("req", "ctx"), None),
        P(("req", "ctx"), None),
        P(("req", "ctx"), None),
        P(),
        P(),
        P(),
    )
    return jax.shard_map(
        on_device, mesh=mesh, in_specs=placed, out_specs=P(("req", "ctx"), None), check_vma=False
    )
```

```python
import functools

import jax
import jax.numpy as jnp
from jax import lax
from jax.experimental import pallas as pl
from jax.experimental.pallas import tpu as pltpu
from jax.sharding import PartitionSpec as P


HEAD = 128
TILE = 256
BF16 = jnp.bfloat16
F32 = jnp.float32


def silu(v):
    h = 0.5 * v
    return h + h * jnp.tanh(h)


def swap(value, axis, mask):
    count = lax.axis_size(axis)
    return lax.ppermute(value, axis, [(i, i ^ mask) for i in range(count)])


def scalar_grid(grid, in_specs, out_specs, scratch_shapes=()):
    return pltpu.PrefetchScalarGridSpec(
        num_scalar_prefetch=1,
        grid=grid,
        in_specs=in_specs,
        out_specs=out_specs,
        scratch_shapes=scratch_shapes,
    )


def cost(flops, moved, transcendentals=0):
    return pl.CostEstimate(
        flops=int(flops), bytes_accessed=int(moved), transcendentals=int(transcendentals)
    )


def query_kernel(_, cand_ref, w_ref, owner_ref, *outs):
    rows = cand_ref.shape[0]
    made = silu(jnp.dot(cand_ref[...], w_ref[...], preferred_element_type=F32)).astype(BF16)
    for k, out in enumerate(outs):

        @pl.when(pl.program_id(0) == k)
        def _(out=out):
            out[:rows, :] = made
            out[rows:, :] = owner_ref[...]


def project_queries(me, candidates, w_qu, owner_rows, parts):
    rows, width = candidates.shape
    cols = width // parts
    extra = owner_rows.shape[0]
    return pl.pallas_call(
        query_kernel,
        grid_spec=scalar_grid(
            (parts,),
            [
                pl.BlockSpec((rows, width), lambda k, m: (0, 0)),
                pl.BlockSpec((width, cols), lambda k, m: (0, k ^ m[0])),
                pl.BlockSpec((extra, cols), lambda k, m: (0, 0)),
            ],
            [pl.BlockSpec((rows + extra, cols), lambda k, m: (0, 0))] * parts,
        ),
        out_shape=[jax.ShapeDtypeStruct((rows + extra, cols), BF16)] * parts,
        cost_estimate=cost(2 * rows * width * width, 2 * width * width + 4 * rows * width),
        name="queries",
    )(me, candidates, w_qu, owner_rows)


def gate_kernel(_, cand_ref, w_ref, out_ref):
    out_ref[0] = silu(jnp.dot(cand_ref[...], w_ref[...], preferred_element_type=F32))


def project_gate(me, candidates, w_qu, parts):
    rows, width = candidates.shape
    cols = width // parts
    return pl.pallas_call(
        gate_kernel,
        grid_spec=scalar_grid(
            (parts,),
            [
                pl.BlockSpec((rows, width), lambda k, m: (0, 0)),
                pl.BlockSpec((width, cols), lambda k, m: (0, parts + (k ^ m[0]))),
            ],
            pl.BlockSpec((1, rows, cols), lambda k, m: (k, 0, 0)),
        ),
        out_shape=jax.ShapeDtypeStruct((parts, rows, cols), F32),
        cost_estimate=cost(2 * rows * width * width, 2 * width * width + 6 * rows * width),
        name="gate",
    )(me, candidates, w_qu)


def keys_values_kernel(_, hist_ref, wk_ref, wv_ref, *outs):
    rows = hist_ref.shape[0]
    step = min(rows, 256)
    for k, out in enumerate(outs):

        @pl.when(pl.program_id(0) == k)
        def _(out=out):
            for at in range(0, rows, step):
                part = hist_ref[at : at + step, :]
                keys = silu(jnp.dot(part, wk_ref[...], preferred_element_type=F32))
                out[at : at + step, :HEAD] = keys.astype(BF16)
                values = jnp.dot(part, wv_ref[...], preferred_element_type=F32)
                out[at : at + step, HEAD:] = values.astype(BF16)


def project_keys_values(me, history, w_kv, each, which, ks):
    rows, width = history.shape
    first, count = ks[0], len(ks)
    heads = width // HEAD
    return pl.pallas_call(
        keys_values_kernel,
        grid_spec=scalar_grid(
            (count,),
            [
                pl.BlockSpec((rows, width), lambda k, m: (0, 0)),
                pl.BlockSpec(
                    (width, HEAD), lambda k, m: (0, ((k + first) ^ m[0]) * each + which)
                ),
                pl.BlockSpec(
                    (width, HEAD), lambda k, m: (0, heads + ((k + first) ^ m[0]) * each + which)
                ),
            ],
            [pl.BlockSpec((rows, 2 * HEAD), lambda k, m: (0, 0))] * count,
        ),
        out_shape=[jax.ShapeDtypeStruct((rows, 2 * HEAD), BF16)] * count,
        cost_estimate=cost(
            4 * rows * width * HEAD * count,
            2 * rows * width + 4 * width * HEAD * count + 4 * rows * HEAD * count,
        ),
    )(me, history, w_kv, w_kv)


def attend_kernel(source, sink, events, room, pos_ref, count_ref, code_ref, *refs):
    codes = len(source)
    n_q = 1 + max(a for a, _ in source)
    n_out = 1 + max(a for a, _ in sink)
    n_kv = len(refs) - n_q - n_out - 3
    kvs, queries = refs[:n_kv], refs[n_kv : n_kv + n_q]
    outs = refs[n_kv + n_q : n_kv + n_q + n_out]
    packed, asked, total = refs[n_kv + n_q + n_out :]
    blocks = kvs[0].shape[0] // events
    cands = asked.shape[0] // codes
    half = 0.5 * HEAD ** (-0.5)
    packed[...] = jnp.zeros_like(packed)
    for s, kv in enumerate(kvs):

        def place(b, carry, s=s, kv=kv):
            at = pl.multiple_of(pos_ref[s * blocks + b] * events, events)
            packed[pl.ds(at, events), :] = kv[pl.ds(pl.multiple_of(b * events, events), events), :]
            return carry

        lax.fori_loop(0, blocks, place, 0, unroll=8)
    for j, (array, at) in enumerate(source):
        asked[j * cands : (j + 1) * cands, :] = queries[array][at : at + cands, :]

    def one_code(j, carry):
        code = code_ref[j]
        base = pl.multiple_of(code * room, TILE)
        rows = pl.ds(pl.multiple_of(j * cands, cands), cands)
        tiles = lax.div(count_ref[code] * events + (TILE - 1), TILE)
        for number in range(room // TILE + 1):

            @pl.when(tiles == number)
            def _(number=number):
                if number == 0:
                    total[rows, :] = jnp.zeros((cands, HEAD), BF16)
                    return
                sums = None
                for t in range(number):
                    at = pl.ds(base + t * TILE, TILE)
                    scores = lax.dot_general(
                        asked[rows, :],
                        packed[at, :HEAD],
                        (((1,), (1,)), ((), ())),
                        preferred_element_type=F32,
                    )
                    h = scores * half
                    weights = (h + h * jnp.tanh(h)).astype(BF16)
                    part = jnp.dot(weights, packed[at, HEAD:], preferred_element_type=F32)
                    sums = part if sums is None else sums + part
                total[rows, :] = sums.astype(BF16)

        return carry

    lax.fori_loop(0, codes, one_code, 0)
    for j, (array, at) in enumerate(sink):
        outs[array][at : at + cands, :] = total[j * cands : (j + 1) * cands, :]


def attend(pos, counts, kvs, arrays, where, groups, cands, events, room):
    codes = [c for group in groups for c in group]
    sink = [(g, j * cands) for g, group in enumerate(groups) for j in range(len(group))]
    used = sorted({where[c][0] for c in codes})
    source = [(used.index(where[c][0]), where[c][1]) for c in codes]
    queries = [arrays[a] for a in used]
    rows = sum(kv.shape[0] for kv in kvs)
    n_req = counts.shape[0]
    share = len(codes) / n_req
    vmem = pl.BlockSpec(memory_space=pltpu.VMEM)
    smem = pl.BlockSpec(memory_space=pltpu.SMEM)
    return pl.pallas_call(
        functools.partial(attend_kernel, source, sink, events, room),
        in_specs=[smem] * 3 + [vmem] * (len(kvs) + len(queries)),
        out_specs=[vmem] * len(groups),
        out_shape=[jax.ShapeDtypeStruct((len(g) * cands, HEAD), BF16) for g in groups],
        scratch_shapes=[
            pltpu.VMEM((n_req * room, 2 * HEAD), BF16),
            pltpu.VMEM((len(codes) * cands, HEAD), BF16),
            pltpu.VMEM((len(codes) * cands, HEAD), BF16),
        ],
        cost_estimate=cost(
            8 * rows * cands * HEAD * share,
            4 * rows * HEAD + 4 * len(codes) * cands * HEAD,
            rows * cands * share,
        ),
    )(pos, counts, jnp.array(codes, dtype=jnp.int32), *kvs, *queries)


def finish_kernel(count, _, cand_ref, gate_ref, w_ref, *refs):
    parts, out_ref, stat, total = refs[:count], refs[count], refs[count + 1], refs[count + 2]
    k = pl.program_id(0)
    width = cand_ref.shape[1]

    @pl.when(k == 0)
    def _():
        mean = sum(jnp.sum(p[...].astype(F32), axis=1, keepdims=True) for p in parts) / width
        square = sum(
            jnp.sum(jnp.square(p[...].astype(F32) - mean), axis=1, keepdims=True) for p in parts
        )
        scale = lax.rsqrt(square / width + 1e-05)
        for j, p in enumerate(parts):
            stat[j] = (p[...].astype(F32) - mean) * scale
        total[...] = cand_ref[...].astype(F32)

    mixed = (stat[k] * gate_ref[0]).astype(BF16)
    total[...] += jnp.dot(mixed, w_ref[...], preferred_element_type=F32)

    @pl.when(k == count - 1)
    def _():
        out_ref[...] = total[...].astype(BF16)


def finish(me, candidates, gate, w_out, parts):
    rows, width = candidates.shape
    count = len(parts)
    cols = width // count
    return pl.pallas_call(
        functools.partial(finish_kernel, count),
        grid_spec=scalar_grid(
            (count,),
            [
                pl.BlockSpec((rows, width), lambda k, m: (0, 0)),
                pl.BlockSpec((1, rows, cols), lambda k, m: (k, 0, 0)),
                pl.BlockSpec((cols, width), lambda k, m: (k ^ m[0], 0)),
            ]
            + [pl.BlockSpec((rows, cols), lambda k, m: (0, 0))] * count,
            pl.BlockSpec((rows, width), lambda k, m: (0, 0)),
            [pltpu.VMEM((count, rows, cols), F32), pltpu.VMEM((rows, width), F32)],
        ),
        out_shape=jax.ShapeDtypeStruct((rows, width), BF16),
        cost_estimate=cost(2 * rows * width * width, 2 * width * width + 10 * rows * width),
        name="finish",
    )(me, candidates, gate, w_out, *parts)


def stages(count, inner_first):
    outer = []
    bit = count // 2
    while bit >= 2:
        outer.append(2 * bit - 2)
        bit //= 2
    inner = [1] if count > 1 else []
    held, plan = [0], []

    def step(mask, codes):
        plan.append((mask, tuple(codes)))
        held.extend(c ^ mask for c in codes)

    if inner_first:
        for mask in inner + outer:
            step(mask, list(held))
        return plan
    for mask in outer[:-1]:
        step(mask, list(held))
    early = list(held)
    if outer:
        if inner:
            plan.append((1, tuple(early)))
        step(outer[-1], early)
    late = [c for c in held if c not in early] or early
    if inner:
        plan.append((1, tuple(late)))
    return plan


def joined(pieces):
    return pieces[0] if len(pieces) == 1 else jnp.concatenate(pieces, axis=0)


def gather_queries(own, count, inner_first):
    cands = own.shape[0]
    arrays, where = [own], {0: (0, 0)}
    for mask, codes in stages(count, inner_first):
        pieces = [arrays[where[c][0]][where[c][1] : where[c][1] + cands] for c in codes]
        arrays.append(swap(joined(pieces), "req", mask))
        for j, c in enumerate(codes):
            where[c ^ mask] = (len(arrays) - 1, j * cands)
    return arrays, where


def scatter_sums(groups, arrays, count, cands):
    whole = {tuple(g): a for g, a in zip(groups, arrays)}
    held = {}
    for group, array in zip(groups, arrays):
        for j, c in enumerate(group):
            held[c] = array[j * cands : (j + 1) * cands]
    plan = stages(count, False)
    for number in reversed(range(len(plan))):
        mask, codes = plan[number]
        away = tuple(c ^ mask for c in codes)
        sent = whole[away] if away in whole else joined([held[c] for c in away])
        got = swap(sent, "req", mask)
        whole = {g: a for g, a in whole.items() if not set(g) & set(codes)}
        for j, c in enumerate(codes):
            part = held[c].astype(F32) + got[j * cands : (j + 1) * cands].astype(F32)
            held[c] = part.astype(BF16)
    return held[0]


def on_device(history, block_owner, candidates, w_kv, w_qu, w_out):
    n_req, n_ctx = lax.axis_size("req"), lax.axis_size("ctx")
    rows, width = history.shape
    blocks = block_owner.shape[0]
    events = rows // blocks
    mine = candidates.shape[0]
    cands = mine * n_ctx
    each = width // HEAD // n_ctx
    cols = each * HEAD
    room = -(-n_ctx * (2 * blocks // n_req) * events // TILE) * TILE
    me_ctx = lax.axis_index("ctx").astype(jnp.int32).reshape(1)
    me_req = lax.axis_index("req").astype(jnp.int32)

    owner_rows = jnp.pad(
        block_owner.reshape(1, blocks).astype(BF16), ((0, 15), (0, cols - blocks))
    )
    made = project_queries(me_ctx, candidates, w_qu, owner_rows, n_ctx)
    arrived = [made[0]] + [swap(made[k], "ctx", k) for k in range(1, n_ctx)]

    far = range(n_ctx // 2, n_ctx)
    near = range(0, n_ctx // 2)
    kvs = []
    for h in range(each):
        sent = project_keys_values(me_ctx, history, w_kv, each, h, list(far))
        got_far = [swap(s, "ctx", k) for s, k in zip(sent, far)]
        kept = project_keys_values(me_ctx, history, w_kv, each, h, list(near))
        got_near = [kept[0]] + [swap(kept[k], "ctx", k) for k in near if k > 0]
        kvs.append(got_near + got_far)

    owners = jnp.concatenate([a[mine, :blocks] for a in arrived]).astype(jnp.int32)
    code = owners ^ me_req
    total_blocks = n_ctx * blocks
    order = jnp.arange(total_blocks, dtype=jnp.int32)
    same = code[:, None] == code[None, :]
    rank = jnp.sum((same & (order[None, :] < order[:, None])).astype(jnp.int32), axis=1)
    pos = code * (room // events) + rank
    counts = jnp.sum(
        (code[None, :] == jnp.arange(n_req, dtype=jnp.int32)[:, None]).astype(jnp.int32), axis=1
    )

    gate = project_gate(me_ctx, candidates, w_qu, n_ctx)

    plan = stages(n_req, False)
    groups = [[c ^ mask for c in codes] for mask, codes in plan] + [[0]]
    summed = []
    for h in range(each):
        own = jnp.concatenate([a[:mine, h * HEAD : (h + 1) * HEAD] for a in arrived], axis=0)
        arrays, where = gather_queries(own, n_req, h % 2 == 1)
        last = len(plan) - 1
        if h == 0:
            calls = [[i for i in range(len(groups)) if i != last], [last]]
        else:
            calls = [[i for i in range(len(plan)) if plan[i][0] == 1]]
            calls.append([i for i in range(len(groups)) if i not in calls[0]])
        sums = {}
        for call in calls:
            if call:
                made = attend(
                    pos, counts, kvs[h], arrays, where, [groups[i] for i in call],
                    cands, events, room,
                )
                sums.update(zip(call, made))
        summed.append(scatter_sums(groups, [sums[i] for i in range(len(groups))], n_req, cands))

    full = jnp.concatenate(summed, axis=1)
    parts = [full[:mine]] + [
        swap(full[k * mine : (k + 1) * mine], "ctx", k) for k in range(1, n_ctx)
    ]
    return finish(me_ctx, candidates, gate, w_out, parts)


def solution(mesh):
    placed = (
        P(("req", "ctx"), None),
        P(("req", "ctx"), None),
        P(("req", "ctx"), None),
        P(),
        P(),
        P(),
    )
    return jax.shard_map(
        on_device, mesh=mesh, in_specs=placed, out_specs=P(("req", "ctx"), None), check_vma=False
    )
```

```python
import functools

import jax
import jax.numpy as jnp
from jax import lax
from jax.experimental import pallas as pl
from jax.experimental.pallas import tpu as pltpu
from jax.sharding import PartitionSpec as P


HEAD = 128
TILE = 256
BF16 = jnp.bfloat16
F32 = jnp.float32


def silu(v):
    h = 0.5 * v
    return h + h * jnp.tanh(h)


def swap(value, axis, mask):
    count = lax.axis_size(axis)
    return lax.ppermute(value, axis, [(i, i ^ mask) for i in range(count)])


def scalar_grid(grid, in_specs, out_specs, scratch_shapes=()):
    return pltpu.PrefetchScalarGridSpec(
        num_scalar_prefetch=1,
        grid=grid,
        in_specs=in_specs,
        out_specs=out_specs,
        scratch_shapes=scratch_shapes,
    )


def cost(flops, moved, transcendentals=0):
    return pl.CostEstimate(
        flops=int(flops), bytes_accessed=int(moved), transcendentals=int(transcendentals)
    )


def query_kernel(me_ref, cand_ref, w_ref, owner_ref, *refs):
    outs, made = refs[:-1], refs[-1]
    rows = cand_ref.shape[0]
    cols = outs[0].shape[1]
    blocks = owner_ref.shape[0]
    projected = jnp.dot(cand_ref[...], w_ref[...], preferred_element_type=F32)
    made[...] = silu(projected).astype(BF16)
    owners = jnp.broadcast_to(owner_ref[...].astype(F32), (blocks, cols)).astype(BF16)
    for k, out in enumerate(outs):
        at = pl.multiple_of((k ^ me_ref[0]) * cols, cols)
        out[:rows, :] = made[:, pl.ds(at, cols)]
        out[rows:, :] = owners


def project_queries(me, candidates, w_qu, block_owner, parts):
    rows, width = candidates.shape
    cols = width // parts
    blocks = block_owner.shape[0]
    return pl.pallas_call(
        query_kernel,
        grid_spec=scalar_grid(
            (1,),
            [
                pl.BlockSpec((rows, width), lambda i, m: (0, 0)),
                pl.BlockSpec((width, width), lambda i, m: (0, 0)),
                pl.BlockSpec((blocks, 1), lambda i, m: (0, 0)),
            ],
            [pl.BlockSpec((rows + blocks, cols), lambda i, m: (0, 0))] * parts,
            [pltpu.VMEM((rows, width), BF16)],
        ),
        out_shape=[jax.ShapeDtypeStruct((rows + blocks, cols), BF16)] * parts,
        cost_estimate=cost(2 * rows * width * width, 2 * width * width + 4 * rows * width),
        name="queries",
    )(me, candidates, w_qu, block_owner)


def gate_kernel(_, cand_ref, w_ref, out_ref):
    out_ref[0] = silu(jnp.dot(cand_ref[...], w_ref[...], preferred_element_type=F32))


def project_gate(me, candidates, w_qu, parts):
    rows, width = candidates.shape
    cols = width // parts
    return pl.pallas_call(
        gate_kernel,
        grid_spec=scalar_grid(
            (parts,),
            [
                pl.BlockSpec((rows, width), lambda k, m: (0, 0)),
                pl.BlockSpec((width, cols), lambda k, m: (0, parts + (k ^ m[0]))),
            ],
            pl.BlockSpec((1, rows, cols), lambda k, m: (k, 0, 0)),
        ),
        out_shape=jax.ShapeDtypeStruct((parts, rows, cols), F32),
        cost_estimate=cost(2 * rows * width * width, 2 * width * width + 6 * rows * width),
        name="gate",
    )(me, candidates, w_qu)


def keys_values_kernel(count, each, _, hist_ref, *refs):
    weights, outs = refs[: 2 * count], refs[2 * count :]
    for k in range(count):
        keys = silu(jnp.dot(hist_ref[...], weights[2 * k][...], preferred_element_type=F32))
        values = jnp.dot(hist_ref[...], weights[2 * k + 1][...], preferred_element_type=F32)
        for h in range(each):
            out = outs[k * each + h]
            out[:, :HEAD] = keys[:, h * HEAD : (h + 1) * HEAD].astype(BF16)
            out[:, HEAD:] = values[:, h * HEAD : (h + 1) * HEAD].astype(BF16)


def project_keys_values(me, history, w_kv, parts, ks):
    rows, width = history.shape
    cols = width // parts
    each = cols // HEAD
    count = len(ks)
    step = rows // 2

    def weight(k, side):
        return pl.BlockSpec((width, cols), lambda r, m: (0, side * parts + (k ^ m[0])))

    made = pl.pallas_call(
        functools.partial(keys_values_kernel, count, each),
        grid_spec=scalar_grid(
            (rows // step,),
            [pl.BlockSpec((step, width), lambda r, m: (r, 0))]
            + [weight(k, side) for k in ks for side in range(2)],
            [pl.BlockSpec((step, 2 * HEAD), lambda r, m: (r, 0))] * (count * each),
        ),
        out_shape=[jax.ShapeDtypeStruct((rows, 2 * HEAD), BF16)] * (count * each),
        cost_estimate=cost(
            4 * rows * width * cols * count,
            2 * rows * width + 4 * width * cols * count + 4 * rows * cols * count,
        ),
    )(me, history, *[w_kv] * (2 * count))
    return [made[k * each : (k + 1) * each] for k in range(count)]


def attend_kernel(source, sink, events, room, pos_ref, count_ref, code_ref, *refs):
    codes = len(source)
    n_q = 1 + max(a for a, _ in source)
    n_out = 1 + max(a for a, _ in sink)
    n_kv = len(refs) - n_q - n_out - 3
    kvs, queries = refs[:n_kv], refs[n_kv : n_kv + n_q]
    outs = refs[n_kv + n_q : n_kv + n_q + n_out]
    packed, asked, total = refs[n_kv + n_q + n_out :]
    blocks = kvs[0].shape[0] // events
    cands = asked.shape[0] // codes
    half = 0.5 * HEAD ** (-0.5)

    def code_tiles(j):
        return lax.div(count_ref[code_ref[j]] * events + (TILE - 1), TILE)

    for j in range(codes):
        at = code_ref[j] * room + (lax.max(code_tiles(j), 1) - 1) * TILE
        packed[pl.ds(pl.multiple_of(at, TILE), TILE), :] = jnp.zeros((TILE, 2 * HEAD), BF16)
    for s, kv in enumerate(kvs):

        def place(b, carry, s=s, kv=kv):
            at = pl.multiple_of(pos_ref[s * blocks + b] * events, events)
            packed[pl.ds(at, events), :] = kv[pl.ds(pl.multiple_of(b * events, events), events), :]
            return carry

        lax.fori_loop(0, blocks, place, 0, unroll=8)
    for j, (array, at) in enumerate(source):
        asked[j * cands : (j + 1) * cands, :] = queries[array][at : at + cands, :]

    def one_code(j, carry):
        code = code_ref[j]
        base = pl.multiple_of(code * room, TILE)
        rows = pl.ds(pl.multiple_of(j * cands, cands), cands)
        tiles = code_tiles(j)
        for number in range(room // TILE + 1):

            @pl.when(tiles == number)
            def _(number=number):
                if number == 0:
                    total[rows, :] = jnp.zeros((cands, HEAD), BF16)
                    return
                sums = None
                for t in range(number):
                    at = pl.ds(base + t * TILE, TILE)
                    scores = lax.dot_general(
                        asked[rows, :],
                        packed[at, :HEAD],
                        (((1,), (1,)), ((), ())),
                        preferred_element_type=F32,
                    )
                    h = scores * half
                    weights = (h + h * jnp.tanh(h)).astype(BF16)
                    part = jnp.dot(weights, packed[at, HEAD:], preferred_element_type=F32)
                    sums = part if sums is None else sums + part
                total[rows, :] = sums.astype(BF16)

        return carry

    lax.fori_loop(0, codes, one_code, 0)
    for j, (array, at) in enumerate(sink):
        outs[array][at : at + cands, :] = total[j * cands : (j + 1) * cands, :]


def attend(pos, counts, kvs, arrays, where, groups, cands, events, room):
    codes = [c for group in groups for c in group]
    sink = [(g, j * cands) for g, group in enumerate(groups) for j in range(len(group))]
    used = sorted({where[c][0] for c in codes})
    source = [(used.index(where[c][0]), where[c][1]) for c in codes]
    queries = [arrays[a] for a in used]
    rows = sum(kv.shape[0] for kv in kvs)
    n_req = counts.shape[0]
    share = len(codes) / n_req
    vmem = pl.BlockSpec(memory_space=pltpu.VMEM)
    smem = pl.BlockSpec(memory_space=pltpu.SMEM)
    return pl.pallas_call(
        functools.partial(attend_kernel, source, sink, events, room),
        in_specs=[smem] * 3 + [vmem] * (len(kvs) + len(queries)),
        out_specs=[vmem] * len(groups),
        out_shape=[jax.ShapeDtypeStruct((len(g) * cands, HEAD), BF16) for g in groups],
        scratch_shapes=[
            pltpu.VMEM((n_req * room, 2 * HEAD), BF16),
            pltpu.VMEM((len(codes) * cands, HEAD), BF16),
            pltpu.VMEM((len(codes) * cands, HEAD), BF16),
        ],
        cost_estimate=cost(
            8 * rows * cands * HEAD * share,
            4 * rows * HEAD + 4 * len(codes) * cands * HEAD,
            rows * cands * share,
        ),
    )(pos, counts, jnp.array(codes, dtype=jnp.int32), *kvs, *queries)


def finish_kernel(me_ref, cand_ref, gate_ref, w_ref, *refs):
    parts, out_ref = refs[:-1], refs[-1]
    width = cand_ref.shape[1]
    cols = parts[0].shape[1]
    values = [p[...].astype(F32) for p in parts]
    mean = sum(jnp.sum(v, axis=1, keepdims=True) for v in values) / width
    values = [v - mean for v in values]
    square = sum(jnp.sum(v * v, axis=1, keepdims=True) for v in values)
    scale = lax.rsqrt(square / width + 1e-05)
    total = cand_ref[...].astype(F32)
    for k, v in enumerate(values):
        mixed = (v * scale * gate_ref[k]).astype(BF16)
        rows = pl.ds(pl.multiple_of((k ^ me_ref[0]) * cols, cols), cols)
        total += jnp.dot(mixed, w_ref[rows, :], preferred_element_type=F32)
    out_ref[...] = total.astype(BF16)


def finish(me, candidates, gate, w_out, parts):
    rows, width = candidates.shape
    vmem = pl.BlockSpec(memory_space=pltpu.VMEM)
    return pl.pallas_call(
        finish_kernel,
        in_specs=[pl.BlockSpec(memory_space=pltpu.SMEM)] + [vmem] * (3 + len(parts)),
        out_specs=vmem,
        out_shape=jax.ShapeDtypeStruct((rows, width), BF16),
        cost_estimate=cost(2 * rows * width * width, 2 * width * width + 10 * rows * width),
        name="finish",
    )(me, candidates, gate, w_out, *parts)


def stages(count, inner_first):
    outer = []
    bit = count // 2
    while bit >= 2:
        outer.append(2 * bit - 2)
        bit //= 2
    inner = [1] if count > 1 else []
    held, plan = [0], []

    def step(mask, codes):
        plan.append((mask, tuple(codes)))
        held.extend(c ^ mask for c in codes)

    if inner_first:
        for mask in inner + outer:
            step(mask, list(held))
        return plan
    for mask in outer[:-1]:
        step(mask, list(held))
    early = list(held)
    if outer:
        if inner:
            plan.append((1, tuple(early)))
        step(outer[-1], early)
    late = [c for c in held if c not in early] or early
    if inner:
        plan.append((1, tuple(late)))
    return plan


def joined(pieces):
    return pieces[0] if len(pieces) == 1 else jnp.concatenate(pieces, axis=0)


def gather_queries(own, count, inner_first):
    cands = own.shape[0]
    arrays, where = [own], {0: (0, 0)}
    for mask, codes in stages(count, inner_first):
        pieces = [arrays[where[c][0]][where[c][1] : where[c][1] + cands] for c in codes]
        arrays.append(swap(joined(pieces), "req", mask))
        for j, c in enumerate(codes):
            where[c ^ mask] = (len(arrays) - 1, j * cands)
    return arrays, where


def scatter_sums(groups, arrays, count, cands):
    whole = {tuple(g): a for g, a in zip(groups, arrays)}
    held = {}
    for group, array in zip(groups, arrays):
        for j, c in enumerate(group):
            held[c] = array[j * cands : (j + 1) * cands]
    plan = stages(count, False)
    for number in reversed(range(len(plan))):
        mask, codes = plan[number]
        away = tuple(c ^ mask for c in codes)
        sent = whole[away] if away in whole else joined([held[c] for c in away])
        got = swap(sent, "req", mask)
        whole = {g: a for g, a in whole.items() if not set(g) & set(codes)}
        for j, c in enumerate(codes):
            part = held[c].astype(F32) + got[j * cands : (j + 1) * cands].astype(F32)
            held[c] = part.astype(BF16)
    return held[0]


def on_device(history, block_owner, candidates, w_kv, w_qu, w_out):
    n_req, n_ctx = lax.axis_size("req"), lax.axis_size("ctx")
    rows, width = history.shape
    blocks = block_owner.shape[0]
    events = rows // blocks
    mine = candidates.shape[0]
    cands = mine * n_ctx
    each = width // HEAD // n_ctx
    room = -(-n_ctx * (2 * blocks // n_req) * events // TILE) * TILE
    me_ctx = lax.axis_index("ctx").astype(jnp.int32).reshape(1)
    me_req = lax.axis_index("req").astype(jnp.int32)

    made = project_queries(me_ctx, candidates, w_qu, block_owner, n_ctx)
    arrived = [made[0]] + [swap(made[k], "ctx", k) for k in range(1, n_ctx)]

    far = list(range(n_ctx // 2, n_ctx))
    near = list(range(0, n_ctx // 2))
    made_far = project_keys_values(me_ctx, history, w_kv, n_ctx, far)
    made_near = project_keys_values(me_ctx, history, w_kv, n_ctx, near)
    kvs = []
    for h in range(each):
        kvs.append(
            [
                heads[h] if k == 0 else swap(heads[h], "ctx", k)
                for k, heads in zip(near + far, made_near + made_far)
            ]
        )

    owners = jnp.concatenate([a[mine:, 0] for a in arrived]).astype(jnp.int32)
    code = owners ^ me_req
    total_blocks = n_ctx * blocks
    order = jnp.arange(total_blocks, dtype=jnp.int32)
    same = code[:, None] == code[None, :]
    rank = jnp.sum((same & (order[None, :] < order[:, None])).astype(jnp.int32), axis=1)
    pos = code * (room // events) + rank
    counts = jnp.sum(
        (code[None, :] == jnp.arange(n_req, dtype=jnp.int32)[:, None]).astype(jnp.int32), axis=1
    )

    gate = project_gate(me_ctx, candidates, w_qu, n_ctx)

    plan = stages(n_req, False)
    groups = [[c ^ mask for c in codes] for mask, codes in plan] + [[0]]
    summed = []
    for h in range(each):
        own = jnp.concatenate([a[:mine, h * HEAD : (h + 1) * HEAD] for a in arrived], axis=0)
        arrays, where = gather_queries(own, n_req, h % 2 == 1)
        last = len(plan) - 1
        if h == 0:
            calls = [[i for i in range(len(groups)) if i != last], [last]]
        else:
            calls = [[i for i in range(len(plan)) if plan[i][0] == 1]]
            calls.append([i for i in range(len(groups)) if i not in calls[0]])
        sums = {}
        for call in calls:
            if call:
                made = attend(
                    pos, counts, kvs[h], arrays, where, [groups[i] for i in call],
                    cands, events, room,
                )
                sums.update(zip(call, made))
        summed.append(scatter_sums(groups, [sums[i] for i in range(len(groups))], n_req, cands))

    full = jnp.concatenate(summed, axis=1)
    parts = [full[:mine]] + [
        swap(full[k * mine : (k + 1) * mine], "ctx", k) for k in range(1, n_ctx)
    ]
    return finish(me_ctx, candidates, gate, w_out, parts)


def solution(mesh):
    placed = (
        P(("req", "ctx"), None),
        P(("req", "ctx"), None),
        P(("req", "ctx"), None),
        P(),
        P(),
        P(),
    )
    return jax.shard_map(
        on_device, mesh=mesh, in_specs=placed, out_specs=P(("req", "ctx"), None), check_vma=False
    )
```

```python
import functools

import jax
import jax.numpy as jnp
from jax import lax
from jax.experimental import pallas as pl
from jax.experimental.pallas import tpu as pltpu
from jax.sharding import PartitionSpec as P


HEAD = 128
TILE = 256
BF16 = jnp.bfloat16
F32 = jnp.float32


def silu(v):
    h = 0.5 * v
    return h + h * jnp.tanh(h)


def swap(value, axis, mask):
    count = lax.axis_size(axis)
    return lax.ppermute(value, axis, [(i, i ^ mask) for i in range(count)])


def scalar_grid(grid, in_specs, out_specs, scratch_shapes=()):
    return pltpu.PrefetchScalarGridSpec(
        num_scalar_prefetch=1,
        grid=grid,
        in_specs=in_specs,
        out_specs=out_specs,
        scratch_shapes=scratch_shapes,
    )


def room_for(*arrays, extra=0):
    total = extra
    for shape, kind in arrays:
        size = jnp.dtype(kind).itemsize
        for dim in shape:
            size *= dim
        total += size
    return pltpu.CompilerParams(vmem_limit_bytes=int(total * 1.25) + (2 << 20))


def cost(flops, moved, transcendentals=0):
    return pl.CostEstimate(
        flops=int(flops), bytes_accessed=int(moved), transcendentals=int(transcendentals)
    )


def query_kernel(me_ref, cand_ref, w_ref, owner_ref, *refs):
    outs, made = refs[:-1], refs[-1]
    rows = cand_ref.shape[0]
    cols = outs[0].shape[1]
    blocks = owner_ref.shape[0]
    projected = jnp.dot(cand_ref[...], w_ref[...], preferred_element_type=F32)
    made[...] = silu(projected).astype(BF16)
    owners = jnp.broadcast_to(owner_ref[...].astype(F32), (blocks, cols)).astype(BF16)
    for k, out in enumerate(outs):
        at = pl.multiple_of((k ^ me_ref[0]) * cols, cols)
        out[:rows, :] = made[:, pl.ds(at, cols)]
        out[rows:, :] = owners


def project_queries(me, candidates, w_qu, block_owner, parts):
    rows, width = candidates.shape
    cols = width // parts
    blocks = block_owner.shape[0]
    return pl.pallas_call(
        query_kernel,
        grid_spec=scalar_grid(
            (1,),
            [
                pl.BlockSpec((rows, width), lambda i, m: (0, 0)),
                pl.BlockSpec((width, width), lambda i, m: (0, 0)),
                pl.BlockSpec((blocks, 1), lambda i, m: (0, 0)),
            ],
            [pl.BlockSpec((rows + blocks, cols), lambda i, m: (0, 0))] * parts,
            [pltpu.VMEM((rows, width), BF16)],
        ),
        out_shape=[jax.ShapeDtypeStruct((rows + blocks, cols), BF16)] * parts,
        compiler_params=room_for(
            ((2, width, width), BF16), ((8, rows + blocks, width), BF16), ((rows, width), F32)
        ),
        cost_estimate=cost(2 * rows * width * width, 2 * width * width + 4 * rows * width),
        name="queries",
    )(me, candidates, w_qu, block_owner)


def gate_kernel(_, cand_ref, w_ref, out_ref):
    out_ref[0] = silu(jnp.dot(cand_ref[...], w_ref[...], preferred_element_type=F32))


def project_gate(me, candidates, w_qu, parts):
    rows, width = candidates.shape
    cols = width // parts
    return pl.pallas_call(
        gate_kernel,
        grid_spec=scalar_grid(
            (parts,),
            [
                pl.BlockSpec((rows, width), lambda k, m: (0, 0)),
                pl.BlockSpec((width, cols), lambda k, m: (0, parts + (k ^ m[0]))),
            ],
            pl.BlockSpec((1, rows, cols), lambda k, m: (k, 0, 0)),
        ),
        out_shape=jax.ShapeDtypeStruct((parts, rows, cols), F32),
        compiler_params=room_for(
            ((2, width, cols), BF16), ((2, rows, width), BF16), ((4, rows, cols), F32)
        ),
        cost_estimate=cost(2 * rows * width * width, 2 * width * width + 6 * rows * width),
        name="gate",
    )(me, candidates, w_qu)


def keys_values_kernel(count, each, _, hist_ref, *refs):
    weights, outs = refs[: 2 * count], refs[2 * count :]
    for k in range(count):
        keys = silu(jnp.dot(hist_ref[...], weights[2 * k][...], preferred_element_type=F32))
        values = jnp.dot(hist_ref[...], weights[2 * k + 1][...], preferred_element_type=F32)
        for h in range(each):
            out = outs[k * each + h]
            out[:, :HEAD] = keys[:, h * HEAD : (h + 1) * HEAD].astype(BF16)
            out[:, HEAD:] = values[:, h * HEAD : (h + 1) * HEAD].astype(BF16)


def project_keys_values(me, history, w_kv, parts, ks):
    rows, width = history.shape
    cols = width // parts
    each = cols // HEAD
    count = len(ks)
    step = rows // 2

    def weight(k, side):
        return pl.BlockSpec((width, cols), lambda r, m: (0, side * parts + (k ^ m[0])))

    made = pl.pallas_call(
        functools.partial(keys_values_kernel, count, each),
        grid_spec=scalar_grid(
            (rows // step,),
            [pl.BlockSpec((step, width), lambda r, m: (r, 0))]
            + [weight(k, side) for k in ks for side in range(2)],
            [pl.BlockSpec((step, 2 * HEAD), lambda r, m: (r, 0))] * (count * each),
        ),
        out_shape=[jax.ShapeDtypeStruct((rows, 2 * HEAD), BF16)] * (count * each),
        cost_estimate=cost(
            4 * rows * width * cols * count,
            2 * rows * width + 4 * width * cols * count + 4 * rows * cols * count,
        ),
        compiler_params=room_for(
            ((2, step, width), BF16),
            ((4 * count, width, cols), BF16),
            ((4 * count, step, cols), BF16),
            ((2, step, cols), F32),
        ),
    )(me, history, *[w_kv] * (2 * count))
    return [made[k * each : (k + 1) * each] for k in range(count)]


def attend_kernel(source, sink, events, room, pos_ref, count_ref, code_ref, *refs):
    codes = len(source)
    n_q = 1 + max(a for a, _ in source)
    n_out = 1 + max(a for a, _ in sink)
    n_kv = len(refs) - n_q - n_out - 3
    kvs, queries = refs[:n_kv], refs[n_kv : n_kv + n_q]
    outs = refs[n_kv + n_q : n_kv + n_q + n_out]
    packed, asked, total = refs[n_kv + n_q + n_out :]
    blocks = kvs[0].shape[0] // events
    cands = asked.shape[0] // codes
    half = 0.5 * HEAD ** (-0.5)

    def code_tiles(j):
        return lax.div(count_ref[code_ref[j]] * events + (TILE - 1), TILE)

    for j in range(codes):
        at = code_ref[j] * room + (lax.max(code_tiles(j), 1) - 1) * TILE
        packed[pl.ds(pl.multiple_of(at, TILE), TILE), :] = jnp.zeros((TILE, 2 * HEAD), BF16)
    for s, kv in enumerate(kvs):

        def place(b, carry, s=s, kv=kv):
            at = pl.multiple_of(pos_ref[s * blocks + b] * events, events)
            packed[pl.ds(at, events), :] = kv[pl.ds(pl.multiple_of(b * events, events), events), :]
            return carry

        lax.fori_loop(0, blocks, place, 0, unroll=8)
    for j, (array, at) in enumerate(source):
        asked[j * cands : (j + 1) * cands, :] = queries[array][at : at + cands, :]

    def one_code(j, carry):
        code = code_ref[j]
        base = pl.multiple_of(code * room, TILE)
        rows = pl.ds(pl.multiple_of(j * cands, cands), cands)
        tiles = code_tiles(j)
        for number in range(room // TILE + 1):

            @pl.when(tiles == number)
            def _(number=number):
                if number == 0:
                    total[rows, :] = jnp.zeros((cands, HEAD), BF16)
                    return
                at = pl.ds(base, number * TILE)
                scores = lax.dot_general(
                    asked[rows, :],
                    packed[at, :HEAD],
                    (((1,), (1,)), ((), ())),
                    preferred_element_type=F32,
                )
                h = scores * half
                weights = (h + h * jnp.tanh(h)).astype(BF16)
                sums = jnp.dot(weights, packed[at, HEAD:], preferred_element_type=F32)
                total[rows, :] = sums.astype(BF16)

        return carry

    lax.fori_loop(0, codes, one_code, 0)
    for j, (array, at) in enumerate(sink):
        outs[array][at : at + cands, :] = total[j * cands : (j + 1) * cands, :]


def attend(pos, counts, kvs, arrays, where, groups, cands, events, room):
    codes = [c for group in groups for c in group]
    sink = [(g, j * cands) for g, group in enumerate(groups) for j in range(len(group))]
    used = sorted({where[c][0] for c in codes})
    source = [(used.index(where[c][0]), where[c][1]) for c in codes]
    queries = [arrays[a] for a in used]
    rows = sum(kv.shape[0] for kv in kvs)
    n_req = counts.shape[0]
    share = len(codes) / n_req
    vmem = pl.BlockSpec(memory_space=pltpu.VMEM)
    smem = pl.BlockSpec(memory_space=pltpu.SMEM)
    return pl.pallas_call(
        functools.partial(attend_kernel, source, sink, events, room),
        in_specs=[smem] * 3 + [vmem] * (len(kvs) + len(queries)),
        out_specs=[vmem] * len(groups),
        out_shape=[jax.ShapeDtypeStruct((len(g) * cands, HEAD), BF16) for g in groups],
        scratch_shapes=[
            pltpu.VMEM((n_req * room, 2 * HEAD), BF16),
            pltpu.VMEM((len(codes) * cands, HEAD), BF16),
            pltpu.VMEM((len(codes) * cands, HEAD), BF16),
        ],
        compiler_params=room_for(
            ((n_req * room + rows, 2 * HEAD), BF16),
            ((5 * len(codes) * cands, HEAD), BF16),
            ((2, cands, room), F32),
        ),
        cost_estimate=cost(
            8 * rows * cands * HEAD * share,
            4 * rows * HEAD + 4 * len(codes) * cands * HEAD,
            rows * cands * share,
        ),
    )(pos, counts, jnp.array(codes, dtype=jnp.int32), *kvs, *queries)


def finish_kernel(me_ref, cand_ref, gate_ref, w_ref, *refs):
    parts, out_ref = refs[:-1], refs[-1]
    width = cand_ref.shape[1]
    cols = parts[0].shape[1]
    values = [p[...].astype(F32) for p in parts]
    mean = sum(jnp.sum(v, axis=1, keepdims=True) for v in values) / width
    values = [v - mean for v in values]
    square = sum(jnp.sum(v * v, axis=1, keepdims=True) for v in values)
    scale = lax.rsqrt(square / width + 1e-05)
    total = cand_ref[...].astype(F32)
    for k, v in enumerate(values):
        mixed = (v * scale * gate_ref[k]).astype(BF16)
        rows = pl.ds(pl.multiple_of((k ^ me_ref[0]) * cols, cols), cols)
        total += jnp.dot(mixed, w_ref[rows, :], preferred_element_type=F32)
    out_ref[...] = total.astype(BF16)


def finish(me, candidates, gate, w_out, parts):
    rows, width = candidates.shape
    vmem = pl.BlockSpec(memory_space=pltpu.VMEM)
    return pl.pallas_call(
        finish_kernel,
        in_specs=[pl.BlockSpec(memory_space=pltpu.SMEM)] + [vmem] * (3 + len(parts)),
        out_specs=vmem,
        out_shape=jax.ShapeDtypeStruct((rows, width), BF16),
        compiler_params=room_for(((width, width), BF16), ((8, rows, width), F32)),
        cost_estimate=cost(2 * rows * width * width, 2 * width * width + 10 * rows * width),
        name="finish",
    )(me, candidates, gate, w_out, *parts)


def stages(count, inner_first):
    outer = []
    bit = count // 2
    while bit >= 2:
        outer.append(2 * bit - 2)
        bit //= 2
    inner = [1] if count > 1 else []
    held, plan = [0], []

    def step(mask, codes):
        plan.append((mask, tuple(codes)))
        held.extend(c ^ mask for c in codes)

    if inner_first:
        for mask in inner + outer:
            step(mask, list(held))
        return plan
    for mask in outer[:-1]:
        step(mask, list(held))
    early = list(held)
    if outer:
        if inner:
            plan.append((1, tuple(early)))
        step(outer[-1], early)
    late = [c for c in held if c not in early] or early
    if inner:
        plan.append((1, tuple(late)))
    return plan


def joined(pieces):
    return pieces[0] if len(pieces) == 1 else jnp.concatenate(pieces, axis=0)


def gather_queries(own, count, inner_first):
    cands = own.shape[0]
    arrays, where = [own], {0: (0, 0)}
    for mask, codes in stages(count, inner_first):
        pieces = [arrays[where[c][0]][where[c][1] : where[c][1] + cands] for c in codes]
        arrays.append(swap(joined(pieces), "req", mask))
        for j, c in enumerate(codes):
            where[c ^ mask] = (len(arrays) - 1, j * cands)
    return arrays, where


def scatter_sums(groups, arrays, count, cands):
    whole = {tuple(g): a for g, a in zip(groups, arrays)}
    held = {}
    for group, array in zip(groups, arrays):
        for j, c in enumerate(group):
            held[c] = array[j * cands : (j + 1) * cands]
    plan = stages(count, False)
    for number in reversed(range(len(plan))):
        mask, codes = plan[number]
        away = tuple(c ^ mask for c in codes)
        sent = whole[away] if away in whole else joined([held[c] for c in away])
        got = swap(sent, "req", mask)
        whole = {g: a for g, a in whole.items() if not set(g) & set(codes)}
        for j, c in enumerate(codes):
            part = held[c].astype(F32) + got[j * cands : (j + 1) * cands].astype(F32)
            held[c] = part.astype(BF16)
    return held[0]


def on_device(history, block_owner, candidates, w_kv, w_qu, w_out):
    n_req, n_ctx = lax.axis_size("req"), lax.axis_size("ctx")
    rows, width = history.shape
    blocks = block_owner.shape[0]
    events = rows // blocks
    mine = candidates.shape[0]
    cands = mine * n_ctx
    each = width // HEAD // n_ctx
    room = -(-n_ctx * (2 * blocks // n_req) * events // TILE) * TILE
    me_ctx = lax.axis_index("ctx").astype(jnp.int32).reshape(1)
    me_req = lax.axis_index("req").astype(jnp.int32)

    made = project_queries(me_ctx, candidates, w_qu, block_owner, n_ctx)
    arrived = [made[0]] + [swap(made[k], "ctx", k) for k in range(1, n_ctx)]

    far = list(range(n_ctx // 2, n_ctx))
    near = list(range(0, n_ctx // 2))
    made_far = project_keys_values(me_ctx, history, w_kv, n_ctx, far)
    made_near = project_keys_values(me_ctx, history, w_kv, n_ctx, near)
    kvs = []
    for h in range(each):
        kvs.append(
            [
                heads[h] if k == 0 else swap(heads[h], "ctx", k)
                for k, heads in zip(near + far, made_near + made_far)
            ]
        )

    owners = jnp.concatenate([a[mine:, 0] for a in arrived]).astype(jnp.int32)
    code = owners ^ me_req
    total_blocks = n_ctx * blocks
    order = jnp.arange(total_blocks, dtype=jnp.int32)
    same = code[:, None] == code[None, :]
    rank = jnp.sum((same & (order[None, :] < order[:, None])).astype(jnp.int32), axis=1)
    pos = code * (room // events) + rank
    counts = jnp.sum(
        (code[None, :] == jnp.arange(n_req, dtype=jnp.int32)[:, None]).astype(jnp.int32), axis=1
    )

    gate = project_gate(me_ctx, candidates, w_qu, n_ctx)

    plan = stages(n_req, False)
    groups = [[c ^ mask for c in codes] for mask, codes in plan] + [[0]]
    summed = []
    for h in range(each):
        own = jnp.concatenate([a[:mine, h * HEAD : (h + 1) * HEAD] for a in arrived], axis=0)
        arrays, where = gather_queries(own, n_req, h % 2 == 1)
        last = len(plan) - 1
        if h == 0:
            calls = [[i for i in range(len(groups)) if i != last], [last]]
        else:
            calls = [[i for i in range(len(plan)) if plan[i][0] == 1]]
            calls.append([i for i in range(len(groups)) if i not in calls[0]])
        sums = {}
        for call in calls:
            if call:
                made = attend(
                    pos, counts, kvs[h], arrays, where, [groups[i] for i in call],
                    cands, events, room,
                )
                sums.update(zip(call, made))
        summed.append(scatter_sums(groups, [sums[i] for i in range(len(groups))], n_req, cands))

    full = jnp.concatenate(summed, axis=1)
    parts = [full[:mine]] + [
        swap(full[k * mine : (k + 1) * mine], "ctx", k) for k in range(1, n_ctx)
    ]
    return finish(me_ctx, candidates, gate, w_out, parts)


def solution(mesh):
    placed = (
        P(("req", "ctx"), None),
        P(("req", "ctx"), None),
        P(("req", "ctx"), None),
        P(),
        P(),
        P(),
    )
    return jax.shard_map(
        on_device, mesh=mesh, in_specs=placed, out_specs=P(("req", "ctx"), None), check_vma=False
    )
```

```python
import functools

import jax
import jax.numpy as jnp
from jax import lax
from jax.experimental import pallas as pl
from jax.experimental.pallas import tpu as pltpu
from jax.sharding import PartitionSpec as P


HEAD = 128
TILE = 256
MOST_DIRECT = 4
BF16 = jnp.bfloat16
F32 = jnp.float32


def silu(v):
    h = 0.5 * v
    return h + h * jnp.tanh(h)


def swap(value, axis, mask):
    count = lax.axis_size(axis)
    return lax.ppermute(value, axis, [(i, i ^ mask) for i in range(count)])


def scalar_grid(grid, in_specs, out_specs, scratch_shapes=()):
    return pltpu.PrefetchScalarGridSpec(
        num_scalar_prefetch=1,
        grid=grid,
        in_specs=in_specs,
        out_specs=out_specs,
        scratch_shapes=scratch_shapes,
    )


def room_for(*arrays, extra=0):
    total = extra
    for shape, kind in arrays:
        size = jnp.dtype(kind).itemsize
        for dim in shape:
            size *= dim
        total += size
    return pltpu.CompilerParams(vmem_limit_bytes=int(total * 1.25) + (2 << 20))


def cost(flops, moved, transcendentals=0):
    return pl.CostEstimate(
        flops=int(flops), bytes_accessed=int(moved), transcendentals=int(transcendentals)
    )


def query_kernel(me_ref, cand_ref, w_ref, owner_ref, *refs):
    outs, made = refs[:-1], refs[-1]
    rows = cand_ref.shape[0]
    cols = outs[0].shape[1]
    blocks = owner_ref.shape[1]
    extra = outs[0].shape[0] - rows
    projected = jnp.dot(cand_ref[...], w_ref[...], preferred_element_type=F32)
    made[...] = silu(projected).astype(BF16)
    owners = jnp.broadcast_to(owner_ref[...].astype(F32), (extra, blocks)).astype(BF16)
    for k, out in enumerate(outs):
        at = pl.multiple_of((k ^ me_ref[0]) * cols, cols)
        out[:rows, :] = made[:, pl.ds(at, cols)]
        out[rows:, :] = jnp.zeros((extra, cols), BF16)
        out[rows:, :blocks] = owners


def project_queries(me, candidates, w_qu, block_owner, parts):
    rows, width = candidates.shape
    cols = width // parts
    blocks = block_owner.shape[0]
    extra = 16
    return pl.pallas_call(
        query_kernel,
        grid_spec=scalar_grid(
            (1,),
            [
                pl.BlockSpec((rows, width), lambda i, m: (0, 0)),
                pl.BlockSpec((width, width), lambda i, m: (0, 0)),
                pl.BlockSpec((1, blocks), lambda i, m: (0, 0)),
            ],
            [pl.BlockSpec((rows + extra, cols), lambda i, m: (0, 0))] * parts,
            [pltpu.VMEM((rows, width), BF16)],
        ),
        out_shape=[jax.ShapeDtypeStruct((rows + extra, cols), BF16)] * parts,
        compiler_params=room_for(
            ((2, width, width), BF16), ((8, rows + extra, width), BF16), ((rows, width), F32)
        ),
        cost_estimate=cost(2 * rows * width * width, 2 * width * width + 4 * rows * width),
        name="queries",
    )(me, candidates, w_qu, block_owner.reshape(1, blocks))


def gate_kernel(_, cand_ref, w_ref, out_ref):
    out_ref[0] = silu(jnp.dot(cand_ref[...], w_ref[...], preferred_element_type=F32))


def project_gate(me, candidates, w_qu, parts):
    rows, width = candidates.shape
    cols = width // parts
    return pl.pallas_call(
        gate_kernel,
        grid_spec=scalar_grid(
            (parts,),
            [
                pl.BlockSpec((rows, width), lambda k, m: (0, 0)),
                pl.BlockSpec((width, cols), lambda k, m: (0, parts + (k ^ m[0]))),
            ],
            pl.BlockSpec((1, rows, cols), lambda k, m: (k, 0, 0)),
        ),
        out_shape=jax.ShapeDtypeStruct((parts, rows, cols), F32),
        compiler_params=room_for(
            ((2, width, cols), BF16), ((2, rows, width), BF16), ((4, rows, cols), F32)
        ),
        cost_estimate=cost(2 * rows * width * width, 2 * width * width + 6 * rows * width),
        name="gate",
    )(me, candidates, w_qu)


def keys_values_kernel(count, each, _, hist_ref, *refs):
    weights, outs = refs[: 2 * count], refs[2 * count :]
    for k in range(count):
        keys = silu(jnp.dot(hist_ref[...], weights[2 * k][...], preferred_element_type=F32))
        values = jnp.dot(hist_ref[...], weights[2 * k + 1][...], preferred_element_type=F32)
        for h in range(each):
            out = outs[k * each + h]
            out[:, :HEAD] = keys[:, h * HEAD : (h + 1) * HEAD].astype(BF16)
            out[:, HEAD:] = values[:, h * HEAD : (h + 1) * HEAD].astype(BF16)


def project_keys_values(me, history, w_kv, parts, ks):
    rows, width = history.shape
    cols = width // parts
    each = cols // HEAD
    count = len(ks)
    step = rows // 2

    def weight(k, side):
        return pl.BlockSpec((width, cols), lambda r, m: (0, side * parts + (k ^ m[0])))

    made = pl.pallas_call(
        functools.partial(keys_values_kernel, count, each),
        grid_spec=scalar_grid(
            (rows // step,),
            [pl.BlockSpec((step, width), lambda r, m: (r, 0))]
            + [weight(k, side) for k in ks for side in range(2)],
            [pl.BlockSpec((step, 2 * HEAD), lambda r, m: (r, 0))] * (count * each),
        ),
        out_shape=[jax.ShapeDtypeStruct((rows, 2 * HEAD), BF16)] * (count * each),
        cost_estimate=cost(
            4 * rows * width * cols * count,
            2 * rows * width + 4 * width * cols * count + 4 * rows * cols * count,
        ),
        compiler_params=room_for(
            ((2, step, width), BF16),
            ((4 * count, width, cols), BF16),
            ((4 * count, step, cols), BF16),
            ((2, step, cols), F32),
        ),
    )(me, history, *[w_kv] * (2 * count))
    return [made[k * each : (k + 1) * each] for k in range(count)]


def attend_kernel(source, sink, events, room, pos_ref, count_ref, code_ref, *refs):
    codes = len(source)
    n_q = 1 + max(a for a, _ in source)
    n_out = 1 + max(a for a, _ in sink)
    n_kv = len(refs) - n_q - n_out - 3
    kvs, queries = refs[:n_kv], refs[n_kv : n_kv + n_q]
    outs = refs[n_kv + n_q : n_kv + n_q + n_out]
    packed, asked, total = refs[n_kv + n_q + n_out :]
    blocks = kvs[0].shape[0] // events
    cands = asked.shape[0] // codes
    half = 0.5 * HEAD ** (-0.5)

    def code_tiles(j):
        return lax.div(count_ref[code_ref[j]] * events + (TILE - 1), TILE)

    for j in range(codes):
        at = code_ref[j] * room + (lax.max(code_tiles(j), 1) - 1) * TILE
        packed[pl.ds(pl.multiple_of(at, TILE), TILE), :] = jnp.zeros((TILE, 2 * HEAD), BF16)
    for s, kv in enumerate(kvs):

        def place(b, carry, s=s, kv=kv):
            at = pl.multiple_of(pos_ref[s * blocks + b] * events, events)
            packed[pl.ds(at, events), :] = kv[pl.ds(pl.multiple_of(b * events, events), events), :]
            return carry

        lax.fori_loop(0, blocks, place, 0, unroll=8)
    for j, (array, at) in enumerate(source):
        asked[j * cands : (j + 1) * cands, :] = queries[array][at : at + cands, :]

    def one_code(j, carry):
        code = code_ref[j]
        base = pl.multiple_of(code * room, TILE)
        rows = pl.ds(pl.multiple_of(j * cands, cands), cands)
        tiles = code_tiles(j)
        for number in range(room // TILE + 1):

            @pl.when(tiles == number)
            def _(number=number):
                if number == 0:
                    total[rows, :] = jnp.zeros((cands, HEAD), BF16)
                    return
                at = pl.ds(base, number * TILE)
                scores = lax.dot_general(
                    asked[rows, :],
                    packed[at, :HEAD],
                    (((1,), (1,)), ((), ())),
                    preferred_element_type=F32,
                )
                h = scores * half
                weights = (h + h * jnp.tanh(h)).astype(BF16)
                sums = jnp.dot(weights, packed[at, HEAD:], preferred_element_type=F32)
                total[rows, :] = sums.astype(BF16)

        return carry

    lax.fori_loop(0, codes, one_code, 0)
    for j, (array, at) in enumerate(sink):
        outs[array][at : at + cands, :] = total[j * cands : (j + 1) * cands, :]


def attend(pos, counts, kvs, arrays, where, groups, cands, events, room):
    codes = [c for group in groups for c in group]
    sink = [(g, j * cands) for g, group in enumerate(groups) for j in range(len(group))]
    used = sorted({where[c][0] for c in codes})
    source = [(used.index(where[c][0]), where[c][1]) for c in codes]
    queries = [arrays[a] for a in used]
    rows = sum(kv.shape[0] for kv in kvs)
    n_req = counts.shape[0]
    share = len(codes) / n_req
    vmem = pl.BlockSpec(memory_space=pltpu.VMEM)
    smem = pl.BlockSpec(memory_space=pltpu.SMEM)
    return pl.pallas_call(
        functools.partial(attend_kernel, source, sink, events, room),
        in_specs=[smem] * 3 + [vmem] * (len(kvs) + len(queries)),
        out_specs=[vmem] * len(groups),
        out_shape=[jax.ShapeDtypeStruct((len(g) * cands, HEAD), BF16) for g in groups],
        scratch_shapes=[
            pltpu.VMEM((n_req * room, 2 * HEAD), BF16),
            pltpu.VMEM((len(codes) * cands, HEAD), BF16),
            pltpu.VMEM((len(codes) * cands, HEAD), BF16),
        ],
        compiler_params=room_for(
            ((n_req * room + rows, 2 * HEAD), BF16),
            ((5 * len(codes) * cands, HEAD), BF16),
            ((2, cands, room), F32),
        ),
        cost_estimate=cost(
            8 * rows * cands * HEAD * share,
            4 * rows * HEAD + 4 * len(codes) * cands * HEAD,
            rows * cands * share,
        ),
    )(pos, counts, jnp.array(codes, dtype=jnp.int32), *kvs, *queries)


def finish_kernel(me_ref, cand_ref, gate_ref, w_ref, *refs):
    parts, out_ref = refs[:-1], refs[-1]
    count, _, cols = gate_ref.shape
    width = cand_ref.shape[1]
    each = len(parts) // count
    values = [
        jnp.concatenate([p[...].astype(F32) for p in parts[k * each : (k + 1) * each]], axis=1)
        for k in range(count)
    ]
    mean = sum(jnp.sum(v, axis=1, keepdims=True) for v in values) / width
    values = [v - mean for v in values]
    square = sum(jnp.sum(v * v, axis=1, keepdims=True) for v in values)
    scale = lax.rsqrt(square / width + 1e-05)
    total = cand_ref[...].astype(F32)
    for k, v in enumerate(values):
        mixed = (v * scale * gate_ref[k]).astype(BF16)
        rows = pl.ds(pl.multiple_of((k ^ me_ref[0]) * cols, cols), cols)
        total += jnp.dot(mixed, w_ref[rows, :], preferred_element_type=F32)
    out_ref[...] = total.astype(BF16)


def finish(me, candidates, gate, w_out, parts):
    rows, width = candidates.shape
    vmem = pl.BlockSpec(memory_space=pltpu.VMEM)
    return pl.pallas_call(
        finish_kernel,
        in_specs=[pl.BlockSpec(memory_space=pltpu.SMEM)] + [vmem] * (3 + len(parts)),
        out_specs=vmem,
        out_shape=jax.ShapeDtypeStruct((rows, width), BF16),
        compiler_params=room_for(((width, width), BF16), ((8, rows, width), F32)),
        cost_estimate=cost(2 * rows * width * width, 2 * width * width + 10 * rows * width),
        name="finish",
    )(me, candidates, gate, w_out, *parts)


def stages(count, inner_first):
    outer = []
    bit = count // 2
    while bit >= 2:
        outer.append(2 * bit - 2)
        bit //= 2
    inner = [1] if count > 1 else []
    held, plan = [0], []

    def step(mask, codes):
        plan.append((mask, tuple(codes)))
        held.extend(c ^ mask for c in codes)

    if inner_first:
        for mask in inner + outer:
            step(mask, list(held))
        return plan
    for mask in outer[:-1]:
        step(mask, list(held))
    early = list(held)
    if outer:
        if inner:
            plan.append((1, tuple(early)))
        step(outer[-1], early)
    late = [c for c in held if c not in early] or early
    if inner:
        plan.append((1, tuple(late)))
    return plan


def joined(pieces):
    return pieces[0] if len(pieces) == 1 else jnp.concatenate(pieces, axis=0)


def direct(count):
    return 2 <= count // 2 <= MOST_DIRECT


def gather_plan(count, head):
    if head % 2 == 1:
        return stages(count, True)
    if not direct(count):
        return stages(count, False)
    even = list(range(0, count, 2))
    cut = len(even) // 2
    plan = [(mask, (0,)) for mask in reversed(even[1:])]
    return plan + [(1, tuple(even[:cut])), (1, tuple(even[cut:]))]


def scatter_plan(count, head):
    plan = stages(count, False)
    if head % 2 == 1 or not direct(count):
        return plan
    even = list(range(0, count, 2))
    cut = len(even) // 2
    plan = [step for step in plan if step[0] != 1]
    return plan + [(1, tuple(even[cut:])), (1, tuple(even[:cut]))]


def gather_queries(own, plan):
    cands = own.shape[0]
    arrays, where = [own], {0: (0, 0)}
    for mask, codes in plan:
        pieces = [arrays[where[c][0]][where[c][1] : where[c][1] + cands] for c in codes]
        arrays.append(swap(joined(pieces), "req", mask))
        for j, c in enumerate(codes):
            where[c ^ mask] = (len(arrays) - 1, j * cands)
    return arrays, where


def scatter_sums(plan, groups, arrays, cands):
    whole = {tuple(g): a for g, a in zip(groups, arrays)}
    held = {}
    for group, array in zip(groups, arrays):
        for j, c in enumerate(group):
            held[c] = array[j * cands : (j + 1) * cands]
    for number in reversed(range(len(plan))):
        mask, codes = plan[number]
        away = tuple(c ^ mask for c in codes)
        sent = whole[away] if away in whole else joined([held[c].astype(BF16) for c in away])
        got = swap(sent, "req", mask)
        whole = {g: a for g, a in whole.items() if not set(g) & set(codes)}
        for j, c in enumerate(codes):
            held[c] = held[c].astype(F32) + got[j * cands : (j + 1) * cands].astype(F32)
    return held[0]


def on_device(history, block_owner, candidates, w_kv, w_qu, w_out):
    n_req, n_ctx = lax.axis_size("req"), lax.axis_size("ctx")
    rows, width = history.shape
    blocks = block_owner.shape[0]
    events = rows // blocks
    mine = candidates.shape[0]
    cands = mine * n_ctx
    each = width // HEAD // n_ctx
    room = -(-n_ctx * (2 * blocks // n_req) * events // TILE) * TILE
    me_ctx = lax.axis_index("ctx").astype(jnp.int32).reshape(1)
    me_req = lax.axis_index("req").astype(jnp.int32)

    made = project_queries(me_ctx, candidates, w_qu, block_owner, n_ctx)
    arrived = [made[0]] + [swap(made[k], "ctx", k) for k in range(1, n_ctx)]

    far = list(range(n_ctx // 2, n_ctx))
    near = list(range(0, n_ctx // 2))
    made_far = project_keys_values(me_ctx, history, w_kv, n_ctx, far)
    made_near = project_keys_values(me_ctx, history, w_kv, n_ctx, near)
    kvs = []
    for h in range(each):
        kvs.append(
            [
                heads[h] if k == 0 else swap(heads[h], "ctx", k)
                for k, heads in zip(near + far, made_near + made_far)
            ]
        )

    owners = jnp.concatenate([a[mine, :blocks] for a in arrived]).astype(jnp.int32)
    code = owners ^ me_req
    total_blocks = n_ctx * blocks
    order = jnp.arange(total_blocks, dtype=jnp.int32)
    same = code[:, None] == code[None, :]
    rank = jnp.sum((same & (order[None, :] < order[:, None])).astype(jnp.int32), axis=1)
    pos = code * (room // events) + rank
    counts = jnp.sum(
        (code[None, :] == jnp.arange(n_req, dtype=jnp.int32)[:, None]).astype(jnp.int32), axis=1
    )

    gate = project_gate(me_ctx, candidates, w_qu, n_ctx)

    parts = [[None] * each for _ in range(n_ctx)]
    for h in range(each):
        own = jnp.concatenate([a[:mine, h * HEAD : (h + 1) * HEAD] for a in arrived], axis=0)
        arrays, where = gather_queries(own, gather_plan(n_req, h))
        plan = scatter_plan(n_req, h)
        groups = [[c ^ mask for c in codes] for mask, codes in plan] + [[0]]
        sums = {}
        for call in calls_of(n_req, h):
            made = attend(
                pos, counts, kvs[h], arrays, where, [groups[i] for i in call],
                cands, events, room,
            )
            sums.update(zip(call, made))
        total = scatter_sums(plan, groups, [sums[i] for i in range(len(groups))], cands)
        parts[0][h] = total[:mine]
        for k in range(1, n_ctx):
            piece = total[k * mine : (k + 1) * mine].astype(BF16)
            parts[k][h] = swap(piece, "ctx", k)
    return finish(me_ctx, candidates, gate, w_out, [p for row in parts for p in row])


def calls_of(count, head):
    plan = scatter_plan(count, head)
    everything = list(range(len(plan) + 1))
    inner = [i for i in range(len(plan)) if plan[i][0] == 1]
    if len(inner) < 2:
        return [everything]
    if head % 2 == 0:
        late = inner[0] if direct(count) else inner[-1]
        return [[i for i in everything if i != late], [late]]
    last = inner[-1]
    return [[i for i in everything if i not in (last, last - 1)], [last], [last - 1]]


def solution(mesh):
    placed = (
        P(("req", "ctx"), None),
        P(("req", "ctx"), None),
        P(("req", "ctx"), None),
        P(),
        P(),
        P(),
    )
    return jax.shard_map(
        on_device, mesh=mesh, in_specs=placed, out_specs=P(("req", "ctx"), None), check_vma=False
    )
```

```python
import functools

import jax
import jax.numpy as jnp
from jax import lax
from jax.experimental import pallas as pl
from jax.experimental.pallas import tpu as pltpu
from jax.sharding import PartitionSpec as P


HEAD = 128
TILE = 256
BF16 = jnp.bfloat16
F32 = jnp.float32


def silu(v):
    h = 0.5 * v
    return h + h * jnp.tanh(h)


def swap(value, axis, mask):
    count = lax.axis_size(axis)
    return lax.ppermute(value, axis, [(i, i ^ mask) for i in range(count)])


def scalar_grid(grid, in_specs, out_specs, scratch_shapes=()):
    return pltpu.PrefetchScalarGridSpec(
        num_scalar_prefetch=1,
        grid=grid,
        in_specs=in_specs,
        out_specs=out_specs,
        scratch_shapes=scratch_shapes,
    )


def room_for(*arrays, extra=0):
    total = extra
    for shape, kind in arrays:
        size = jnp.dtype(kind).itemsize
        for dim in shape:
            size *= dim
        total += size
    return pltpu.CompilerParams(vmem_limit_bytes=int(total * 1.25) + (2 << 20))


def cost(flops, moved, transcendentals=0):
    return pl.CostEstimate(
        flops=int(flops), bytes_accessed=int(moved), transcendentals=int(transcendentals)
    )


def query_kernel(me_ref, cand_hbm, w_hbm, owner_ref, *refs):
    outs, (cand, weight, made, sems) = refs[:-4], refs[-4:]
    rows = cand.shape[0]
    parts = len(outs)
    cols = outs[0].shape[1]
    blocks = owner_ref.shape[1]
    extra = outs[0].shape[0] - rows
    fetch = [pltpu.make_async_copy(cand_hbm, cand, sems.at[parts])]
    for k in range(parts):
        at = pl.ds(k * cols, cols)
        fetch.append(pltpu.make_async_copy(w_hbm.at[:, at], weight.at[:, at], sems.at[k]))
    for copy in fetch:
        copy.start()
    owners = jnp.broadcast_to(owner_ref[...].astype(F32), (extra, blocks)).astype(BF16)
    for out in outs:
        out[rows:, :] = jnp.zeros((extra, cols), BF16)
        out[rows:, :blocks] = owners
    fetch[0].wait()
    for k in range(parts):
        fetch[k + 1].wait()
        at = slice(k * cols, (k + 1) * cols)
        projected = jnp.dot(cand[...], weight[:, at], preferred_element_type=F32)
        made[:, at] = silu(projected).astype(BF16)
    for k, out in enumerate(outs):
        at = pl.multiple_of((k ^ me_ref[0]) * cols, cols)
        out[:rows, :] = made[:, pl.ds(at, cols)]


def project_queries(me, candidates, w_qu, block_owner, parts):
    rows, width = candidates.shape
    cols = width // parts
    blocks = block_owner.shape[0]
    extra = 16
    vmem = pl.BlockSpec(memory_space=pltpu.VMEM)
    hbm = pl.BlockSpec(memory_space=pltpu.HBM)
    return pl.pallas_call(
        query_kernel,
        in_specs=[pl.BlockSpec(memory_space=pltpu.SMEM), hbm, hbm, vmem],
        out_specs=[vmem] * parts,
        out_shape=[jax.ShapeDtypeStruct((rows + extra, cols), BF16)] * parts,
        scratch_shapes=[
            pltpu.VMEM((rows, width), BF16),
            pltpu.VMEM((width, width), BF16),
            pltpu.VMEM((rows, width), BF16),
            pltpu.SemaphoreType.DMA((parts + 1,)),
        ],
        compiler_params=room_for(
            ((width, width), BF16), ((4, rows + extra, width), BF16), ((rows, width), F32)
        ),
        cost_estimate=cost(2 * rows * width * width, 2 * width * width + 4 * rows * width),
        name="queries",
    )(me, candidates, w_qu, block_owner.reshape(1, blocks))


def assemble_kernel(count, *refs):
    arrived, outs, owner_ref = refs[:count], refs[count:-1], refs[-1]
    blocks = owner_ref.shape[1]
    rows = outs[0].shape[0] // count
    for k, ref in enumerate(arrived):
        for h, out in enumerate(outs):
            out[k * rows : (k + 1) * rows, :] = ref[:rows, h * HEAD : (h + 1) * HEAD]
        below = ref[rows : rows + 16, :HEAD].astype(F32)
        owner_ref[k : k + 1, :] = below[:1, :blocks].astype(jnp.int32)


def assemble(arrived, rows, each, blocks):
    count = len(arrived)
    vmem = pl.BlockSpec(memory_space=pltpu.VMEM)
    made = pl.pallas_call(
        functools.partial(assemble_kernel, count),
        in_specs=[vmem] * count,
        out_specs=[vmem] * (each + 1),
        out_shape=[jax.ShapeDtypeStruct((count * rows, HEAD), BF16)] * each
        + [jax.ShapeDtypeStruct((count, blocks), jnp.int32)],
        compiler_params=room_for(((4, count * rows, each * HEAD), BF16)),
        cost_estimate=cost(0, 4 * count * rows * each * HEAD),
        name="assemble",
    )(*arrived)
    return made[:each], made[each]


def gate_kernel(_, cand_ref, w_ref, out_ref):
    out_ref[0] = silu(jnp.dot(cand_ref[...], w_ref[...], preferred_element_type=F32))


def project_gate(me, candidates, w_qu, parts):
    rows, width = candidates.shape
    cols = width // parts
    return pl.pallas_call(
        gate_kernel,
        grid_spec=scalar_grid(
            (parts,),
            [
                pl.BlockSpec((rows, width), lambda k, m: (0, 0)),
                pl.BlockSpec((width, cols), lambda k, m: (0, parts + (k ^ m[0]))),
            ],
            pl.BlockSpec((1, rows, cols), lambda k, m: (k, 0, 0)),
        ),
        out_shape=jax.ShapeDtypeStruct((parts, rows, cols), F32),
        compiler_params=room_for(
            ((2, width, cols), BF16), ((2, rows, width), BF16), ((4, rows, cols), F32)
        ),
        cost_estimate=cost(2 * rows * width * width, 2 * width * width + 6 * rows * width),
        name="gate",
    )(me, candidates, w_qu)


def keys_values_kernel(count, each, _, hist_ref, *refs):
    weights, outs = refs[: 2 * count], refs[2 * count :]
    for k in range(count):
        keys = silu(jnp.dot(hist_ref[...], weights[2 * k][...], preferred_element_type=F32))
        values = jnp.dot(hist_ref[...], weights[2 * k + 1][...], preferred_element_type=F32)
        for h in range(each):
            out = outs[k * each + h]
            out[:, :HEAD] = keys[:, h * HEAD : (h + 1) * HEAD].astype(BF16)
            out[:, HEAD:] = values[:, h * HEAD : (h + 1) * HEAD].astype(BF16)


def project_keys_values(me, history, w_kv, parts, ks):
    rows, width = history.shape
    cols = width // parts
    each = cols // HEAD
    count = len(ks)
    step = rows // 2

    def weight(k, side):
        return pl.BlockSpec((width, cols), lambda r, m: (0, side * parts + (k ^ m[0])))

    made = pl.pallas_call(
        functools.partial(keys_values_kernel, count, each),
        grid_spec=scalar_grid(
            (rows // step,),
            [pl.BlockSpec((step, width), lambda r, m: (r, 0))]
            + [weight(k, side) for k in ks for side in range(2)],
            [pl.BlockSpec((step, 2 * HEAD), lambda r, m: (r, 0))] * (count * each),
        ),
        out_shape=[jax.ShapeDtypeStruct((rows, 2 * HEAD), BF16)] * (count * each),
        cost_estimate=cost(
            4 * rows * width * cols * count,
            2 * rows * width + 4 * width * cols * count + 4 * rows * cols * count,
        ),
        compiler_params=room_for(
            ((2, step, width), BF16),
            ((4 * count, width, cols), BF16),
            ((4 * count, step, cols), BF16),
            ((2, step, cols), F32),
        ),
    )(me, history, *[w_kv] * (2 * count))
    return [made[k * each : (k + 1) * each] for k in range(count)]


def attend_kernel(source, sink, events, room, pos_ref, count_ref, code_ref, *refs):
    codes = len(source)
    n_q = 1 + max(a for a, _ in source)
    n_out = 1 + max(a for a, _ in sink)
    n_kv = len(refs) - n_q - n_out - 3
    kvs, queries = refs[:n_kv], refs[n_kv : n_kv + n_q]
    outs = refs[n_kv + n_q : n_kv + n_q + n_out]
    packed, asked, total = refs[n_kv + n_q + n_out :]
    blocks = kvs[0].shape[0] // events
    cands = asked.shape[0] // codes
    half = 0.5 * HEAD ** (-0.5)

    def code_tiles(j):
        return lax.div(count_ref[code_ref[j]] * events + (TILE - 1), TILE)

    for j in range(codes):
        at = code_ref[j] * room + (lax.max(code_tiles(j), 1) - 1) * TILE
        packed[pl.ds(pl.multiple_of(at, TILE), TILE), :] = jnp.zeros((TILE, 2 * HEAD), BF16)
    for s, kv in enumerate(kvs):

        def place(b, carry, s=s, kv=kv):
            at = pl.multiple_of(pos_ref[s * blocks + b] * events, events)
            packed[pl.ds(at, events), :] = kv[pl.ds(pl.multiple_of(b * events, events), events), :]
            return carry

        lax.fori_loop(0, blocks, place, 0, unroll=8)
    for j, (array, at) in enumerate(source):
        asked[j * cands : (j + 1) * cands, :] = queries[array][at : at + cands, :]

    def one_code(j, carry):
        code = code_ref[j]
        base = pl.multiple_of(code * room, TILE)
        rows = pl.ds(pl.multiple_of(j * cands, cands), cands)
        tiles = code_tiles(j)
        for number in range(room // TILE + 1):

            @pl.when(tiles == number)
            def _(number=number):
                if number == 0:
                    total[rows, :] = jnp.zeros((cands, HEAD), BF16)
                    return
                at = pl.ds(base, number * TILE)
                scores = lax.dot_general(
                    asked[rows, :],
                    packed[at, :HEAD],
                    (((1,), (1,)), ((), ())),
                    preferred_element_type=F32,
                )
                h = scores * half
                weights = (h + h * jnp.tanh(h)).astype(BF16)
                sums = jnp.dot(weights, packed[at, HEAD:], preferred_element_type=F32)
                total[rows, :] = sums.astype(BF16)

        return carry

    lax.fori_loop(0, codes, one_code, 0)
    for j, (array, at) in enumerate(sink):
        outs[array][at : at + cands, :] = total[j * cands : (j + 1) * cands, :]


def attend(pos, counts, kvs, arrays, where, groups, cands, events, room):
    codes = [c for group in groups for c in group]
    sink = [(g, j * cands) for g, group in enumerate(groups) for j in range(len(group))]
    used = sorted({where[c][0] for c in codes})
    source = [(used.index(where[c][0]), where[c][1]) for c in codes]
    queries = [arrays[a] for a in used]
    rows = sum(kv.shape[0] for kv in kvs)
    n_req = counts.shape[0]
    share = len(codes) / n_req
    vmem = pl.BlockSpec(memory_space=pltpu.VMEM)
    smem = pl.BlockSpec(memory_space=pltpu.SMEM)
    return pl.pallas_call(
        functools.partial(attend_kernel, source, sink, events, room),
        in_specs=[smem] * 3 + [vmem] * (len(kvs) + len(queries)),
        out_specs=[vmem] * len(groups),
        out_shape=[jax.ShapeDtypeStruct((len(g) * cands, HEAD), BF16) for g in groups],
        scratch_shapes=[
            pltpu.VMEM((n_req * room, 2 * HEAD), BF16),
            pltpu.VMEM((len(codes) * cands, HEAD), BF16),
            pltpu.VMEM((len(codes) * cands, HEAD), BF16),
        ],
        compiler_params=room_for(
            ((n_req * room + rows, 2 * HEAD), BF16),
            ((5 * len(codes) * cands, HEAD), BF16),
            ((2, cands, room), F32),
        ),
        cost_estimate=cost(
            8 * rows * cands * HEAD * share,
            4 * rows * HEAD + 4 * len(codes) * cands * HEAD,
            rows * cands * share,
        ),
    )(pos, counts, jnp.array(codes, dtype=jnp.int32), *kvs, *queries)


def finish_kernel(me_ref, cand_ref, gate_ref, w_ref, *refs):
    parts, out_ref = refs[:-1], refs[-1]
    count, _, cols = gate_ref.shape
    width = cand_ref.shape[1]
    each = len(parts) // count
    values = [
        jnp.concatenate([p[...].astype(F32) for p in parts[k * each : (k + 1) * each]], axis=1)
        for k in range(count)
    ]
    mean = sum(jnp.sum(v, axis=1, keepdims=True) for v in values) / width
    values = [v - mean for v in values]
    square = sum(jnp.sum(v * v, axis=1, keepdims=True) for v in values)
    scale = lax.rsqrt(square / width + 1e-05)
    total = cand_ref[...].astype(F32)
    for k, v in enumerate(values):
        mixed = (v * scale * gate_ref[k]).astype(BF16)
        rows = pl.ds(pl.multiple_of((k ^ me_ref[0]) * cols, cols), cols)
        total += jnp.dot(mixed, w_ref[rows, :], preferred_element_type=F32)
    out_ref[...] = total.astype(BF16)


def finish(me, candidates, gate, w_out, parts):
    rows, width = candidates.shape
    vmem = pl.BlockSpec(memory_space=pltpu.VMEM)
    return pl.pallas_call(
        finish_kernel,
        in_specs=[pl.BlockSpec(memory_space=pltpu.SMEM)] + [vmem] * (3 + len(parts)),
        out_specs=vmem,
        out_shape=jax.ShapeDtypeStruct((rows, width), BF16),
        compiler_params=room_for(((width, width), BF16), ((8, rows, width), F32)),
        cost_estimate=cost(2 * rows * width * width, 2 * width * width + 10 * rows * width),
        name="finish",
    )(me, candidates, gate, w_out, *parts)


def stages(count, inner_first):
    outer = []
    bit = count // 2
    while bit >= 2:
        outer.append(2 * bit - 2)
        bit //= 2
    inner = [1] if count > 1 else []
    held, plan = [0], []

    def step(mask, codes):
        plan.append((mask, tuple(codes)))
        held.extend(c ^ mask for c in codes)

    if inner_first:
        for mask in inner + outer:
            step(mask, list(held))
        return plan
    for mask in outer[:-1]:
        step(mask, list(held))
    early = list(held)
    if outer:
        if inner:
            plan.append((1, tuple(early)))
        step(outer[-1], early)
    late = [c for c in held if c not in early] or early
    if inner:
        plan.append((1, tuple(late)))
    return plan


def joined(pieces):
    return pieces[0] if len(pieces) == 1 else jnp.concatenate(pieces, axis=0)


def gather_plan(count, head):
    return stages(count, head % 2 == 1)


def scatter_plan(count):
    return stages(count, False)


def gather_queries(own, plan):
    cands = own.shape[0]
    arrays, where = [own], {0: (0, 0)}
    for mask, codes in plan:
        pieces = [arrays[where[c][0]][where[c][1] : where[c][1] + cands] for c in codes]
        arrays.append(swap(joined(pieces), "req", mask))
        for j, c in enumerate(codes):
            where[c ^ mask] = (len(arrays) - 1, j * cands)
    return arrays, where


def scatter_sums(plan, groups, arrays, cands):
    whole = {tuple(g): a for g, a in zip(groups, arrays)}
    held = {}
    for group, array in zip(groups, arrays):
        for j, c in enumerate(group):
            held[c] = array[j * cands : (j + 1) * cands]
    for number in reversed(range(len(plan))):
        mask, codes = plan[number]
        away = tuple(c ^ mask for c in codes)
        sent = whole[away] if away in whole else joined([held[c].astype(BF16) for c in away])
        got = swap(sent, "req", mask)
        whole = {g: a for g, a in whole.items() if not set(g) & set(codes)}
        for j, c in enumerate(codes):
            held[c] = held[c].astype(F32) + got[j * cands : (j + 1) * cands].astype(F32)
    return held[0]


def on_device(history, block_owner, candidates, w_kv, w_qu, w_out):
    n_req, n_ctx = lax.axis_size("req"), lax.axis_size("ctx")
    rows, width = history.shape
    blocks = block_owner.shape[0]
    events = rows // blocks
    mine = candidates.shape[0]
    cands = mine * n_ctx
    each = width // HEAD // n_ctx
    room = -(-n_ctx * (2 * blocks // n_req) * events // TILE) * TILE
    me_ctx = lax.axis_index("ctx").astype(jnp.int32).reshape(1)
    me_req = lax.axis_index("req").astype(jnp.int32)

    made = project_queries(me_ctx, candidates, w_qu, block_owner, n_ctx)
    arrived = [made[0]] + [swap(made[k], "ctx", k) for k in range(1, n_ctx)]

    far = list(range(n_ctx // 2, n_ctx))
    near = list(range(0, n_ctx // 2))
    made_far = project_keys_values(me_ctx, history, w_kv, n_ctx, far)
    made_near = project_keys_values(me_ctx, history, w_kv, n_ctx, near)
    kvs = []
    for h in range(each):
        kvs.append(
            [
                heads[h] if k == 0 else swap(heads[h], "ctx", k)
                for k, heads in zip(near + far, made_near + made_far)
            ]
        )

    asked, owners = assemble(arrived, mine, each, blocks)
    owners = owners.reshape(-1)
    code = owners ^ me_req
    total_blocks = n_ctx * blocks
    order = jnp.arange(total_blocks, dtype=jnp.int32)
    same = code[:, None] == code[None, :]
    rank = jnp.sum((same & (order[None, :] < order[:, None])).astype(jnp.int32), axis=1)
    pos = code * (room // events) + rank
    counts = jnp.sum(
        (code[None, :] == jnp.arange(n_req, dtype=jnp.int32)[:, None]).astype(jnp.int32), axis=1
    )

    gate = project_gate(me_ctx, candidates, w_qu, n_ctx)

    parts = [[None] * each for _ in range(n_ctx)]
    for h in range(each):
        arrays, where = gather_queries(asked[h], gather_plan(n_req, h))
        plan = scatter_plan(n_req)
        groups = [[c ^ mask for c in codes] for mask, codes in plan] + [[0]]
        sums = {}
        for call in calls_of(n_req, h):
            made = attend(
                pos, counts, kvs[h], arrays, where, [groups[i] for i in call],
                cands, events, room,
            )
            sums.update(zip(call, made))
        total = scatter_sums(plan, groups, [sums[i] for i in range(len(groups))], cands)
        parts[0][h] = total[:mine]
        for k in range(1, n_ctx):
            piece = total[k * mine : (k + 1) * mine].astype(BF16)
            parts[k][h] = swap(piece, "ctx", k)
    return finish(me_ctx, candidates, gate, w_out, [p for row in parts for p in row])


def calls_of(count, head):
    plan = scatter_plan(count)
    everything = list(range(len(plan) + 1))
    inner = [i for i in range(len(plan)) if plan[i][0] == 1]
    if len(inner) < 2:
        return [everything]
    last = inner[-1]
    rest = [i for i in everything if i != last]
    return [rest, [last]] if head % 2 == 0 else [[last], rest]


def solution(mesh):
    placed = (
        P(("req", "ctx"), None),
        P(("req", "ctx"), None),
        P(("req", "ctx"), None),
        P(),
        P(),
        P(),
    )
    return jax.shard_map(
        on_device, mesh=mesh, in_specs=placed, out_specs=P(("req", "ctx"), None), check_vma=False
    )
```

```python
import functools

import jax
import jax.numpy as jnp
from jax import lax
from jax.experimental import pallas as pl
from jax.experimental.pallas import tpu as pltpu
from jax.sharding import PartitionSpec as P


HEAD = 128
TILE = 256
VMEM = 67043328
BF16 = jnp.bfloat16
F32 = jnp.float32


def silu(v):
    h = 0.5 * v
    return h + h * jnp.tanh(h)


def swap(value, axis, mask):
    count = lax.axis_size(axis)
    return lax.ppermute(value, axis, [(i, i ^ mask) for i in range(count)])


def scalar_grid(grid, in_specs, out_specs, scratch_shapes=()):
    return pltpu.PrefetchScalarGridSpec(
        num_scalar_prefetch=1,
        grid=grid,
        in_specs=in_specs,
        out_specs=out_specs,
        scratch_shapes=scratch_shapes,
    )


def room_for(*arrays, extra=0):
    total = extra
    for shape, kind in arrays:
        size = jnp.dtype(kind).itemsize
        for dim in shape:
            size *= dim
        total += size
    return pltpu.CompilerParams(vmem_limit_bytes=int(total * 1.25) + (2 << 20))


def cost(flops, moved, transcendentals=0):
    return pl.CostEstimate(
        flops=int(flops), bytes_accessed=int(moved), transcendentals=int(transcendentals)
    )


def query_kernel(me_ref, cand_hbm, w_hbm, owner_ref, *refs):
    outs, (cand, weight, made, sems) = refs[:-4], refs[-4:]
    rows = cand.shape[0]
    parts = len(outs)
    cols = outs[0].shape[1]
    blocks = owner_ref.shape[1]
    extra = outs[0].shape[0] - rows
    fetch = [pltpu.make_async_copy(cand_hbm, cand, sems.at[parts])]
    for k in range(parts):
        at = pl.ds(k * cols, cols)
        fetch.append(pltpu.make_async_copy(w_hbm.at[:, at], weight.at[:, at], sems.at[k]))
    for copy in fetch:
        copy.start()
    owners = jnp.broadcast_to(owner_ref[...].astype(F32), (extra, blocks)).astype(BF16)
    for out in outs:
        out[rows:, :] = jnp.zeros((extra, cols), BF16)
        out[rows:, :blocks] = owners
    fetch[0].wait()
    for k in range(parts):
        fetch[k + 1].wait()
        at = slice(k * cols, (k + 1) * cols)
        projected = jnp.dot(cand[...], weight[:, at], preferred_element_type=F32)
        made[:, at] = silu(projected).astype(BF16)
    for k, out in enumerate(outs):
        at = pl.multiple_of((k ^ me_ref[0]) * cols, cols)
        out[:rows, :] = made[:, pl.ds(at, cols)]


def project_queries(me, candidates, w_qu, block_owner, parts):
    rows, width = candidates.shape
    cols = width // parts
    blocks = block_owner.shape[0]
    extra = 16
    vmem = pl.BlockSpec(memory_space=pltpu.VMEM)
    hbm = pl.BlockSpec(memory_space=pltpu.HBM)
    return pl.pallas_call(
        query_kernel,
        in_specs=[pl.BlockSpec(memory_space=pltpu.SMEM), hbm, hbm, vmem],
        out_specs=[vmem] * parts,
        out_shape=[jax.ShapeDtypeStruct((rows + extra, cols), BF16)] * parts,
        scratch_shapes=[
            pltpu.VMEM((rows, width), BF16),
            pltpu.VMEM((width, width), BF16),
            pltpu.VMEM((rows, width), BF16),
            pltpu.SemaphoreType.DMA((parts + 1,)),
        ],
        compiler_params=pltpu.CompilerParams(vmem_limit_bytes=VMEM - 2 * w_qu.size),
        cost_estimate=cost(2 * rows * width * width, 2 * width * width + 4 * rows * width),
        name="queries",
    )(me, candidates, w_qu, block_owner.reshape(1, blocks))


def assemble_kernel(count, *refs):
    arrived, outs, owner_ref = refs[:count], refs[count:-1], refs[-1]
    blocks = owner_ref.shape[1]
    rows = outs[0].shape[0] // count
    for k, ref in enumerate(arrived):
        for h, out in enumerate(outs):
            out[k * rows : (k + 1) * rows, :] = ref[:rows, h * HEAD : (h + 1) * HEAD]
        below = ref[rows : rows + 16, :HEAD].astype(F32)
        owner_ref[k : k + 1, :] = below[:1, :blocks].astype(jnp.int32)


def assemble(arrived, rows, each, blocks):
    count = len(arrived)
    vmem = pl.BlockSpec(memory_space=pltpu.VMEM)
    made = pl.pallas_call(
        functools.partial(assemble_kernel, count),
        in_specs=[vmem] * count,
        out_specs=[vmem] * (each + 1),
        out_shape=[jax.ShapeDtypeStruct((count * rows, HEAD), BF16)] * each
        + [jax.ShapeDtypeStruct((count, blocks), jnp.int32)],
        compiler_params=room_for(((4, count * rows, each * HEAD), BF16)),
        cost_estimate=cost(0, 4 * count * rows * each * HEAD),
        name="assemble",
    )(*arrived)
    return made[:each], made[each]


def gate_kernel(_, cand_ref, w_ref, out_ref):
    out_ref[0] = silu(jnp.dot(cand_ref[...], w_ref[...], preferred_element_type=F32))


def project_gate(me, candidates, w_qu, parts):
    rows, width = candidates.shape
    cols = width // parts
    return pl.pallas_call(
        gate_kernel,
        grid_spec=scalar_grid(
            (parts,),
            [
                pl.BlockSpec((rows, width), lambda k, m: (0, 0)),
                pl.BlockSpec((width, cols), lambda k, m: (0, parts + (k ^ m[0]))),
            ],
            pl.BlockSpec((1, rows, cols), lambda k, m: (k, 0, 0)),
        ),
        out_shape=jax.ShapeDtypeStruct((parts, rows, cols), F32),
        compiler_params=room_for(
            ((2, width, cols), BF16), ((2, rows, width), BF16), ((4, rows, cols), F32)
        ),
        cost_estimate=cost(2 * rows * width * width, 2 * width * width + 6 * rows * width),
        name="gate",
    )(me, candidates, w_qu)


def keys_values_kernel(count, each, _, hist_ref, *refs):
    weights, outs = refs[: 2 * count], refs[2 * count :]
    for k in range(count):
        keys = silu(jnp.dot(hist_ref[...], weights[2 * k][...], preferred_element_type=F32))
        values = jnp.dot(hist_ref[...], weights[2 * k + 1][...], preferred_element_type=F32)
        for h in range(each):
            out = outs[k * each + h]
            out[:, :HEAD] = keys[:, h * HEAD : (h + 1) * HEAD].astype(BF16)
            out[:, HEAD:] = values[:, h * HEAD : (h + 1) * HEAD].astype(BF16)


def project_keys_values(me, history, w_kv, parts, ks):
    rows, width = history.shape
    cols = width // parts
    each = cols // HEAD
    count = len(ks)
    step = rows // 2

    def weight(k, side):
        return pl.BlockSpec((width, cols), lambda r, m: (0, side * parts + (k ^ m[0])))

    made = pl.pallas_call(
        functools.partial(keys_values_kernel, count, each),
        grid_spec=scalar_grid(
            (rows // step,),
            [pl.BlockSpec((step, width), lambda r, m: (r, 0))]
            + [weight(k, side) for k in ks for side in range(2)],
            [pl.BlockSpec((step, 2 * HEAD), lambda r, m: (r, 0))] * (count * each),
        ),
        out_shape=[jax.ShapeDtypeStruct((rows, 2 * HEAD), BF16)] * (count * each),
        cost_estimate=cost(
            4 * rows * width * cols * count,
            2 * rows * width + 4 * width * cols * count + 4 * rows * cols * count,
        ),
        compiler_params=room_for(
            ((2, step, width), BF16),
            ((4 * count, width, cols), BF16),
            ((4 * count, step, cols), BF16),
            ((2, step, cols), F32),
        ),
    )(me, history, *[w_kv] * (2 * count))
    return [made[k * each : (k + 1) * each] for k in range(count)]


def attend_kernel(source, sink, events, room, pos_ref, count_ref, code_ref, *refs):
    codes = len(source)
    n_q = 1 + max(a for a, _ in source)
    n_out = 1 + max(a for a, _ in sink)
    n_kv = len(refs) - n_q - n_out - 3
    kvs, queries = refs[:n_kv], refs[n_kv : n_kv + n_q]
    outs = refs[n_kv + n_q : n_kv + n_q + n_out]
    packed, asked, total = refs[n_kv + n_q + n_out :]
    blocks = kvs[0].shape[0] // events
    cands = asked.shape[0] // codes
    half = 0.5 * HEAD ** (-0.5)

    def code_tiles(j):
        return lax.div(count_ref[code_ref[j]] * events + (TILE - 1), TILE)

    for j in range(codes):
        at = code_ref[j] * room + (lax.max(code_tiles(j), 1) - 1) * TILE
        packed[pl.ds(pl.multiple_of(at, TILE), TILE), :] = jnp.zeros((TILE, 2 * HEAD), BF16)
    for s, kv in enumerate(kvs):

        def place(b, carry, s=s, kv=kv):
            at = pl.multiple_of(pos_ref[s * blocks + b] * events, events)
            packed[pl.ds(at, events), :] = kv[pl.ds(pl.multiple_of(b * events, events), events), :]
            return carry

        lax.fori_loop(0, blocks, place, 0, unroll=8)
    for j, (array, at) in enumerate(source):
        asked[j * cands : (j + 1) * cands, :] = queries[array][at : at + cands, :]

    def one_code(j, carry):
        code = code_ref[j]
        base = pl.multiple_of(code * room, TILE)
        rows = pl.ds(pl.multiple_of(j * cands, cands), cands)
        tiles = code_tiles(j)
        for number in range(room // TILE + 1):

            @pl.when(tiles == number)
            def _(number=number):
                if number == 0:
                    total[rows, :] = jnp.zeros((cands, HEAD), BF16)
                    return
                at = pl.ds(base, number * TILE)
                scores = lax.dot_general(
                    asked[rows, :],
                    packed[at, :HEAD],
                    (((1,), (1,)), ((), ())),
                    preferred_element_type=F32,
                )
                h = scores * half
                weights = (h + h * jnp.tanh(h)).astype(BF16)
                sums = jnp.dot(weights, packed[at, HEAD:], preferred_element_type=F32)
                total[rows, :] = sums.astype(BF16)

        return carry

    lax.fori_loop(0, codes, one_code, 0)
    for j, (array, at) in enumerate(sink):
        outs[array][at : at + cands, :] = total[j * cands : (j + 1) * cands, :]


def attend(pos, counts, kvs, arrays, where, groups, cands, events, room):
    codes = [c for group in groups for c in group]
    sink = [(g, j * cands) for g, group in enumerate(groups) for j in range(len(group))]
    used = sorted({where[c][0] for c in codes})
    source = [(used.index(where[c][0]), where[c][1]) for c in codes]
    queries = [arrays[a] for a in used]
    rows = sum(kv.shape[0] for kv in kvs)
    n_req = counts.shape[0]
    share = len(codes) / n_req
    vmem = pl.BlockSpec(memory_space=pltpu.VMEM)
    smem = pl.BlockSpec(memory_space=pltpu.SMEM)
    return pl.pallas_call(
        functools.partial(attend_kernel, source, sink, events, room),
        in_specs=[smem] * 3 + [vmem] * (len(kvs) + len(queries)),
        out_specs=[vmem] * len(groups),
        out_shape=[jax.ShapeDtypeStruct((len(g) * cands, HEAD), BF16) for g in groups],
        scratch_shapes=[
            pltpu.VMEM((n_req * room, 2 * HEAD), BF16),
            pltpu.VMEM((len(codes) * cands, HEAD), BF16),
            pltpu.VMEM((len(codes) * cands, HEAD), BF16),
        ],
        compiler_params=room_for(
            ((n_req * room + rows, 2 * HEAD), BF16),
            ((5 * len(codes) * cands, HEAD), BF16),
            ((2, cands, room), F32),
        ),
        cost_estimate=cost(
            8 * rows * cands * HEAD * share,
            4 * rows * HEAD + 4 * len(codes) * cands * HEAD,
            rows * cands * share,
        ),
    )(pos, counts, jnp.array(codes, dtype=jnp.int32), *kvs, *queries)


def finish_kernel(me_ref, cand_ref, gate_ref, w_ref, *refs):
    parts, out_ref = refs[:-1], refs[-1]
    count, _, cols = gate_ref.shape
    width = cand_ref.shape[1]
    each = len(parts) // count
    values = [
        jnp.concatenate([p[...].astype(F32) for p in parts[k * each : (k + 1) * each]], axis=1)
        for k in range(count)
    ]
    mean = sum(jnp.sum(v, axis=1, keepdims=True) for v in values) / width
    values = [v - mean for v in values]
    square = sum(jnp.sum(v * v, axis=1, keepdims=True) for v in values)
    scale = lax.rsqrt(square / width + 1e-05)
    total = cand_ref[...].astype(F32)
    for k, v in enumerate(values):
        mixed = (v * scale * gate_ref[k]).astype(BF16)
        rows = pl.ds(pl.multiple_of((k ^ me_ref[0]) * cols, cols), cols)
        total += jnp.dot(mixed, w_ref[rows, :], preferred_element_type=F32)
    out_ref[...] = total.astype(BF16)


def finish(me, candidates, gate, w_out, parts):
    rows, width = candidates.shape
    vmem = pl.BlockSpec(memory_space=pltpu.VMEM)
    return pl.pallas_call(
        finish_kernel,
        in_specs=[pl.BlockSpec(memory_space=pltpu.SMEM)] + [vmem] * (3 + len(parts)),
        out_specs=vmem,
        out_shape=jax.ShapeDtypeStruct((rows, width), BF16),
        compiler_params=room_for(((width, width), BF16), ((8, rows, width), F32)),
        cost_estimate=cost(2 * rows * width * width, 2 * width * width + 10 * rows * width),
        name="finish",
    )(me, candidates, gate, w_out, *parts)


def stages(count, inner_first):
    outer = []
    bit = count // 2
    while bit >= 2:
        outer.append(2 * bit - 2)
        bit //= 2
    inner = [1] if count > 1 else []
    held, plan = [0], []

    def step(mask, codes):
        plan.append((mask, tuple(codes)))
        held.extend(c ^ mask for c in codes)

    if inner_first:
        for mask in inner + outer:
            step(mask, list(held))
        return plan
    for mask in outer[:-1]:
        step(mask, list(held))
    early = list(held)
    if outer:
        if inner:
            plan.append((1, tuple(early)))
        step(outer[-1], early)
    late = [c for c in held if c not in early] or early
    if inner:
        plan.append((1, tuple(late)))
    return plan


def joined(pieces):
    return pieces[0] if len(pieces) == 1 else jnp.concatenate(pieces, axis=0)


def gather_plan(count, head):
    return stages(count, head % 2 == 1)


def scatter_plan(count):
    return stages(count, False)


def gather_queries(own, plan):
    cands = own.shape[0]
    arrays, where = [own], {0: (0, 0)}
    for mask, codes in plan:
        pieces = [arrays[where[c][0]][where[c][1] : where[c][1] + cands] for c in codes]
        arrays.append(swap(joined(pieces), "req", mask))
        for j, c in enumerate(codes):
            where[c ^ mask] = (len(arrays) - 1, j * cands)
    return arrays, where


def scatter_sums(plan, groups, arrays, cands):
    whole = {tuple(g): a for g, a in zip(groups, arrays)}
    held = {}
    for group, array in zip(groups, arrays):
        for j, c in enumerate(group):
            held[c] = array[j * cands : (j + 1) * cands]
    for number in reversed(range(len(plan))):
        mask, codes = plan[number]
        away = tuple(c ^ mask for c in codes)
        sent = whole[away] if away in whole else joined([held[c].astype(BF16) for c in away])
        got = swap(sent, "req", mask)
        whole = {g: a for g, a in whole.items() if not set(g) & set(codes)}
        for j, c in enumerate(codes):
            held[c] = held[c].astype(F32) + got[j * cands : (j + 1) * cands].astype(F32)
    return held[0]


def on_device(history, block_owner, candidates, w_kv, w_qu, w_out):
    n_req, n_ctx = lax.axis_size("req"), lax.axis_size("ctx")
    rows, width = history.shape
    blocks = block_owner.shape[0]
    events = rows // blocks
    mine = candidates.shape[0]
    cands = mine * n_ctx
    each = width // HEAD // n_ctx
    room = -(-n_ctx * (2 * blocks // n_req) * events // TILE) * TILE
    me_ctx = lax.axis_index("ctx").astype(jnp.int32).reshape(1)
    me_req = lax.axis_index("req").astype(jnp.int32)

    made = project_queries(me_ctx, candidates, w_qu, block_owner, n_ctx)
    arrived = [made[0]] + [swap(made[k], "ctx", k) for k in range(1, n_ctx)]

    far = list(range(n_ctx // 2, n_ctx))
    near = list(range(0, n_ctx // 2))
    made_far = project_keys_values(me_ctx, history, w_kv, n_ctx, far)
    made_near = project_keys_values(me_ctx, history, w_kv, n_ctx, near)
    kvs = []
    for h in range(each):
        kvs.append(
            [
                heads[h] if k == 0 else swap(heads[h], "ctx", k)
                for k, heads in zip(near + far, made_near + made_far)
            ]
        )

    asked, owners = assemble(arrived, mine, each, blocks)
    owners = owners.reshape(-1)
    code = owners ^ me_req
    total_blocks = n_ctx * blocks
    order = jnp.arange(total_blocks, dtype=jnp.int32)
    same = code[:, None] == code[None, :]
    rank = jnp.sum((same & (order[None, :] < order[:, None])).astype(jnp.int32), axis=1)
    pos = code * (room // events) + rank
    counts = jnp.sum(
        (code[None, :] == jnp.arange(n_req, dtype=jnp.int32)[:, None]).astype(jnp.int32), axis=1
    )

    gate = project_gate(me_ctx, candidates, w_qu, n_ctx)

    parts = [[None] * each for _ in range(n_ctx)]
    for h in range(each):
        arrays, where = gather_queries(asked[h], gather_plan(n_req, h))
        plan = scatter_plan(n_req)
        groups = [[c ^ mask for c in codes] for mask, codes in plan] + [[0]]
        sums = {}
        for call in calls_of(n_req, h):
            made = attend(
                pos, counts, kvs[h], arrays, where, [groups[i] for i in call],
                cands, events, room,
            )
            sums.update(zip(call, made))
        total = scatter_sums(plan, groups, [sums[i] for i in range(len(groups))], cands)
        parts[0][h] = total[:mine]
        for k in range(1, n_ctx):
            piece = total[k * mine : (k + 1) * mine].astype(BF16)
            parts[k][h] = swap(piece, "ctx", k)
    return finish(me_ctx, candidates, gate, w_out, [p for row in parts for p in row])


def calls_of(count, head):
    plan = scatter_plan(count)
    everything = list(range(len(plan) + 1))
    inner = [i for i in range(len(plan)) if plan[i][0] == 1]
    if len(inner) < 2:
        return [everything]
    last = inner[-1]
    rest = [i for i in everything if i != last]
    return [rest, [last]] if head % 2 == 0 else [[last], rest]


def solution(mesh):
    placed = (
        P(("req", "ctx"), None),
        P(("req", "ctx"), None),
        P(("req", "ctx"), None),
        P(),
        P(),
        P(),
    )
    return jax.shard_map(
        on_device, mesh=mesh, in_specs=placed, out_specs=P(("req", "ctx"), None), check_vma=False
    )
```

```python
import functools

import jax
import jax.numpy as jnp
from jax import lax
from jax.experimental import pallas as pl
from jax.experimental.pallas import tpu as pltpu
from jax.sharding import PartitionSpec as P


HEAD = 128
TILE = 256
VMEM = 67043328
BF16 = jnp.bfloat16
F32 = jnp.float32


def silu(v):
    h = 0.5 * v
    return h + h * jnp.tanh(h)


def swap(value, axis, mask):
    count = lax.axis_size(axis)
    return lax.ppermute(value, axis, [(i, i ^ mask) for i in range(count)])


def scalar_grid(grid, in_specs, out_specs, scratch_shapes=()):
    return pltpu.PrefetchScalarGridSpec(
        num_scalar_prefetch=1,
        grid=grid,
        in_specs=in_specs,
        out_specs=out_specs,
        scratch_shapes=scratch_shapes,
    )


def room_for(*arrays, extra=0):
    total = extra
    for shape, kind in arrays:
        size = jnp.dtype(kind).itemsize
        for dim in shape:
            size *= dim
        total += size
    return pltpu.CompilerParams(vmem_limit_bytes=int(total * 1.25) + (2 << 20))


def cost(flops, moved, transcendentals=0):
    return pl.CostEstimate(
        flops=int(flops), bytes_accessed=int(moved), transcendentals=int(transcendentals)
    )


def query_kernel(me_ref, cand_hbm, w_hbm, owner_ref, *refs):
    outs, (cand, weight, made, sems) = refs[:-4], refs[-4:]
    rows = cand.shape[0]
    parts = len(outs)
    cols = outs[0].shape[1]
    blocks = owner_ref.shape[1]
    extra = outs[0].shape[0] - rows
    width = cand.shape[1]
    step = width // parts
    fetch = [pltpu.make_async_copy(cand_hbm, cand, sems.at[parts])]
    for k in range(parts):
        at = pl.ds(k * step, step)
        fetch.append(
            pltpu.make_async_copy(w_hbm.at[at, pl.ds(0, width)], weight.at[at, :], sems.at[k])
        )
    for copy in fetch:
        copy.start()
    owners = jnp.broadcast_to(owner_ref[...].astype(F32), (extra, blocks)).astype(BF16)
    for out in outs:
        out[rows:, :] = jnp.zeros((extra, cols), BF16)
        out[rows:, :blocks] = owners
    fetch[0].wait()
    projected = None
    for k in range(parts):
        fetch[k + 1].wait()
        at = slice(k * step, (k + 1) * step)
        part = jnp.dot(cand[:, at], weight[at, :], preferred_element_type=F32)
        projected = part if projected is None else projected + part
    made[...] = silu(projected).astype(BF16)
    for k, out in enumerate(outs):
        at = pl.multiple_of((k ^ me_ref[0]) * cols, cols)
        out[:rows, :] = made[:, pl.ds(at, cols)]


def project_queries(me, candidates, w_qu, block_owner, parts):
    rows, width = candidates.shape
    cols = width // parts
    blocks = block_owner.shape[0]
    extra = 16
    vmem = pl.BlockSpec(memory_space=pltpu.VMEM)
    hbm = pl.BlockSpec(memory_space=pltpu.HBM)
    return pl.pallas_call(
        query_kernel,
        in_specs=[pl.BlockSpec(memory_space=pltpu.SMEM), hbm, hbm, vmem],
        out_specs=[vmem] * parts,
        out_shape=[jax.ShapeDtypeStruct((rows + extra, cols), BF16)] * parts,
        scratch_shapes=[
            pltpu.VMEM((rows, width), BF16),
            pltpu.VMEM((width, width), BF16),
            pltpu.VMEM((rows, width), BF16),
            pltpu.SemaphoreType.DMA((parts + 1,)),
        ],
        compiler_params=pltpu.CompilerParams(vmem_limit_bytes=VMEM - 2 * w_qu.size),
        cost_estimate=cost(2 * rows * width * width, 2 * width * width + 4 * rows * width),
        name="queries",
    )(me, candidates, w_qu, block_owner.reshape(1, blocks))


def assemble_kernel(count, *refs):
    arrived, outs, owner_ref = refs[:count], refs[count:-1], refs[-1]
    blocks = owner_ref.shape[1]
    rows = outs[0].shape[0] // count
    for k, ref in enumerate(arrived):
        for h, out in enumerate(outs):
            out[k * rows : (k + 1) * rows, :] = ref[:rows, h * HEAD : (h + 1) * HEAD]
        below = ref[rows : rows + 16, :HEAD].astype(F32)
        owner_ref[k : k + 1, :] = below[:1, :blocks].astype(jnp.int32)


def assemble(arrived, rows, each, blocks):
    count = len(arrived)
    vmem = pl.BlockSpec(memory_space=pltpu.VMEM)
    made = pl.pallas_call(
        functools.partial(assemble_kernel, count),
        in_specs=[vmem] * count,
        out_specs=[vmem] * (each + 1),
        out_shape=[jax.ShapeDtypeStruct((count * rows, HEAD), BF16)] * each
        + [jax.ShapeDtypeStruct((count, blocks), jnp.int32)],
        compiler_params=room_for(((4, count * rows, each * HEAD), BF16)),
        cost_estimate=cost(0, 4 * count * rows * each * HEAD),
        name="assemble",
    )(*arrived)
    return made[:each], made[each]


def gate_kernel(_, cand_ref, w_ref, out_ref):
    out_ref[0] = silu(jnp.dot(cand_ref[...], w_ref[...], preferred_element_type=F32))


def project_gate(me, candidates, w_qu, parts):
    rows, width = candidates.shape
    cols = width // parts
    return pl.pallas_call(
        gate_kernel,
        grid_spec=scalar_grid(
            (parts,),
            [
                pl.BlockSpec((rows, width), lambda k, m: (0, 0)),
                pl.BlockSpec((width, cols), lambda k, m: (0, parts + (k ^ m[0]))),
            ],
            pl.BlockSpec((1, rows, cols), lambda k, m: (k, 0, 0)),
        ),
        out_shape=jax.ShapeDtypeStruct((parts, rows, cols), F32),
        compiler_params=room_for(
            ((2, width, cols), BF16), ((2, rows, width), BF16), ((4, rows, cols), F32)
        ),
        cost_estimate=cost(2 * rows * width * width, 2 * width * width + 6 * rows * width),
        name="gate",
    )(me, candidates, w_qu)


def keys_values_kernel(count, each, _, hist_ref, *refs):
    weights, outs = refs[: 2 * count], refs[2 * count :]
    for k in range(count):
        keys = silu(jnp.dot(hist_ref[...], weights[2 * k][...], preferred_element_type=F32))
        values = jnp.dot(hist_ref[...], weights[2 * k + 1][...], preferred_element_type=F32)
        for h in range(each):
            out = outs[k * each + h]
            out[:, :HEAD] = keys[:, h * HEAD : (h + 1) * HEAD].astype(BF16)
            out[:, HEAD:] = values[:, h * HEAD : (h + 1) * HEAD].astype(BF16)


def project_keys_values(me, history, w_kv, parts, ks):
    rows, width = history.shape
    cols = width // parts
    each = cols // HEAD
    count = len(ks)
    step = rows // 2

    def weight(k, side):
        return pl.BlockSpec((width, cols), lambda r, m: (0, side * parts + (k ^ m[0])))

    made = pl.pallas_call(
        functools.partial(keys_values_kernel, count, each),
        grid_spec=scalar_grid(
            (rows // step,),
            [pl.BlockSpec((step, width), lambda r, m: (r, 0))]
            + [weight(k, side) for k in ks for side in range(2)],
            [pl.BlockSpec((step, 2 * HEAD), lambda r, m: (r, 0))] * (count * each),
        ),
        out_shape=[jax.ShapeDtypeStruct((rows, 2 * HEAD), BF16)] * (count * each),
        cost_estimate=cost(
            4 * rows * width * cols * count,
            2 * rows * width + 4 * width * cols * count + 4 * rows * cols * count,
        ),
        compiler_params=room_for(
            ((2, step, width), BF16),
            ((4 * count, width, cols), BF16),
            ((4 * count, step, cols), BF16),
            ((2, step, cols), F32),
        ),
    )(me, history, *[w_kv] * (2 * count))
    return [made[k * each : (k + 1) * each] for k in range(count)]


def attend_kernel(source, sink, events, room, pos_ref, count_ref, code_ref, *refs):
    codes = len(source)
    n_q = 1 + max(a for a, _ in source)
    n_out = 1 + max(a for a, _ in sink)
    n_kv = len(refs) - n_q - n_out - 3
    kvs, queries = refs[:n_kv], refs[n_kv : n_kv + n_q]
    outs = refs[n_kv + n_q : n_kv + n_q + n_out]
    packed, asked, total = refs[n_kv + n_q + n_out :]
    blocks = kvs[0].shape[0] // events
    cands = asked.shape[0] // codes
    half = 0.5 * HEAD ** (-0.5)

    def code_tiles(j):
        return lax.div(count_ref[code_ref[j]] * events + (TILE - 1), TILE)

    for j in range(codes):
        at = code_ref[j] * room + (lax.max(code_tiles(j), 1) - 1) * TILE
        packed[pl.ds(pl.multiple_of(at, TILE), TILE), :] = jnp.zeros((TILE, 2 * HEAD), BF16)
    for s, kv in enumerate(kvs):

        def place(b, carry, s=s, kv=kv):
            at = pl.multiple_of(pos_ref[s * blocks + b] * events, events)
            packed[pl.ds(at, events), :] = kv[pl.ds(pl.multiple_of(b * events, events), events), :]
            return carry

        lax.fori_loop(0, blocks, place, 0, unroll=8)
    for j, (array, at) in enumerate(source):
        asked[j * cands : (j + 1) * cands, :] = queries[array][at : at + cands, :]

    def one_code(j, carry):
        code = code_ref[j]
        base = pl.multiple_of(code * room, TILE)
        rows = pl.ds(pl.multiple_of(j * cands, cands), cands)
        tiles = code_tiles(j)
        for number in range(room // TILE + 1):

            @pl.when(tiles == number)
            def _(number=number):
                if number == 0:
                    total[rows, :] = jnp.zeros((cands, HEAD), BF16)
                    return
                at = pl.ds(base, number * TILE)
                scores = lax.dot_general(
                    asked[rows, :],
                    packed[at, :HEAD],
                    (((1,), (1,)), ((), ())),
                    preferred_element_type=F32,
                )
                h = scores * half
                weights = (h + h * jnp.tanh(h)).astype(BF16)
                sums = jnp.dot(weights, packed[at, HEAD:], preferred_element_type=F32)
                total[rows, :] = sums.astype(BF16)

        return carry

    lax.fori_loop(0, codes, one_code, 0)
    for j, (array, at) in enumerate(sink):
        outs[array][at : at + cands, :] = total[j * cands : (j + 1) * cands, :]


def attend(pos, counts, kvs, arrays, where, groups, cands, events, room):
    codes = [c for group in groups for c in group]
    sink = [(g, j * cands) for g, group in enumerate(groups) for j in range(len(group))]
    used = sorted({where[c][0] for c in codes})
    source = [(used.index(where[c][0]), where[c][1]) for c in codes]
    queries = [arrays[a] for a in used]
    rows = sum(kv.shape[0] for kv in kvs)
    n_req = counts.shape[0]
    share = len(codes) / n_req
    vmem = pl.BlockSpec(memory_space=pltpu.VMEM)
    smem = pl.BlockSpec(memory_space=pltpu.SMEM)
    return pl.pallas_call(
        functools.partial(attend_kernel, source, sink, events, room),
        in_specs=[smem] * 3 + [vmem] * (len(kvs) + len(queries)),
        out_specs=[vmem] * len(groups),
        out_shape=[jax.ShapeDtypeStruct((len(g) * cands, HEAD), BF16) for g in groups],
        scratch_shapes=[
            pltpu.VMEM((n_req * room, 2 * HEAD), BF16),
            pltpu.VMEM((len(codes) * cands, HEAD), BF16),
            pltpu.VMEM((len(codes) * cands, HEAD), BF16),
        ],
        compiler_params=room_for(
            ((n_req * room + rows, 2 * HEAD), BF16),
            ((5 * len(codes) * cands, HEAD), BF16),
            ((2, cands, room), F32),
        ),
        cost_estimate=cost(
            8 * rows * cands * HEAD * share,
            4 * rows * HEAD + 4 * len(codes) * cands * HEAD,
            rows * cands * share,
        ),
    )(pos, counts, jnp.array(codes, dtype=jnp.int32), *kvs, *queries)


def finish_kernel(me_ref, cand_ref, gate_ref, w_ref, *refs):
    parts, out_ref = refs[:-1], refs[-1]
    count, _, cols = gate_ref.shape
    width = cand_ref.shape[1]
    each = len(parts) // count
    values = [
        jnp.concatenate([p[...].astype(F32) for p in parts[k * each : (k + 1) * each]], axis=1)
        for k in range(count)
    ]
    mean = sum(jnp.sum(v, axis=1, keepdims=True) for v in values) / width
    values = [v - mean for v in values]
    square = sum(jnp.sum(v * v, axis=1, keepdims=True) for v in values)
    scale = lax.rsqrt(square / width + 1e-05)
    total = cand_ref[...].astype(F32)
    for k, v in enumerate(values):
        mixed = (v * scale * gate_ref[k]).astype(BF16)
        rows = pl.ds(pl.multiple_of((k ^ me_ref[0]) * cols, cols), cols)
        total += jnp.dot(mixed, w_ref[rows, :], preferred_element_type=F32)
    out_ref[...] = total.astype(BF16)


def finish(me, candidates, gate, w_out, parts):
    rows, width = candidates.shape
    vmem = pl.BlockSpec(memory_space=pltpu.VMEM)
    return pl.pallas_call(
        finish_kernel,
        in_specs=[pl.BlockSpec(memory_space=pltpu.SMEM)] + [vmem] * (3 + len(parts)),
        out_specs=vmem,
        out_shape=jax.ShapeDtypeStruct((rows, width), BF16),
        compiler_params=room_for(((width, width), BF16), ((8, rows, width), F32)),
        cost_estimate=cost(2 * rows * width * width, 2 * width * width + 10 * rows * width),
        name="finish",
    )(me, candidates, gate, w_out, *parts)


def stages(count, inner_first):
    outer = []
    bit = count // 2
    while bit >= 2:
        outer.append(2 * bit - 2)
        bit //= 2
    inner = [1] if count > 1 else []
    held, plan = [0], []

    def step(mask, codes):
        plan.append((mask, tuple(codes)))
        held.extend(c ^ mask for c in codes)

    if inner_first:
        for mask in inner + outer:
            step(mask, list(held))
        return plan
    for mask in outer[:-1]:
        step(mask, list(held))
    early = list(held)
    if outer:
        if inner:
            plan.append((1, tuple(early)))
        step(outer[-1], early)
    late = [c for c in held if c not in early] or early
    if inner:
        plan.append((1, tuple(late)))
    return plan


def joined(pieces):
    return pieces[0] if len(pieces) == 1 else jnp.concatenate(pieces, axis=0)


def gather_plan(count, head):
    return stages(count, head % 2 == 1)


def scatter_plan(count):
    return stages(count, False)


def gather_queries(own, plan):
    cands = own.shape[0]
    arrays, where = [own], {0: (0, 0)}
    for mask, codes in plan:
        pieces = [arrays[where[c][0]][where[c][1] : where[c][1] + cands] for c in codes]
        arrays.append(swap(joined(pieces), "req", mask))
        for j, c in enumerate(codes):
            where[c ^ mask] = (len(arrays) - 1, j * cands)
    return arrays, where


def scatter_sums(plan, groups, arrays, cands):
    whole = {tuple(g): a for g, a in zip(groups, arrays)}
    held = {}
    for group, array in zip(groups, arrays):
        for j, c in enumerate(group):
            held[c] = array[j * cands : (j + 1) * cands]
    for number in reversed(range(len(plan))):
        mask, codes = plan[number]
        away = tuple(c ^ mask for c in codes)
        sent = whole[away] if away in whole else joined([held[c].astype(BF16) for c in away])
        got = swap(sent, "req", mask)
        whole = {g: a for g, a in whole.items() if not set(g) & set(codes)}
        for j, c in enumerate(codes):
            held[c] = held[c].astype(F32) + got[j * cands : (j + 1) * cands].astype(F32)
    return held[0]


def on_device(history, block_owner, candidates, w_kv, w_qu, w_out):
    n_req, n_ctx = lax.axis_size("req"), lax.axis_size("ctx")
    rows, width = history.shape
    blocks = block_owner.shape[0]
    events = rows // blocks
    mine = candidates.shape[0]
    cands = mine * n_ctx
    each = width // HEAD // n_ctx
    room = -(-n_ctx * (2 * blocks // n_req) * events // TILE) * TILE
    me_ctx = lax.axis_index("ctx").astype(jnp.int32).reshape(1)
    me_req = lax.axis_index("req").astype(jnp.int32)

    made = project_queries(me_ctx, candidates, w_qu, block_owner, n_ctx)
    arrived = [made[0]] + [swap(made[k], "ctx", k) for k in range(1, n_ctx)]

    far = list(range(n_ctx // 2, n_ctx))
    near = list(range(0, n_ctx // 2))
    made_far = project_keys_values(me_ctx, history, w_kv, n_ctx, far)
    made_near = project_keys_values(me_ctx, history, w_kv, n_ctx, near)
    kvs = []
    for h in range(each):
        kvs.append(
            [
                heads[h] if k == 0 else swap(heads[h], "ctx", k)
                for k, heads in zip(near + far, made_near + made_far)
            ]
        )

    asked, owners = assemble(arrived, mine, each, blocks)
    owners = owners.reshape(-1)
    code = owners ^ me_req
    total_blocks = n_ctx * blocks
    order = jnp.arange(total_blocks, dtype=jnp.int32)
    same = code[:, None] == code[None, :]
    rank = jnp.sum((same & (order[None, :] < order[:, None])).astype(jnp.int32), axis=1)
    pos = code * (room // events) + rank
    counts = jnp.sum(
        (code[None, :] == jnp.arange(n_req, dtype=jnp.int32)[:, None]).astype(jnp.int32), axis=1
    )

    gate = project_gate(me_ctx, candidates, w_qu, n_ctx)

    parts = [[None] * each for _ in range(n_ctx)]
    for h in range(each):
        arrays, where = gather_queries(asked[h], gather_plan(n_req, h))
        plan = scatter_plan(n_req)
        groups = [[c ^ mask for c in codes] for mask, codes in plan] + [[0]]
        sums = {}
        for call in calls_of(n_req, h):
            made = attend(
                pos, counts, kvs[h], arrays, where, [groups[i] for i in call],
                cands, events, room,
            )
            sums.update(zip(call, made))
        total = scatter_sums(plan, groups, [sums[i] for i in range(len(groups))], cands)
        parts[0][h] = total[:mine]
        for k in range(1, n_ctx):
            piece = total[k * mine : (k + 1) * mine].astype(BF16)
            parts[k][h] = swap(piece, "ctx", k)
    return finish(me_ctx, candidates, gate, w_out, [p for row in parts for p in row])


def calls_of(count, head):
    plan = scatter_plan(count)
    everything = list(range(len(plan) + 1))
    inner = [i for i in range(len(plan)) if plan[i][0] == 1]
    if len(inner) < 2:
        return [everything]
    last = inner[-1]
    rest = [i for i in everything if i != last]
    return [rest, [last]] if head % 2 == 0 else [[last], rest]


def solution(mesh):
    placed = (
        P(("req", "ctx"), None),
        P(("req", "ctx"), None),
        P(("req", "ctx"), None),
        P(),
        P(),
        P(),
    )
    return jax.shard_map(
        on_device, mesh=mesh, in_specs=placed, out_specs=P(("req", "ctx"), None), check_vma=False
    )
```

```python
import functools

import jax
import jax.numpy as jnp
from jax import lax
from jax.experimental import pallas as pl
from jax.experimental.pallas import tpu as pltpu
from jax.sharding import PartitionSpec as P


HEAD = 128
TILE = 256
VMEM = 67043328
BF16 = jnp.bfloat16
F32 = jnp.float32


def silu(v):
    h = 0.5 * v
    return h + h * jnp.tanh(h)


def swap(value, axis, mask):
    count = lax.axis_size(axis)
    return lax.ppermute(value, axis, [(i, i ^ mask) for i in range(count)])


def scalar_grid(grid, in_specs, out_specs, scratch_shapes=()):
    return pltpu.PrefetchScalarGridSpec(
        num_scalar_prefetch=1,
        grid=grid,
        in_specs=in_specs,
        out_specs=out_specs,
        scratch_shapes=scratch_shapes,
    )


def room_for(*arrays, extra=0):
    total = extra
    for shape, kind in arrays:
        size = jnp.dtype(kind).itemsize
        for dim in shape:
            size *= dim
        total += size
    return pltpu.CompilerParams(vmem_limit_bytes=int(total * 1.25) + (2 << 20))


def cost(flops, moved, transcendentals=0):
    return pl.CostEstimate(
        flops=int(flops), bytes_accessed=int(moved), transcendentals=int(transcendentals)
    )


def query_kernel(me_ref, cand_hbm, w_hbm, owner_ref, *refs):
    outs, (cand, weight, made, sems) = refs[:-4], refs[-4:]
    rows = cand.shape[0]
    parts = len(outs)
    cols = outs[0].shape[1]
    blocks = owner_ref.shape[1]
    extra = outs[0].shape[0] - rows
    width = cand.shape[1]
    step = width // parts
    fetch = [pltpu.make_async_copy(cand_hbm, cand, sems.at[parts])]
    for k in range(parts):
        at = pl.ds(k * step, step)
        fetch.append(
            pltpu.make_async_copy(w_hbm.at[at, pl.ds(0, width)], weight.at[at, :], sems.at[k])
        )
    for copy in fetch:
        copy.start()
    owners = jnp.broadcast_to(owner_ref[...].astype(F32), (extra, blocks)).astype(BF16)
    for out in outs:
        out[rows:, :] = jnp.zeros((extra, cols), BF16)
        out[rows:, :blocks] = owners
    fetch[0].wait()
    projected = None
    for k in range(parts):
        fetch[k + 1].wait()
        at = slice(k * step, (k + 1) * step)
        part = jnp.dot(cand[:, at], weight[at, :], preferred_element_type=F32)
        projected = part if projected is None else projected + part
    made[...] = silu(projected).astype(BF16)
    for k, out in enumerate(outs):
        at = pl.multiple_of((k ^ me_ref[0]) * cols, cols)
        out[:rows, :] = made[:, pl.ds(at, cols)]


def project_queries(me, candidates, w_qu, block_owner, parts):
    rows, width = candidates.shape
    cols = width // parts
    blocks = block_owner.shape[0]
    extra = 16
    vmem = pl.BlockSpec(memory_space=pltpu.VMEM)
    hbm = pl.BlockSpec(memory_space=pltpu.HBM)
    return pl.pallas_call(
        query_kernel,
        in_specs=[pl.BlockSpec(memory_space=pltpu.SMEM), hbm, hbm, vmem],
        out_specs=[vmem] * parts,
        out_shape=[jax.ShapeDtypeStruct((rows + extra, cols), BF16)] * parts,
        scratch_shapes=[
            pltpu.VMEM((rows, width), BF16),
            pltpu.VMEM((width, width), BF16),
            pltpu.VMEM((rows, width), BF16),
            pltpu.SemaphoreType.DMA((parts + 1,)),
        ],
        compiler_params=pltpu.CompilerParams(vmem_limit_bytes=VMEM - 2 * w_qu.size),
        cost_estimate=cost(2 * rows * width * width, 2 * width * width + 4 * rows * width),
        name="queries",
    )(me, candidates, w_qu, block_owner.reshape(1, blocks))


def assemble_kernel(count, *refs):
    arrived, outs, owner_ref = refs[:count], refs[count:-1], refs[-1]
    blocks = owner_ref.shape[1]
    rows = outs[0].shape[0] // count
    for k, ref in enumerate(arrived):
        for h, out in enumerate(outs):
            out[k * rows : (k + 1) * rows, :] = ref[:rows, h * HEAD : (h + 1) * HEAD]
        below = ref[rows : rows + 16, :HEAD].astype(F32)
        owner_ref[k : k + 1, :] = below[:1, :blocks].astype(jnp.int32)


def assemble(arrived, rows, each, blocks):
    count = len(arrived)
    vmem = pl.BlockSpec(memory_space=pltpu.VMEM)
    made = pl.pallas_call(
        functools.partial(assemble_kernel, count),
        in_specs=[vmem] * count,
        out_specs=[vmem] * (each + 1),
        out_shape=[jax.ShapeDtypeStruct((count * rows, HEAD), BF16)] * each
        + [jax.ShapeDtypeStruct((count, blocks), jnp.int32)],
        compiler_params=room_for(((4, count * rows, each * HEAD), BF16)),
        cost_estimate=cost(0, 4 * count * rows * each * HEAD),
        name="assemble",
    )(*arrived)
    return made[:each], made[each]


def gate_kernel(_, cand_ref, w_ref, out_ref):
    out_ref[0] = silu(jnp.dot(cand_ref[...], w_ref[...], preferred_element_type=F32))


def project_gate(me, candidates, w_qu, parts):
    rows, width = candidates.shape
    cols = width // parts
    return pl.pallas_call(
        gate_kernel,
        grid_spec=scalar_grid(
            (parts,),
            [
                pl.BlockSpec((rows, width), lambda k, m: (0, 0)),
                pl.BlockSpec((width, cols), lambda k, m: (0, parts + (k ^ m[0]))),
            ],
            pl.BlockSpec((1, rows, cols), lambda k, m: (k, 0, 0)),
        ),
        out_shape=jax.ShapeDtypeStruct((parts, rows, cols), F32),
        compiler_params=room_for(
            ((2, width, cols), BF16), ((2, rows, width), BF16), ((4, rows, cols), F32)
        ),
        cost_estimate=cost(2 * rows * width * width, 2 * width * width + 6 * rows * width),
        name="gate",
    )(me, candidates, w_qu)


def keys_values_kernel(count, each, _, hist_ref, *refs):
    weights, outs = refs[: 2 * count], refs[2 * count :]
    for k in range(count):
        keys = silu(jnp.dot(hist_ref[...], weights[2 * k][...], preferred_element_type=F32))
        values = jnp.dot(hist_ref[...], weights[2 * k + 1][...], preferred_element_type=F32)
        for h in range(each):
            out = outs[k * each + h]
            out[:, :HEAD] = keys[:, h * HEAD : (h + 1) * HEAD].astype(BF16)
            out[:, HEAD:] = values[:, h * HEAD : (h + 1) * HEAD].astype(BF16)


def project_keys_values(me, history, w_kv, parts, ks):
    rows, width = history.shape
    cols = width // parts
    each = cols // HEAD
    count = len(ks)
    step = rows // 2

    def weight(k, side):
        return pl.BlockSpec((width, cols), lambda r, m: (0, side * parts + (k ^ m[0])))

    made = pl.pallas_call(
        functools.partial(keys_values_kernel, count, each),
        grid_spec=scalar_grid(
            (rows // step,),
            [pl.BlockSpec((step, width), lambda r, m: (r, 0))]
            + [weight(k, side) for k in ks for side in range(2)],
            [pl.BlockSpec((step, 2 * HEAD), lambda r, m: (r, 0))] * (count * each),
        ),
        out_shape=[jax.ShapeDtypeStruct((rows, 2 * HEAD), BF16)] * (count * each),
        cost_estimate=cost(
            4 * rows * width * cols * count,
            2 * rows * width + 4 * width * cols * count + 4 * rows * cols * count,
        ),
        compiler_params=room_for(
            ((2, step, width), BF16),
            ((4 * count, width, cols), BF16),
            ((4 * count, step, cols), BF16),
            ((2, step, cols), F32),
        ),
    )(me, history, *[w_kv] * (2 * count))
    return [made[k * each : (k + 1) * each] for k in range(count)]


def attend_kernel(source, sink, events, room, pos_ref, count_ref, code_ref, *refs):
    codes = len(source)
    n_q = 1 + max(a for a, _ in source)
    n_out = 1 + max(a for a, _ in sink)
    n_kv = len(refs) - n_q - n_out - 3
    kvs, queries = refs[:n_kv], refs[n_kv : n_kv + n_q]
    outs = refs[n_kv + n_q : n_kv + n_q + n_out]
    packed, asked, total = refs[n_kv + n_q + n_out :]
    blocks = kvs[0].shape[0] // events
    cands = asked.shape[0] // codes
    half = 0.5 * HEAD ** (-0.5)

    def code_tiles(j):
        return lax.div(count_ref[code_ref[j]] * events + (TILE - 1), TILE)

    for j in range(codes):
        at = code_ref[j] * room + (lax.max(code_tiles(j), 1) - 1) * TILE
        packed[pl.ds(pl.multiple_of(at, TILE), TILE), :] = jnp.zeros((TILE, 2 * HEAD), BF16)
    for s, kv in enumerate(kvs):

        def place(b, carry, s=s, kv=kv):
            at = pl.multiple_of(pos_ref[s * blocks + b] * events, events)
            packed[pl.ds(at, events), :] = kv[pl.ds(pl.multiple_of(b * events, events), events), :]
            return carry

        lax.fori_loop(0, blocks, place, 0, unroll=8)
    for j, (array, at) in enumerate(source):
        asked[j * cands : (j + 1) * cands, :] = queries[array][at : at + cands, :]

    def one_code(j, carry):
        code = code_ref[j]
        base = pl.multiple_of(code * room, TILE)
        rows = pl.ds(pl.multiple_of(j * cands, cands), cands)
        tiles = code_tiles(j)
        for number in range(room // TILE + 1):

            @pl.when(tiles == number)
            def _(number=number):
                if number == 0:
                    total[rows, :] = jnp.zeros((cands, HEAD), BF16)
                    return
                at = pl.ds(base, number * TILE)
                scores = lax.dot_general(
                    asked[rows, :],
                    packed[at, :HEAD],
                    (((1,), (1,)), ((), ())),
                    preferred_element_type=F32,
                )
                h = scores * half
                weights = (h + h * jnp.tanh(h)).astype(BF16)
                sums = jnp.dot(weights, packed[at, HEAD:], preferred_element_type=F32)
                total[rows, :] = sums.astype(BF16)

        return carry

    lax.fori_loop(0, codes, one_code, 0)
    for j, (array, at) in enumerate(sink):
        outs[array][at : at + cands, :] = total[j * cands : (j + 1) * cands, :]


def attend(pos, counts, kvs, arrays, where, groups, cands, events, room):
    codes = [c for group in groups for c in group]
    sink = [(g, j * cands) for g, group in enumerate(groups) for j in range(len(group))]
    used = sorted({where[c][0] for c in codes})
    source = [(used.index(where[c][0]), where[c][1]) for c in codes]
    queries = [arrays[a] for a in used]
    rows = sum(kv.shape[0] for kv in kvs)
    n_req = counts.shape[0]
    share = len(codes) / n_req
    vmem = pl.BlockSpec(memory_space=pltpu.VMEM)
    smem = pl.BlockSpec(memory_space=pltpu.SMEM)
    return pl.pallas_call(
        functools.partial(attend_kernel, source, sink, events, room),
        in_specs=[smem] * 3 + [vmem] * (len(kvs) + len(queries)),
        out_specs=[vmem] * len(groups),
        out_shape=[jax.ShapeDtypeStruct((len(g) * cands, HEAD), BF16) for g in groups],
        scratch_shapes=[
            pltpu.VMEM((n_req * room, 2 * HEAD), BF16),
            pltpu.VMEM((len(codes) * cands, HEAD), BF16),
            pltpu.VMEM((len(codes) * cands, HEAD), BF16),
        ],
        compiler_params=room_for(
            ((n_req * room + rows, 2 * HEAD), BF16),
            ((5 * len(codes) * cands, HEAD), BF16),
            ((2, cands, room), F32),
        ),
        cost_estimate=cost(
            8 * rows * cands * HEAD * share,
            4 * rows * HEAD + 4 * len(codes) * cands * HEAD,
            rows * cands * share,
        ),
    )(pos, counts, jnp.array(codes, dtype=jnp.int32), *kvs, *queries)


def finish_kernel(me_ref, cand_ref, gate_ref, w_ref, *refs):
    parts, out_ref = refs[:-1], refs[-1]
    count, _, cols = gate_ref.shape
    width = cand_ref.shape[1]
    each = len(parts) // count
    values = [
        jnp.concatenate([p[...].astype(F32) for p in parts[k * each : (k + 1) * each]], axis=1)
        for k in range(count)
    ]
    mean = sum(jnp.sum(v, axis=1, keepdims=True) for v in values) / width
    values = [v - mean for v in values]
    square = sum(jnp.sum(v * v, axis=1, keepdims=True) for v in values)
    scale = lax.rsqrt(square / width + 1e-05)
    total = cand_ref[...].astype(F32)
    for k, v in enumerate(values):
        mixed = (v * scale * gate_ref[k]).astype(BF16)
        rows = pl.ds(pl.multiple_of((k ^ me_ref[0]) * cols, cols), cols)
        total += jnp.dot(mixed, w_ref[rows, :], preferred_element_type=F32)
    out_ref[...] = total.astype(BF16)


def finish(me, candidates, gate, w_out, parts):
    rows, width = candidates.shape
    vmem = pl.BlockSpec(memory_space=pltpu.VMEM)
    return pl.pallas_call(
        finish_kernel,
        in_specs=[pl.BlockSpec(memory_space=pltpu.SMEM)] + [vmem] * (3 + len(parts)),
        out_specs=vmem,
        out_shape=jax.ShapeDtypeStruct((rows, width), BF16),
        compiler_params=room_for(((width, width), BF16), ((8, rows, width), F32)),
        cost_estimate=cost(2 * rows * width * width, 2 * width * width + 10 * rows * width),
        name="finish",
    )(me, candidates, gate, w_out, *parts)


def stages(count, inner_first):
    outer = []
    bit = count // 2
    while bit >= 2:
        outer.append(2 * bit - 2)
        bit //= 2
    inner = [1] if count > 1 else []
    held, plan = [0], []

    def step(mask, codes):
        plan.append((mask, tuple(codes)))
        held.extend(c ^ mask for c in codes)

    if inner_first:
        for mask in inner + outer:
            step(mask, list(held))
        return plan
    for mask in outer[:-1]:
        step(mask, list(held))
    early = list(held)
    if outer:
        if inner:
            plan.append((1, tuple(early)))
        step(outer[-1], early)
    late = [c for c in held if c not in early] or early
    if inner:
        plan.append((1, tuple(late)))
    return plan


def joined(pieces):
    return pieces[0] if len(pieces) == 1 else jnp.concatenate(pieces, axis=0)


def gather_plan(count, head):
    return stages(count, head % 2 == 1)


def scatter_plan(count):
    outer = [mask for mask, codes in stages(count, True) if mask != 1]
    plan, main, side = [], [0], [1]
    for mask in outer[:-1]:
        plan.append((mask, tuple(main)))
        main += [c ^ mask for c in main]
    plan.append((1, (0,)))
    for mask in outer[:-1]:
        plan.append((mask, tuple(side)))
        side += [c ^ mask for c in side]
    for mask in outer[-1:]:
        plan.append((mask, tuple(main)))
        plan.append((1, tuple(c ^ mask for c in main)))
    return plan


def gather_queries(own, plan):
    cands = own.shape[0]
    arrays, where = [own], {0: (0, 0)}
    for mask, codes in plan:
        pieces = [arrays[where[c][0]][where[c][1] : where[c][1] + cands] for c in codes]
        arrays.append(swap(joined(pieces), "req", mask))
        for j, c in enumerate(codes):
            where[c ^ mask] = (len(arrays) - 1, j * cands)
    return arrays, where


def scatter_sums(plan, groups, arrays, cands):
    whole = {tuple(g): a for g, a in zip(groups, arrays)}
    held = {}
    for group, array in zip(groups, arrays):
        for j, c in enumerate(group):
            held[c] = [(array, j * cands)]
    for number in reversed(range(len(plan))):
        mask, codes = plan[number]
        away = tuple(c ^ mask for c in codes)
        if away in whole:
            sent = whole[away]
        else:
            sums = [sum(a[at : at + cands].astype(F32) for a, at in held[c]) for c in away]
            sent = joined([part.astype(BF16) for part in sums])
        got = swap(sent, "req", mask)
        whole = {g: a for g, a in whole.items() if not set(g) & set(codes)}
        for j, c in enumerate(codes):
            held[c].append((got, j * cands))
    return held[0]


def total_kernel(starts, *refs):
    arrays, outs = refs[: len(starts)], refs[len(starts) :]
    mine = outs[0].shape[0]
    for k, out in enumerate(outs):
        rows = [slice(at + k * mine, at + (k + 1) * mine) for at in starts]
        total = sum(ref[r, :].astype(F32) for ref, r in zip(arrays, rows))
        out[...] = total.astype(out.dtype)


def add_up(terms, cands, count):
    vmem = pl.BlockSpec(memory_space=pltpu.VMEM)
    mine = cands // count
    kinds = [F32] + [BF16] * (count - 1)
    return pl.pallas_call(
        functools.partial(total_kernel, [at for _, at in terms]),
        in_specs=[vmem] * len(terms),
        out_specs=[vmem] * count,
        out_shape=[jax.ShapeDtypeStruct((mine, HEAD), kind) for kind in kinds],
        compiler_params=room_for(*[(a.shape, a.dtype) for a, _ in terms], ((cands, HEAD), F32)),
        cost_estimate=cost(len(terms) * cands * HEAD, 4 * len(terms) * cands * HEAD),
    )(*[a for a, _ in terms])


def on_device(history, block_owner, candidates, w_kv, w_qu, w_out):
    n_req, n_ctx = lax.axis_size("req"), lax.axis_size("ctx")
    rows, width = history.shape
    blocks = block_owner.shape[0]
    events = rows // blocks
    mine = candidates.shape[0]
    cands = mine * n_ctx
    each = width // HEAD // n_ctx
    room = -(-n_ctx * (2 * blocks // n_req) * events // TILE) * TILE
    me_ctx = lax.axis_index("ctx").astype(jnp.int32).reshape(1)
    me_req = lax.axis_index("req").astype(jnp.int32)

    made = project_queries(me_ctx, candidates, w_qu, block_owner, n_ctx)
    arrived = [made[0]] + [swap(made[k], "ctx", k) for k in range(1, n_ctx)]

    far = list(range(n_ctx // 2, n_ctx))
    near = list(range(0, n_ctx // 2))
    made_far = project_keys_values(me_ctx, history, w_kv, n_ctx, far)
    made_near = project_keys_values(me_ctx, history, w_kv, n_ctx, near)
    kvs = []
    for h in range(each):
        kvs.append(
            [
                heads[h] if k == 0 else swap(heads[h], "ctx", k)
                for k, heads in zip(near + far, made_near + made_far)
            ]
        )

    asked, owners = assemble(arrived, mine, each, blocks)
    owners = owners.reshape(-1)
    code = owners ^ me_req
    total_blocks = n_ctx * blocks
    order = jnp.arange(total_blocks, dtype=jnp.int32)
    same = code[:, None] == code[None, :]
    rank = jnp.sum((same & (order[None, :] < order[:, None])).astype(jnp.int32), axis=1)
    pos = code * (room // events) + rank
    counts = jnp.sum(
        (code[None, :] == jnp.arange(n_req, dtype=jnp.int32)[:, None]).astype(jnp.int32), axis=1
    )

    gate = project_gate(me_ctx, candidates, w_qu, n_ctx)

    parts = [[None] * each for _ in range(n_ctx)]
    for h in range(each):
        arrays, where = gather_queries(asked[h], gather_plan(n_req, h))
        plan = scatter_plan(n_req)
        groups = [[c ^ mask for c in codes] for mask, codes in plan] + [[0]]
        sums = {}
        for call in calls_of(n_req, h):
            made = attend(
                pos, counts, kvs[h], arrays, where, [groups[i] for i in call],
                cands, events, room,
            )
            sums.update(zip(call, made))
        terms = scatter_sums(plan, groups, [sums[i] for i in range(len(groups))], cands)
        pieces = add_up(terms, cands, n_ctx)
        for k, piece in enumerate(pieces):
            parts[k][h] = piece if k == 0 else swap(piece, "ctx", k)
    return finish(me_ctx, candidates, gate, w_out, [p for row in parts for p in row])


def calls_of(count, head):
    last = len(scatter_plan(count)) - 1
    rest = [i for i in range(last + 2) if i != last]
    return [rest, [last]] if head % 2 == 0 else [[last], rest]


def solution(mesh):
    placed = (
        P(("req", "ctx"), None),
        P(("req", "ctx"), None),
        P(("req", "ctx"), None),
        P(),
        P(),
        P(),
    )
    return jax.shard_map(
        on_device, mesh=mesh, in_specs=placed, out_specs=P(("req", "ctx"), None), check_vma=False
    )
```

```python
import functools

import jax
import jax.numpy as jnp
from jax import lax
from jax.experimental import pallas as pl
from jax.experimental.pallas import tpu as pltpu
from jax.sharding import PartitionSpec as P


HEAD = 128
TILE = 256
VMEM = 67043328
BF16 = jnp.bfloat16
F32 = jnp.float32


def silu(v):
    h = 0.5 * v
    return h + h * jnp.tanh(h)


def swap(value, axis, mask):
    count = lax.axis_size(axis)
    return lax.ppermute(value, axis, [(i, i ^ mask) for i in range(count)])


def scalar_grid(grid, in_specs, out_specs, scratch_shapes=()):
    return pltpu.PrefetchScalarGridSpec(
        num_scalar_prefetch=1,
        grid=grid,
        in_specs=in_specs,
        out_specs=out_specs,
        scratch_shapes=scratch_shapes,
    )


def room_for(*arrays, extra=0):
    total = extra
    for shape, kind in arrays:
        size = jnp.dtype(kind).itemsize
        for dim in shape:
            size *= dim
        total += size
    return pltpu.CompilerParams(vmem_limit_bytes=int(total * 1.25) + (2 << 20))


def cost(flops, moved, transcendentals=0):
    return pl.CostEstimate(
        flops=int(flops), bytes_accessed=int(moved), transcendentals=int(transcendentals)
    )


def query_kernel(me_ref, cand_hbm, w_hbm, owner_ref, *refs):
    outs, (cand, weight, made, sems) = refs[:-4], refs[-4:]
    rows = cand.shape[0]
    parts = len(outs)
    cols = outs[0].shape[1]
    blocks = owner_ref.shape[1]
    extra = outs[0].shape[0] - rows
    width = cand.shape[1]
    step = width // parts
    fetch = [pltpu.make_async_copy(cand_hbm, cand, sems.at[parts])]
    for k in range(parts):
        at = pl.ds(k * step, step)
        fetch.append(
            pltpu.make_async_copy(w_hbm.at[at, pl.ds(0, width)], weight.at[at, :], sems.at[k])
        )
    for copy in fetch:
        copy.start()
    owners = jnp.broadcast_to(owner_ref[...].astype(F32), (extra, blocks)).astype(BF16)
    for out in outs:
        out[rows:, :] = jnp.zeros((extra, cols), BF16)
        out[rows:, :blocks] = owners
    fetch[0].wait()
    projected = None
    for k in range(parts):
        fetch[k + 1].wait()
        at = slice(k * step, (k + 1) * step)
        part = jnp.dot(cand[:, at], weight[at, :], preferred_element_type=F32)
        projected = part if projected is None else projected + part
    made[...] = silu(projected).astype(BF16)
    for k, out in enumerate(outs):
        at = pl.multiple_of((k ^ me_ref[0]) * cols, cols)
        out[:rows, :] = made[:, pl.ds(at, cols)]


def project_queries(me, candidates, w_qu, block_owner, parts):
    rows, width = candidates.shape
    cols = width // parts
    blocks = block_owner.shape[0]
    extra = 16
    vmem = pl.BlockSpec(memory_space=pltpu.VMEM)
    hbm = pl.BlockSpec(memory_space=pltpu.HBM)
    return pl.pallas_call(
        query_kernel,
        in_specs=[pl.BlockSpec(memory_space=pltpu.SMEM), hbm, hbm, vmem],
        out_specs=[vmem] * parts,
        out_shape=[jax.ShapeDtypeStruct((rows + extra, cols), BF16)] * parts,
        scratch_shapes=[
            pltpu.VMEM((rows, width), BF16),
            pltpu.VMEM((width, width), BF16),
            pltpu.VMEM((rows, width), BF16),
            pltpu.SemaphoreType.DMA((parts + 1,)),
        ],
        compiler_params=pltpu.CompilerParams(vmem_limit_bytes=VMEM - 2 * w_qu.size),
        cost_estimate=cost(2 * rows * width * width, 2 * width * width + 4 * rows * width),
        name="queries",
    )(me, candidates, w_qu, block_owner.reshape(1, blocks))


def assemble_kernel(count, *refs):
    arrived, outs, owner_ref = refs[:count], refs[count:-1], refs[-1]
    blocks = owner_ref.shape[1]
    rows = outs[0].shape[0] // count
    for k, ref in enumerate(arrived):
        for h, out in enumerate(outs):
            out[k * rows : (k + 1) * rows, :] = ref[:rows, h * HEAD : (h + 1) * HEAD]
        below = ref[rows : rows + 16, :HEAD].astype(F32)
        owner_ref[k : k + 1, :] = below[:1, :blocks].astype(jnp.int32)


def assemble(arrived, rows, each, blocks):
    count = len(arrived)
    vmem = pl.BlockSpec(memory_space=pltpu.VMEM)
    made = pl.pallas_call(
        functools.partial(assemble_kernel, count),
        in_specs=[vmem] * count,
        out_specs=[vmem] * (each + 1),
        out_shape=[jax.ShapeDtypeStruct((count * rows, HEAD), BF16)] * each
        + [jax.ShapeDtypeStruct((count, blocks), jnp.int32)],
        compiler_params=room_for(((4, count * rows, each * HEAD), BF16)),
        cost_estimate=cost(0, 4 * count * rows * each * HEAD),
        name="assemble",
    )(*arrived)
    return made[:each], made[each]


def gate_kernel(_, cand_ref, w_ref, out_ref):
    out_ref[0] = silu(jnp.dot(cand_ref[...], w_ref[...], preferred_element_type=F32))


def project_gate(me, candidates, w_qu, parts):
    rows, width = candidates.shape
    cols = width // parts
    return pl.pallas_call(
        gate_kernel,
        grid_spec=scalar_grid(
            (parts,),
            [
                pl.BlockSpec((rows, width), lambda k, m: (0, 0)),
                pl.BlockSpec((width, cols), lambda k, m: (0, parts + (k ^ m[0]))),
            ],
            pl.BlockSpec((1, rows, cols), lambda k, m: (k, 0, 0)),
        ),
        out_shape=jax.ShapeDtypeStruct((parts, rows, cols), F32),
        compiler_params=room_for(
            ((2, width, cols), BF16), ((2, rows, width), BF16), ((4, rows, cols), F32)
        ),
        cost_estimate=cost(2 * rows * width * width, 2 * width * width + 6 * rows * width),
        name="gate",
    )(me, candidates, w_qu)


def keys_values_kernel(count, each, _, hist_ref, *refs):
    weights, outs = refs[: 2 * count], refs[2 * count :]
    for k in range(count):
        keys = silu(jnp.dot(hist_ref[...], weights[2 * k][...], preferred_element_type=F32))
        values = jnp.dot(hist_ref[...], weights[2 * k + 1][...], preferred_element_type=F32)
        for h in range(each):
            out = outs[k * each + h]
            out[:, :HEAD] = keys[:, h * HEAD : (h + 1) * HEAD].astype(BF16)
            out[:, HEAD:] = values[:, h * HEAD : (h + 1) * HEAD].astype(BF16)


def project_keys_values(me, history, w_kv, parts, ks):
    rows, width = history.shape
    cols = width // parts
    each = cols // HEAD
    count = len(ks)
    step = rows // 2

    def weight(k, side):
        return pl.BlockSpec((width, cols), lambda r, m: (0, side * parts + (k ^ m[0])))

    made = pl.pallas_call(
        functools.partial(keys_values_kernel, count, each),
        grid_spec=scalar_grid(
            (rows // step,),
            [pl.BlockSpec((step, width), lambda r, m: (r, 0))]
            + [weight(k, side) for k in ks for side in range(2)],
            [pl.BlockSpec((step, 2 * HEAD), lambda r, m: (r, 0))] * (count * each),
        ),
        out_shape=[jax.ShapeDtypeStruct((rows, 2 * HEAD), BF16)] * (count * each),
        cost_estimate=cost(
            4 * rows * width * cols * count,
            2 * rows * width + 4 * width * cols * count + 4 * rows * cols * count,
        ),
        compiler_params=room_for(
            ((2, step, width), BF16),
            ((4 * count, width, cols), BF16),
            ((4 * count, step, cols), BF16),
            ((2, step, cols), F32),
        ),
    )(me, history, *[w_kv] * (2 * count))
    return [made[k * each : (k + 1) * each] for k in range(count)]


def attend_kernel(source, sink, events, room, pos_ref, count_ref, code_ref, *refs):
    codes = len(source)
    n_q = 1 + max(a for a, _ in source)
    n_out = 1 + max(a for a, _ in sink)
    n_kv = len(refs) - n_q - n_out - 3
    kvs, queries = refs[:n_kv], refs[n_kv : n_kv + n_q]
    outs = refs[n_kv + n_q : n_kv + n_q + n_out]
    packed, asked, total = refs[n_kv + n_q + n_out :]
    blocks = kvs[0].shape[0] // events
    cands = asked.shape[0] // codes
    half = 0.5 * HEAD ** (-0.5)

    def code_tiles(j):
        return lax.div(count_ref[code_ref[j]] * events + (TILE - 1), TILE)

    for j in range(codes):
        at = code_ref[j] * room + (lax.max(code_tiles(j), 1) - 1) * TILE
        packed[pl.ds(pl.multiple_of(at, TILE), TILE), :] = jnp.zeros((TILE, 2 * HEAD), BF16)
    for s, kv in enumerate(kvs):

        def place(b, carry, s=s, kv=kv):
            at = pl.multiple_of(pos_ref[s * blocks + b] * events, events)
            packed[pl.ds(at, events), :] = kv[pl.ds(pl.multiple_of(b * events, events), events), :]
            return carry

        lax.fori_loop(0, blocks, place, 0, unroll=8)
    for j, (array, at) in enumerate(source):
        asked[j * cands : (j + 1) * cands, :] = queries[array][at : at + cands, :]

    def one_code(j, carry):
        code = code_ref[j]
        base = pl.multiple_of(code * room, TILE)
        rows = pl.ds(pl.multiple_of(j * cands, cands), cands)
        tiles = code_tiles(j)
        for number in range(room // TILE + 1):

            @pl.when(tiles == number)
            def _(number=number):
                if number == 0:
                    total[rows, :] = jnp.zeros((cands, HEAD), BF16)
                    return
                at = pl.ds(base, number * TILE)
                scores = lax.dot_general(
                    asked[rows, :],
                    packed[at, :HEAD],
                    (((1,), (1,)), ((), ())),
                    preferred_element_type=F32,
                )
                h = scores * half
                weights = (h + h * jnp.tanh(h)).astype(BF16)
                sums = jnp.dot(weights, packed[at, HEAD:], preferred_element_type=F32)
                total[rows, :] = sums.astype(BF16)

        return carry

    lax.fori_loop(0, codes, one_code, 0)
    for j, (array, at) in enumerate(sink):
        outs[array][at : at + cands, :] = total[j * cands : (j + 1) * cands, :]


def attend(pos, counts, kvs, arrays, where, groups, cands, events, room):
    codes = [c for group in groups for c in group]
    sink = [(g, j * cands) for g, group in enumerate(groups) for j in range(len(group))]
    used = sorted({where[c][0] for c in codes})
    source = [(used.index(where[c][0]), where[c][1]) for c in codes]
    queries = [arrays[a] for a in used]
    rows = sum(kv.shape[0] for kv in kvs)
    n_req = counts.shape[0]
    share = len(codes) / n_req
    vmem = pl.BlockSpec(memory_space=pltpu.VMEM)
    smem = pl.BlockSpec(memory_space=pltpu.SMEM)
    return pl.pallas_call(
        functools.partial(attend_kernel, source, sink, events, room),
        in_specs=[smem] * 3 + [vmem] * (len(kvs) + len(queries)),
        out_specs=[vmem] * len(groups),
        out_shape=[jax.ShapeDtypeStruct((len(g) * cands, HEAD), BF16) for g in groups],
        scratch_shapes=[
            pltpu.VMEM((n_req * room, 2 * HEAD), BF16),
            pltpu.VMEM((len(codes) * cands, HEAD), BF16),
            pltpu.VMEM((len(codes) * cands, HEAD), BF16),
        ],
        compiler_params=room_for(
            ((n_req * room + rows, 2 * HEAD), BF16),
            ((5 * len(codes) * cands, HEAD), BF16),
            ((2, cands, room), F32),
        ),
        cost_estimate=cost(
            8 * rows * cands * HEAD * share,
            4 * rows * HEAD + 4 * len(codes) * cands * HEAD,
            rows * cands * share,
        ),
    )(pos, counts, jnp.array(codes, dtype=jnp.int32), *kvs, *queries)


def finish_kernel(me_ref, cand_ref, gate_ref, w_ref, *refs):
    parts, out_ref = refs[:-1], refs[-1]
    count, _, cols = gate_ref.shape
    width = cand_ref.shape[1]
    each = len(parts) // count
    values = [
        jnp.concatenate([p[...].astype(F32) for p in parts[k * each : (k + 1) * each]], axis=1)
        for k in range(count)
    ]
    mean = sum(jnp.sum(v, axis=1, keepdims=True) for v in values) / width
    values = [v - mean for v in values]
    square = sum(jnp.sum(v * v, axis=1, keepdims=True) for v in values)
    scale = lax.rsqrt(square / width + 1e-05)
    total = cand_ref[...].astype(F32)
    for k, v in enumerate(values):
        mixed = (v * scale * gate_ref[k]).astype(BF16)
        rows = pl.ds(pl.multiple_of((k ^ me_ref[0]) * cols, cols), cols)
        total += jnp.dot(mixed, w_ref[rows, :], preferred_element_type=F32)
    out_ref[...] = total.astype(BF16)


def finish(me, candidates, gate, w_out, parts):
    rows, width = candidates.shape
    vmem = pl.BlockSpec(memory_space=pltpu.VMEM)
    return pl.pallas_call(
        finish_kernel,
        in_specs=[pl.BlockSpec(memory_space=pltpu.SMEM)] + [vmem] * (3 + len(parts)),
        out_specs=vmem,
        out_shape=jax.ShapeDtypeStruct((rows, width), BF16),
        compiler_params=room_for(((width, width), BF16), ((8, rows, width), F32)),
        cost_estimate=cost(2 * rows * width * width, 2 * width * width + 10 * rows * width),
        name="finish",
    )(me, candidates, gate, w_out, *parts)


def stages(count, inner_first):
    outer = []
    bit = count // 2
    while bit >= 2:
        outer.append(2 * bit - 2)
        bit //= 2
    inner = [1] if count > 1 else []
    held, plan = [0], []

    def step(mask, codes):
        plan.append((mask, tuple(codes)))
        held.extend(c ^ mask for c in codes)

    if inner_first:
        for mask in inner + outer:
            step(mask, list(held))
        return plan
    for mask in outer[:-1]:
        step(mask, list(held))
    early = list(held)
    if outer:
        if inner:
            plan.append((1, tuple(early)))
        step(outer[-1], early)
    late = [c for c in held if c not in early] or early
    if inner:
        plan.append((1, tuple(late)))
    return plan


def joined(pieces):
    return pieces[0] if len(pieces) == 1 else jnp.concatenate(pieces, axis=0)


def gather_plan(count, head):
    plan = stages(count, head % 2 == 1)
    if head % 2 == 1:
        mask, codes = plan.pop()
        cut = len(codes) // 2
        plan += [(mask, half) for half in (codes[:cut], codes[cut:]) if half]
    return plan


def scatter_plan(count, head):
    if head % 2 == 1:
        return stages(count, False)
    outer = [mask for mask, codes in stages(count, True) if mask != 1]
    plan, main, side = [], [0], [1]
    for mask in outer[:-1]:
        plan.append((mask, tuple(main)))
        main += [c ^ mask for c in main]
    plan.append((1, (0,)))
    for mask in outer[:-1]:
        plan.append((mask, tuple(side)))
        side += [c ^ mask for c in side]
    for mask in outer[-1:]:
        plan.append((mask, tuple(main)))
        plan.append((1, tuple(c ^ mask for c in main)))
    return plan


def gather_queries(own, plan):
    cands = own.shape[0]
    arrays, where = [own], {0: (0, 0)}
    for mask, codes in plan:
        pieces = [arrays[where[c][0]][where[c][1] : where[c][1] + cands] for c in codes]
        arrays.append(swap(joined(pieces), "req", mask))
        for j, c in enumerate(codes):
            where[c ^ mask] = (len(arrays) - 1, j * cands)
    return arrays, where


def scatter_sums(plan, groups, arrays, cands):
    whole = {tuple(g): a for g, a in zip(groups, arrays)}
    held = {}
    for group, array in zip(groups, arrays):
        for j, c in enumerate(group):
            held[c] = [(array, j * cands)]
    for number in reversed(range(len(plan))):
        mask, codes = plan[number]
        away = tuple(c ^ mask for c in codes)
        if away in whole:
            sent = whole[away]
        else:
            sums = [sum(a[at : at + cands].astype(F32) for a, at in held[c]) for c in away]
            sent = joined([part.astype(BF16) for part in sums])
        got = swap(sent, "req", mask)
        whole = {g: a for g, a in whole.items() if not set(g) & set(codes)}
        for j, c in enumerate(codes):
            held[c].append((got, j * cands))
    return held[0]


def total_kernel(starts, *refs):
    arrays, outs = refs[: len(starts)], refs[len(starts) :]
    mine = outs[0].shape[0]
    for k, out in enumerate(outs):
        rows = [slice(at + k * mine, at + (k + 1) * mine) for at in starts]
        total = sum(ref[r, :].astype(F32) for ref, r in zip(arrays, rows))
        out[...] = total.astype(out.dtype)


def add_up(terms, cands, count):
    vmem = pl.BlockSpec(memory_space=pltpu.VMEM)
    mine = cands // count
    kinds = [F32] + [BF16] * (count - 1)
    return pl.pallas_call(
        functools.partial(total_kernel, [at for _, at in terms]),
        in_specs=[vmem] * len(terms),
        out_specs=[vmem] * count,
        out_shape=[jax.ShapeDtypeStruct((mine, HEAD), kind) for kind in kinds],
        compiler_params=room_for(*[(a.shape, a.dtype) for a, _ in terms], ((cands, HEAD), F32)),
        cost_estimate=cost(len(terms) * cands * HEAD, 4 * len(terms) * cands * HEAD),
    )(*[a for a, _ in terms])


def on_device(history, block_owner, candidates, w_kv, w_qu, w_out):
    n_req, n_ctx = lax.axis_size("req"), lax.axis_size("ctx")
    rows, width = history.shape
    blocks = block_owner.shape[0]
    events = rows // blocks
    mine = candidates.shape[0]
    cands = mine * n_ctx
    each = width // HEAD // n_ctx
    room = -(-n_ctx * (2 * blocks // n_req) * events // TILE) * TILE
    me_ctx = lax.axis_index("ctx").astype(jnp.int32).reshape(1)
    me_req = lax.axis_index("req").astype(jnp.int32)

    made = project_queries(me_ctx, candidates, w_qu, block_owner, n_ctx)
    arrived = [made[0]] + [swap(made[k], "ctx", k) for k in range(1, n_ctx)]

    far = list(range(n_ctx // 2, n_ctx))
    near = list(range(0, n_ctx // 2))
    made_far = project_keys_values(me_ctx, history, w_kv, n_ctx, far)
    made_near = project_keys_values(me_ctx, history, w_kv, n_ctx, near)
    kvs = []
    for h in range(each):
        kvs.append(
            [
                heads[h] if k == 0 else swap(heads[h], "ctx", k)
                for k, heads in zip(near + far, made_near + made_far)
            ]
        )

    asked, owners = assemble(arrived, mine, each, blocks)
    owners = owners.reshape(-1)
    code = owners ^ me_req
    total_blocks = n_ctx * blocks
    order = jnp.arange(total_blocks, dtype=jnp.int32)
    same = code[:, None] == code[None, :]
    rank = jnp.sum((same & (order[None, :] < order[:, None])).astype(jnp.int32), axis=1)
    pos = code * (room // events) + rank
    counts = jnp.sum(
        (code[None, :] == jnp.arange(n_req, dtype=jnp.int32)[:, None]).astype(jnp.int32), axis=1
    )

    gate = project_gate(me_ctx, candidates, w_qu, n_ctx)

    parts = [[None] * each for _ in range(n_ctx)]
    for h in range(each):
        arrays, where = gather_queries(asked[h], gather_plan(n_req, h))
        plan = scatter_plan(n_req, h)
        groups = [[c ^ mask for c in codes] for mask, codes in plan] + [[0]]
        sums = {}
        for call in calls_of(n_req, h):
            made = attend(
                pos, counts, kvs[h], arrays, where, [groups[i] for i in call],
                cands, events, room,
            )
            sums.update(zip(call, made))
        terms = scatter_sums(plan, groups, [sums[i] for i in range(len(groups))], cands)
        pieces = add_up(terms, cands, n_ctx)
        for k, piece in enumerate(pieces):
            parts[k][h] = piece if k == 0 else swap(piece, "ctx", k)
    return finish(me_ctx, candidates, gate, w_out, [p for row in parts for p in row])


def calls_of(count, head):
    last = len(scatter_plan(count, head)) - 1
    rest = [i for i in range(last + 2) if i != last]
    return [rest, [last]] if head % 2 == 0 else [[last], rest]


def solution(mesh):
    placed = (
        P(("req", "ctx"), None),
        P(("req", "ctx"), None),
        P(("req", "ctx"), None),
        P(),
        P(),
        P(),
    )
    return jax.shard_map(
        on_device, mesh=mesh, in_specs=placed, out_specs=P(("req", "ctx"), None), check_vma=False
    )
```

```python
import functools

import jax
import jax.numpy as jnp
from jax import lax
from jax.experimental import pallas as pl
from jax.experimental.pallas import tpu as pltpu
from jax.sharding import PartitionSpec as P


HEAD = 128
TILE = 256
VMEM = 67043328
BF16 = jnp.bfloat16
F32 = jnp.float32


def silu(v):
    h = 0.5 * v
    return h + h * jnp.tanh(h)


def swap(value, axis, mask):
    count = lax.axis_size(axis)
    return lax.ppermute(value, axis, [(i, i ^ mask) for i in range(count)])


def scalar_grid(grid, in_specs, out_specs, scratch_shapes=()):
    return pltpu.PrefetchScalarGridSpec(
        num_scalar_prefetch=1,
        grid=grid,
        in_specs=in_specs,
        out_specs=out_specs,
        scratch_shapes=scratch_shapes,
    )


def room_for(*arrays, extra=0):
    total = extra
    for shape, kind in arrays:
        size = jnp.dtype(kind).itemsize
        for dim in shape:
            size *= dim
        total += size
    return pltpu.CompilerParams(vmem_limit_bytes=int(total * 1.25) + (2 << 20))


def cost(flops, moved, transcendentals=0):
    return pl.CostEstimate(
        flops=int(flops), bytes_accessed=int(moved), transcendentals=int(transcendentals)
    )


def query_kernel(me_ref, cand_hbm, w_hbm, owner_ref, *refs):
    outs, (cand, weight, made, sems) = refs[:-4], refs[-4:]
    rows = cand.shape[0]
    parts = len(outs)
    cols = outs[0].shape[1]
    blocks = owner_ref.shape[1]
    extra = outs[0].shape[0] - rows
    width = cand.shape[1]
    step = width // parts
    fetch = [pltpu.make_async_copy(cand_hbm, cand, sems.at[parts])]
    for k in range(parts):
        at = pl.ds(k * step, step)
        fetch.append(
            pltpu.make_async_copy(w_hbm.at[at, pl.ds(0, width)], weight.at[at, :], sems.at[k])
        )
    for copy in fetch:
        copy.start()
    owners = jnp.broadcast_to(owner_ref[...].astype(F32), (extra, blocks)).astype(BF16)
    for out in outs:
        out[rows:, :] = jnp.zeros((extra, cols), BF16)
        out[rows:, :blocks] = owners
    fetch[0].wait()
    projected = None
    for k in range(parts):
        fetch[k + 1].wait()
        at = slice(k * step, (k + 1) * step)
        part = jnp.dot(cand[:, at], weight[at, :], preferred_element_type=F32)
        projected = part if projected is None else projected + part
    made[...] = silu(projected).astype(BF16)
    for k, out in enumerate(outs):
        at = pl.multiple_of((k ^ me_ref[0]) * cols, cols)
        out[:rows, :] = made[:, pl.ds(at, cols)]


def project_queries(me, candidates, w_qu, block_owner, parts):
    rows, width = candidates.shape
    cols = width // parts
    blocks = block_owner.shape[0]
    extra = 16
    vmem = pl.BlockSpec(memory_space=pltpu.VMEM)
    hbm = pl.BlockSpec(memory_space=pltpu.HBM)
    return pl.pallas_call(
        query_kernel,
        in_specs=[pl.BlockSpec(memory_space=pltpu.SMEM), hbm, hbm, vmem],
        out_specs=[vmem] * parts,
        out_shape=[jax.ShapeDtypeStruct((rows + extra, cols), BF16)] * parts,
        scratch_shapes=[
            pltpu.VMEM((rows, width), BF16),
            pltpu.VMEM((width, width), BF16),
            pltpu.VMEM((rows, width), BF16),
            pltpu.SemaphoreType.DMA((parts + 1,)),
        ],
        compiler_params=pltpu.CompilerParams(vmem_limit_bytes=VMEM - 2 * w_qu.size),
        cost_estimate=cost(2 * rows * width * width, 2 * width * width + 4 * rows * width),
        name="queries",
    )(me, candidates, w_qu, block_owner.reshape(1, blocks))


def assemble_kernel(count, *refs):
    arrived, outs, owner_ref = refs[:count], refs[count:-1], refs[-1]
    blocks = owner_ref.shape[1]
    rows = outs[0].shape[0] // count
    for k, ref in enumerate(arrived):
        for h, out in enumerate(outs):
            out[k * rows : (k + 1) * rows, :] = ref[:rows, h * HEAD : (h + 1) * HEAD]
        below = ref[rows : rows + 16, :HEAD].astype(F32)
        owner_ref[k : k + 1, :] = below[:1, :blocks].astype(jnp.int32)


def assemble(arrived, rows, each, blocks):
    count = len(arrived)
    vmem = pl.BlockSpec(memory_space=pltpu.VMEM)
    made = pl.pallas_call(
        functools.partial(assemble_kernel, count),
        in_specs=[vmem] * count,
        out_specs=[vmem] * (each + 1),
        out_shape=[jax.ShapeDtypeStruct((count * rows, HEAD), BF16)] * each
        + [jax.ShapeDtypeStruct((count, blocks), jnp.int32)],
        compiler_params=room_for(((4, count * rows, each * HEAD), BF16)),
        cost_estimate=cost(0, 4 * count * rows * each * HEAD),
        name="assemble",
    )(*arrived)
    return made[:each], made[each]


def gate_kernel(_, cand_ref, w_ref, out_ref):
    out_ref[0] = silu(jnp.dot(cand_ref[...], w_ref[...], preferred_element_type=F32))


def project_gate(me, candidates, w_qu, parts):
    rows, width = candidates.shape
    cols = width // parts
    return pl.pallas_call(
        gate_kernel,
        grid_spec=scalar_grid(
            (parts,),
            [
                pl.BlockSpec((rows, width), lambda k, m: (0, 0)),
                pl.BlockSpec((width, cols), lambda k, m: (0, parts + (k ^ m[0]))),
            ],
            pl.BlockSpec((1, rows, cols), lambda k, m: (k, 0, 0)),
        ),
        out_shape=jax.ShapeDtypeStruct((parts, rows, cols), F32),
        compiler_params=room_for(
            ((2, width, cols), BF16), ((2, rows, width), BF16), ((4, rows, cols), F32)
        ),
        cost_estimate=cost(2 * rows * width * width, 2 * width * width + 6 * rows * width),
        name="gate",
    )(me, candidates, w_qu)


def keys_values_kernel(count, each, _, hist_ref, *refs):
    weights, outs = refs[: 2 * count], refs[2 * count :]
    for k in range(count):
        keys = silu(jnp.dot(hist_ref[...], weights[2 * k][...], preferred_element_type=F32))
        values = jnp.dot(hist_ref[...], weights[2 * k + 1][...], preferred_element_type=F32)
        for h in range(each):
            out = outs[k * each + h]
            out[:, :HEAD] = keys[:, h * HEAD : (h + 1) * HEAD].astype(BF16)
            out[:, HEAD:] = values[:, h * HEAD : (h + 1) * HEAD].astype(BF16)


def project_keys_values(me, history, w_kv, parts, ks):
    rows, width = history.shape
    cols = width // parts
    each = cols // HEAD
    count = len(ks)
    step = rows // 2

    def weight(k, side):
        return pl.BlockSpec((width, cols), lambda r, m: (0, side * parts + (k ^ m[0])))

    made = pl.pallas_call(
        functools.partial(keys_values_kernel, count, each),
        grid_spec=scalar_grid(
            (rows // step,),
            [pl.BlockSpec((step, width), lambda r, m: (r, 0))]
            + [weight(k, side) for k in ks for side in range(2)],
            [pl.BlockSpec((step, 2 * HEAD), lambda r, m: (r, 0))] * (count * each),
        ),
        out_shape=[jax.ShapeDtypeStruct((rows, 2 * HEAD), BF16)] * (count * each),
        cost_estimate=cost(
            4 * rows * width * cols * count,
            2 * rows * width + 4 * width * cols * count + 4 * rows * cols * count,
        ),
        compiler_params=room_for(
            ((2, step, width), BF16),
            ((4 * count, width, cols), BF16),
            ((4 * count, step, cols), BF16),
            ((2, step, cols), F32),
        ),
    )(me, history, *[w_kv] * (2 * count))
    return [made[k * each : (k + 1) * each] for k in range(count)]


def attend_kernel(source, sink, events, room, pos_ref, count_ref, code_ref, *refs):
    codes = len(source)
    n_q = 1 + max(a for a, _ in source)
    n_out = 1 + max(a for a, _ in sink)
    n_kv = len(refs) - n_q - n_out - 3
    kvs, queries = refs[:n_kv], refs[n_kv : n_kv + n_q]
    outs = refs[n_kv + n_q : n_kv + n_q + n_out]
    packed, asked, total = refs[n_kv + n_q + n_out :]
    blocks = kvs[0].shape[0] // events
    cands = asked.shape[0] // codes
    half = 0.5 * HEAD ** (-0.5)

    def code_tiles(j):
        return lax.div(count_ref[code_ref[j]] * events + (TILE - 1), TILE)

    for j in range(codes):
        at = code_ref[j] * room + (lax.max(code_tiles(j), 1) - 1) * TILE
        packed[pl.ds(pl.multiple_of(at, TILE), TILE), :] = jnp.zeros((TILE, 2 * HEAD), BF16)
    for s, kv in enumerate(kvs):

        def place(b, carry, s=s, kv=kv):
            at = pl.multiple_of(pos_ref[s * blocks + b] * events, events)
            packed[pl.ds(at, events), :] = kv[pl.ds(pl.multiple_of(b * events, events), events), :]
            return carry

        lax.fori_loop(0, blocks, place, 0, unroll=8)
    for j, (array, at) in enumerate(source):
        asked[j * cands : (j + 1) * cands, :] = queries[array][at : at + cands, :]

    def one_code(j, carry):
        code = code_ref[j]
        base = pl.multiple_of(code * room, TILE)
        rows = pl.ds(pl.multiple_of(j * cands, cands), cands)
        tiles = code_tiles(j)
        for number in range(room // TILE + 1):

            @pl.when(tiles == number)
            def _(number=number):
                if number == 0:
                    total[rows, :] = jnp.zeros((cands, HEAD), BF16)
                    return
                at = pl.ds(base, number * TILE)
                scores = lax.dot_general(
                    asked[rows, :],
                    packed[at, :HEAD],
                    (((1,), (1,)), ((), ())),
                    preferred_element_type=F32,
                )
                h = scores * half
                weights = (h + h * jnp.tanh(h)).astype(BF16)
                sums = jnp.dot(weights, packed[at, HEAD:], preferred_element_type=F32)
                total[rows, :] = sums.astype(BF16)

        return carry

    lax.fori_loop(0, codes, one_code, 0)
    for j, (array, at) in enumerate(sink):
        outs[array][at : at + cands, :] = total[j * cands : (j + 1) * cands, :]


def attend(pos, counts, kvs, arrays, where, groups, cands, events, room):
    codes = [c for group in groups for c in group]
    sink = [(g, j * cands) for g, group in enumerate(groups) for j in range(len(group))]
    used = sorted({where[c][0] for c in codes})
    source = [(used.index(where[c][0]), where[c][1]) for c in codes]
    queries = [arrays[a] for a in used]
    rows = sum(kv.shape[0] for kv in kvs)
    n_req = counts.shape[0]
    share = len(codes) / n_req
    vmem = pl.BlockSpec(memory_space=pltpu.VMEM)
    smem = pl.BlockSpec(memory_space=pltpu.SMEM)
    return pl.pallas_call(
        functools.partial(attend_kernel, source, sink, events, room),
        in_specs=[smem] * 3 + [vmem] * (len(kvs) + len(queries)),
        out_specs=[vmem] * len(groups),
        out_shape=[jax.ShapeDtypeStruct((len(g) * cands, HEAD), BF16) for g in groups],
        scratch_shapes=[
            pltpu.VMEM((n_req * room, 2 * HEAD), BF16),
            pltpu.VMEM((len(codes) * cands, HEAD), BF16),
            pltpu.VMEM((len(codes) * cands, HEAD), BF16),
        ],
        compiler_params=room_for(
            ((n_req * room + rows, 2 * HEAD), BF16),
            ((5 * len(codes) * cands, HEAD), BF16),
            ((2, cands, room), F32),
        ),
        cost_estimate=cost(
            8 * rows * cands * HEAD * share,
            4 * rows * HEAD + 4 * len(codes) * cands * HEAD,
            rows * cands * share,
        ),
    )(pos, counts, jnp.array(codes, dtype=jnp.int32), *kvs, *queries)


def finish_kernel(me_ref, cand_ref, gate_ref, w_ref, *refs):
    parts, out_ref = refs[:-1], refs[-1]
    count, _, cols = gate_ref.shape
    width = cand_ref.shape[1]
    each = len(parts) // count
    values = [
        jnp.concatenate([p[...].astype(F32) for p in parts[k * each : (k + 1) * each]], axis=1)
        for k in range(count)
    ]
    mean = sum(jnp.sum(v, axis=1, keepdims=True) for v in values) / width
    values = [v - mean for v in values]
    square = sum(jnp.sum(v * v, axis=1, keepdims=True) for v in values)
    scale = lax.rsqrt(square / width + 1e-05)
    total = cand_ref[...].astype(F32)
    for k, v in enumerate(values):
        mixed = (v * scale * gate_ref[k]).astype(BF16)
        rows = pl.ds(pl.multiple_of((k ^ me_ref[0]) * cols, cols), cols)
        total += jnp.dot(mixed, w_ref[rows, :], preferred_element_type=F32)
    out_ref[...] = total.astype(BF16)


def finish(me, candidates, gate, w_out, parts):
    rows, width = candidates.shape
    vmem = pl.BlockSpec(memory_space=pltpu.VMEM)
    return pl.pallas_call(
        finish_kernel,
        in_specs=[pl.BlockSpec(memory_space=pltpu.SMEM)] + [vmem] * (3 + len(parts)),
        out_specs=vmem,
        out_shape=jax.ShapeDtypeStruct((rows, width), BF16),
        compiler_params=room_for(((width, width), BF16), ((8, rows, width), F32)),
        cost_estimate=cost(2 * rows * width * width, 2 * width * width + 10 * rows * width),
        name="finish",
    )(me, candidates, gate, w_out, *parts)


def stages(count, inner_first):
    outer = []
    bit = count // 2
    while bit >= 2:
        outer.append(2 * bit - 2)
        bit //= 2
    inner = [1] if count > 1 else []
    held, plan = [0], []

    def step(mask, codes):
        plan.append((mask, tuple(codes)))
        held.extend(c ^ mask for c in codes)

    if inner_first:
        for mask in inner + outer:
            step(mask, list(held))
        return plan
    for mask in outer[:-1]:
        step(mask, list(held))
    early = list(held)
    if outer:
        if inner:
            plan.append((1, tuple(early)))
        step(outer[-1], early)
    late = [c for c in held if c not in early] or early
    if inner:
        plan.append((1, tuple(late)))
    return plan


def joined(pieces):
    return pieces[0] if len(pieces) == 1 else jnp.concatenate(pieces, axis=0)


def gather_plan(count, head):
    return stages(count, head % 2 == 1)


def scatter_plan(count):
    return stages(count, False)


def gather_queries(own, plan):
    cands = own.shape[0]
    arrays, where = [own], {0: (0, 0)}
    for mask, codes in plan:
        pieces = [arrays[where[c][0]][where[c][1] : where[c][1] + cands] for c in codes]
        arrays.append(swap(joined(pieces), "req", mask))
        for j, c in enumerate(codes):
            where[c ^ mask] = (len(arrays) - 1, j * cands)
    return arrays, where


def scatter_sums(plan, groups, arrays, cands):
    whole = {tuple(g): a for g, a in zip(groups, arrays)}
    held = {}
    for group, array in zip(groups, arrays):
        for j, c in enumerate(group):
            held[c] = [(array, j * cands)]
    for number in reversed(range(len(plan))):
        mask, codes = plan[number]
        away = tuple(c ^ mask for c in codes)
        if away in whole:
            sent = whole[away]
        else:
            sums = [sum(a[at : at + cands].astype(F32) for a, at in held[c]) for c in away]
            sent = joined([part.astype(BF16) for part in sums])
        got = swap(sent, "req", mask)
        whole = {g: a for g, a in whole.items() if not set(g) & set(codes)}
        for j, c in enumerate(codes):
            held[c].append((got, j * cands))
    return held[0]


def total_kernel(starts, *refs):
    arrays, outs = refs[: len(starts)], refs[len(starts) :]
    mine = outs[0].shape[0]
    for k, out in enumerate(outs):
        rows = [slice(at + k * mine, at + (k + 1) * mine) for at in starts]
        total = sum(ref[r, :].astype(F32) for ref, r in zip(arrays, rows))
        out[...] = total.astype(out.dtype)


def add_up(terms, cands, count):
    vmem = pl.BlockSpec(memory_space=pltpu.VMEM)
    mine = cands // count
    kinds = [F32] + [BF16] * (count - 1)
    return pl.pallas_call(
        functools.partial(total_kernel, [at for _, at in terms]),
        in_specs=[vmem] * len(terms),
        out_specs=[vmem] * count,
        out_shape=[jax.ShapeDtypeStruct((mine, HEAD), kind) for kind in kinds],
        compiler_params=room_for(*[(a.shape, a.dtype) for a, _ in terms], ((cands, HEAD), F32)),
        cost_estimate=cost(len(terms) * cands * HEAD, 4 * len(terms) * cands * HEAD),
    )(*[a for a, _ in terms])


def on_device(history, block_owner, candidates, w_kv, w_qu, w_out):
    n_req, n_ctx = lax.axis_size("req"), lax.axis_size("ctx")
    rows, width = history.shape
    blocks = block_owner.shape[0]
    events = rows // blocks
    mine = candidates.shape[0]
    cands = mine * n_ctx
    each = width // HEAD // n_ctx
    room = -(-n_ctx * (2 * blocks // n_req) * events // TILE) * TILE
    me_ctx = lax.axis_index("ctx").astype(jnp.int32).reshape(1)
    me_req = lax.axis_index("req").astype(jnp.int32)

    made = project_queries(me_ctx, candidates, w_qu, block_owner, n_ctx)
    arrived = [made[0]] + [swap(made[k], "ctx", k) for k in range(1, n_ctx)]

    far = list(range(n_ctx // 2, n_ctx))
    near = list(range(0, n_ctx // 2))
    made_far = project_keys_values(me_ctx, history, w_kv, n_ctx, far)
    made_near = project_keys_values(me_ctx, history, w_kv, n_ctx, near)
    kvs = []
    for h in range(each):
        kvs.append(
            [
                heads[h] if k == 0 else swap(heads[h], "ctx", k)
                for k, heads in zip(near + far, made_near + made_far)
            ]
        )

    asked, owners = assemble(arrived, mine, each, blocks)
    owners = owners.reshape(-1)
    code = owners ^ me_req
    total_blocks = n_ctx * blocks
    order = jnp.arange(total_blocks, dtype=jnp.int32)
    same = code[:, None] == code[None, :]
    rank = jnp.sum((same & (order[None, :] < order[:, None])).astype(jnp.int32), axis=1)
    pos = code * (room // events) + rank
    counts = jnp.sum(
        (code[None, :] == jnp.arange(n_req, dtype=jnp.int32)[:, None]).astype(jnp.int32), axis=1
    )

    gate = project_gate(me_ctx, candidates, w_qu, n_ctx)

    parts = [[None] * each for _ in range(n_ctx)]
    for h in range(each):
        arrays, where = gather_queries(asked[h], gather_plan(n_req, h))
        plan = scatter_plan(n_req)
        groups = [[c ^ mask for c in codes] for mask, codes in plan] + [[0]]
        sums = {}
        for call in calls_of(n_req, h):
            made = attend(
                pos, counts, kvs[h], arrays, where, [groups[i] for i in call],
                cands, events, room,
            )
            sums.update(zip(call, made))
        terms = scatter_sums(plan, groups, [sums[i] for i in range(len(groups))], cands)
        pieces = add_up(terms, cands, n_ctx)
        for k, piece in enumerate(pieces):
            parts[k][h] = piece if k == 0 else swap(piece, "ctx", k)
    return finish(me_ctx, candidates, gate, w_out, [p for row in parts for p in row])


def calls_of(count, head):
    last = len(scatter_plan(count)) - 1
    rest = [i for i in range(last + 2) if i != last]
    return [rest, [last]] if head % 2 == 0 else [[last], rest]


def solution(mesh):
    placed = (
        P(("req", "ctx"), None),
        P(("req", "ctx"), None),
        P(("req", "ctx"), None),
        P(),
        P(),
        P(),
    )
    return jax.shard_map(
        on_device, mesh=mesh, in_specs=placed, out_specs=P(("req", "ctx"), None), check_vma=False
    )
```

```python
import functools

import jax
import jax.numpy as jnp
from jax import lax
from jax.experimental import pallas as pl
from jax.experimental.pallas import tpu as pltpu
from jax.sharding import PartitionSpec as P


HEAD = 128
TILE = 256
VMEM = 67043328
BF16 = jnp.bfloat16
F32 = jnp.float32


def silu(v):
    h = 0.5 * v
    return h + h * jnp.tanh(h)


def swap(value, axis, mask):
    count = lax.axis_size(axis)
    return lax.ppermute(value, axis, [(i, i ^ mask) for i in range(count)])


def scalar_grid(grid, in_specs, out_specs, scratch_shapes=()):
    return pltpu.PrefetchScalarGridSpec(
        num_scalar_prefetch=1,
        grid=grid,
        in_specs=in_specs,
        out_specs=out_specs,
        scratch_shapes=scratch_shapes,
    )


def room_for(*arrays, extra=0):
    total = extra
    for shape, kind in arrays:
        size = jnp.dtype(kind).itemsize
        for dim in shape:
            size *= dim
        total += size
    return pltpu.CompilerParams(vmem_limit_bytes=int(total * 1.25) + (2 << 20))


def cost(flops, moved, transcendentals=0):
    return pl.CostEstimate(
        flops=int(flops), bytes_accessed=int(moved), transcendentals=int(transcendentals)
    )


def query_kernel(me_ref, cand_hbm, w_hbm, owner_ref, *refs):
    outs, (cand, weight, made, sems) = refs[:-4], refs[-4:]
    rows = cand.shape[0]
    parts = len(outs)
    cols = outs[0].shape[1]
    blocks = owner_ref.shape[1]
    extra = outs[0].shape[0] - rows
    width = cand.shape[1]
    step = width // parts
    fetch = [pltpu.make_async_copy(cand_hbm, cand, sems.at[parts])]
    for k in range(parts):
        at = pl.ds(k * step, step)
        fetch.append(
            pltpu.make_async_copy(w_hbm.at[at, pl.ds(0, width)], weight.at[at, :], sems.at[k])
        )
    for copy in fetch:
        copy.start()
    owners = jnp.broadcast_to(owner_ref[...].astype(F32), (extra, blocks)).astype(BF16)
    for out in outs:
        out[rows:, :] = jnp.zeros((extra, cols), BF16)
        out[rows:, :blocks] = owners
    fetch[0].wait()
    projected = None
    for k in range(parts):
        fetch[k + 1].wait()
        at = slice(k * step, (k + 1) * step)
        part = jnp.dot(cand[:, at], weight[at, :], preferred_element_type=F32)
        projected = part if projected is None else projected + part
    made[...] = silu(projected).astype(BF16)
    for k, out in enumerate(outs):
        at = pl.multiple_of((k ^ me_ref[0]) * cols, cols)
        out[:rows, :] = made[:, pl.ds(at, cols)]


def project_queries(me, candidates, w_qu, block_owner, parts):
    rows, width = candidates.shape
    cols = width // parts
    blocks = block_owner.shape[0]
    extra = 16
    vmem = pl.BlockSpec(memory_space=pltpu.VMEM)
    hbm = pl.BlockSpec(memory_space=pltpu.HBM)
    return pl.pallas_call(
        query_kernel,
        in_specs=[pl.BlockSpec(memory_space=pltpu.SMEM), hbm, hbm, vmem],
        out_specs=[vmem] * parts,
        out_shape=[jax.ShapeDtypeStruct((rows + extra, cols), BF16)] * parts,
        scratch_shapes=[
            pltpu.VMEM((rows, width), BF16),
            pltpu.VMEM((width, width), BF16),
            pltpu.VMEM((rows, width), BF16),
            pltpu.SemaphoreType.DMA((parts + 1,)),
        ],
        compiler_params=pltpu.CompilerParams(vmem_limit_bytes=VMEM - 2 * w_qu.size),
        cost_estimate=cost(2 * rows * width * width, 2 * width * width + 4 * rows * width),
        name="queries",
    )(me, candidates, w_qu, block_owner.reshape(1, blocks))


def assemble_kernel(count, *refs):
    arrived, outs, owner_ref = refs[:count], refs[count:-1], refs[-1]
    blocks = owner_ref.shape[1]
    rows = outs[0].shape[0] // count
    for k, ref in enumerate(arrived):
        for h, out in enumerate(outs):
            out[k * rows : (k + 1) * rows, :] = ref[:rows, h * HEAD : (h + 1) * HEAD]
        below = ref[rows : rows + 16, :HEAD].astype(F32)
        owner_ref[k : k + 1, :] = below[:1, :blocks].astype(jnp.int32)


def assemble(arrived, rows, each, blocks):
    count = len(arrived)
    vmem = pl.BlockSpec(memory_space=pltpu.VMEM)
    made = pl.pallas_call(
        functools.partial(assemble_kernel, count),
        in_specs=[vmem] * count,
        out_specs=[vmem] * (each + 1),
        out_shape=[jax.ShapeDtypeStruct((count * rows, HEAD), BF16)] * each
        + [jax.ShapeDtypeStruct((count, blocks), jnp.int32)],
        compiler_params=room_for(((4, count * rows, each * HEAD), BF16)),
        cost_estimate=cost(0, 4 * count * rows * each * HEAD),
        name="assemble",
    )(*arrived)
    return made[:each], made[each]


def gate_kernel(_, cand_ref, w_ref, out_ref):
    out_ref[0] = silu(jnp.dot(cand_ref[...], w_ref[...], preferred_element_type=F32))


def project_gate(me, candidates, w_qu, parts):
    rows, width = candidates.shape
    cols = width // parts
    return pl.pallas_call(
        gate_kernel,
        grid_spec=scalar_grid(
            (parts,),
            [
                pl.BlockSpec((rows, width), lambda k, m: (0, 0)),
                pl.BlockSpec((width, cols), lambda k, m: (0, parts + (k ^ m[0]))),
            ],
            pl.BlockSpec((1, rows, cols), lambda k, m: (k, 0, 0)),
        ),
        out_shape=jax.ShapeDtypeStruct((parts, rows, cols), F32),
        compiler_params=room_for(
            ((2, width, cols), BF16), ((2, rows, width), BF16), ((4, rows, cols), F32)
        ),
        cost_estimate=cost(2 * rows * width * width, 2 * width * width + 6 * rows * width),
        name="gate",
    )(me, candidates, w_qu)


def keys_values_kernel(count, each, _, hist_ref, *refs):
    weights, outs = refs[: 2 * count], refs[2 * count :]
    for k in range(count):
        keys = silu(jnp.dot(hist_ref[...], weights[2 * k][...], preferred_element_type=F32))
        values = jnp.dot(hist_ref[...], weights[2 * k + 1][...], preferred_element_type=F32)
        for h in range(each):
            out = outs[k * each + h]
            out[:, :HEAD] = keys[:, h * HEAD : (h + 1) * HEAD].astype(BF16)
            out[:, HEAD:] = values[:, h * HEAD : (h + 1) * HEAD].astype(BF16)


def project_keys_values(me, history, w_kv, parts, ks):
    rows, width = history.shape
    cols = width // parts
    each = cols // HEAD
    count = len(ks)
    step = rows // 2

    def weight(k, side):
        return pl.BlockSpec((width, cols), lambda r, m: (0, side * parts + (k ^ m[0])))

    made = pl.pallas_call(
        functools.partial(keys_values_kernel, count, each),
        grid_spec=scalar_grid(
            (rows // step,),
            [pl.BlockSpec((step, width), lambda r, m: (r, 0))]
            + [weight(k, side) for k in ks for side in range(2)],
            [pl.BlockSpec((step, 2 * HEAD), lambda r, m: (r, 0))] * (count * each),
        ),
        out_shape=[jax.ShapeDtypeStruct((rows, 2 * HEAD), BF16)] * (count * each),
        cost_estimate=cost(
            4 * rows * width * cols * count,
            2 * rows * width + 4 * width * cols * count + 4 * rows * cols * count,
        ),
        compiler_params=room_for(
            ((2, step, width), BF16),
            ((4 * count, width, cols), BF16),
            ((4 * count, step, cols), BF16),
            ((2, step, cols), F32),
        ),
    )(me, history, *[w_kv] * (2 * count))
    return [made[k * each : (k + 1) * each] for k in range(count)]


def attend_kernel(source, sink, events, room, pos_ref, count_ref, code_ref, *refs):
    codes = len(source)
    n_q = 1 + max(a for a, _ in source)
    n_out = 1 + max(a for a, _ in sink)
    n_kv = len(refs) - n_q - n_out - 3
    kvs, queries = refs[:n_kv], refs[n_kv : n_kv + n_q]
    outs = refs[n_kv + n_q : n_kv + n_q + n_out]
    packed, asked, total = refs[n_kv + n_q + n_out :]
    blocks = kvs[0].shape[0] // events
    cands = asked.shape[0] // codes
    half = 0.5 * HEAD ** (-0.5)

    def code_tiles(j):
        return lax.div(count_ref[code_ref[j]] * events + (TILE - 1), TILE)

    for j in range(codes):
        at = code_ref[j] * room + (lax.max(code_tiles(j), 1) - 1) * TILE
        packed[pl.ds(pl.multiple_of(at, TILE), TILE), :] = jnp.zeros((TILE, 2 * HEAD), BF16)
    for s, kv in enumerate(kvs):

        def place(b, carry, s=s, kv=kv):
            at = pl.multiple_of(pos_ref[s * blocks + b] * events, events)
            packed[pl.ds(at, events), :] = kv[pl.ds(pl.multiple_of(b * events, events), events), :]
            return carry

        lax.fori_loop(0, blocks, place, 0, unroll=8)
    for j, (array, at) in enumerate(source):
        asked[j * cands : (j + 1) * cands, :] = queries[array][at : at + cands, :]

    def one_code(j, carry):
        code = code_ref[j]
        base = pl.multiple_of(code * room, TILE)
        rows = pl.ds(pl.multiple_of(j * cands, cands), cands)
        tiles = code_tiles(j)
        for number in range(room // TILE + 1):

            @pl.when(tiles == number)
            def _(number=number):
                if number == 0:
                    total[rows, :] = jnp.zeros((cands, HEAD), BF16)
                    return
                at = pl.ds(base, number * TILE)
                scores = lax.dot_general(
                    asked[rows, :],
                    packed[at, :HEAD],
                    (((1,), (1,)), ((), ())),
                    preferred_element_type=F32,
                )
                h = scores * half
                weights = (h + h * jnp.tanh(h)).astype(BF16)
                sums = jnp.dot(weights, packed[at, HEAD:], preferred_element_type=F32)
                total[rows, :] = sums.astype(BF16)

        return carry

    lax.fori_loop(0, codes, one_code, 0)
    for j, (array, at) in enumerate(sink):
        outs[array][at : at + cands, :] = total[j * cands : (j + 1) * cands, :]


def attend(pos, counts, kvs, arrays, where, groups, cands, events, room):
    codes = [c for group in groups for c in group]
    sink = [(g, j * cands) for g, group in enumerate(groups) for j in range(len(group))]
    used = sorted({where[c][0] for c in codes})
    source = [(used.index(where[c][0]), where[c][1]) for c in codes]
    queries = [arrays[a] for a in used]
    rows = sum(kv.shape[0] for kv in kvs)
    n_req = counts.shape[0]
    share = len(codes) / n_req
    vmem = pl.BlockSpec(memory_space=pltpu.VMEM)
    smem = pl.BlockSpec(memory_space=pltpu.SMEM)
    return pl.pallas_call(
        functools.partial(attend_kernel, source, sink, events, room),
        in_specs=[smem] * 3 + [vmem] * (len(kvs) + len(queries)),
        out_specs=[vmem] * len(groups),
        out_shape=[jax.ShapeDtypeStruct((len(g) * cands, HEAD), BF16) for g in groups],
        scratch_shapes=[
            pltpu.VMEM((n_req * room, 2 * HEAD), BF16),
            pltpu.VMEM((len(codes) * cands, HEAD), BF16),
            pltpu.VMEM((len(codes) * cands, HEAD), BF16),
        ],
        compiler_params=room_for(
            ((n_req * room + rows, 2 * HEAD), BF16),
            ((5 * len(codes) * cands, HEAD), BF16),
            ((2, cands, room), F32),
        ),
        cost_estimate=cost(
            8 * rows * cands * HEAD * share,
            4 * rows * HEAD + 4 * len(codes) * cands * HEAD,
            rows * cands * share,
        ),
    )(pos, counts, jnp.array(codes, dtype=jnp.int32), *kvs, *queries)


def finish_kernel(me_ref, cand_ref, gate_ref, w_ref, *refs):
    parts, out_ref = refs[:-1], refs[-1]
    count, _, cols = gate_ref.shape
    width = cand_ref.shape[1]
    each = len(parts) // count
    values = [
        jnp.concatenate([p[...].astype(F32) for p in parts[k * each : (k + 1) * each]], axis=1)
        for k in range(count)
    ]
    mean = sum(jnp.sum(v, axis=1, keepdims=True) for v in values) / width
    values = [v - mean for v in values]
    square = sum(jnp.sum(v * v, axis=1, keepdims=True) for v in values)
    scale = lax.rsqrt(square / width + 1e-05)
    total = cand_ref[...].astype(F32)
    for k, v in enumerate(values):
        mixed = (v * scale * gate_ref[k]).astype(BF16)
        rows = pl.ds(pl.multiple_of((k ^ me_ref[0]) * cols, cols), cols)
        total += jnp.dot(mixed, w_ref[rows, :], preferred_element_type=F32)
    out_ref[...] = total.astype(BF16)


def finish(me, candidates, gate, w_out, parts):
    rows, width = candidates.shape
    vmem = pl.BlockSpec(memory_space=pltpu.VMEM)
    return pl.pallas_call(
        finish_kernel,
        in_specs=[pl.BlockSpec(memory_space=pltpu.SMEM)] + [vmem] * (3 + len(parts)),
        out_specs=vmem,
        out_shape=jax.ShapeDtypeStruct((rows, width), BF16),
        compiler_params=room_for(((width, width), BF16), ((8, rows, width), F32)),
        cost_estimate=cost(2 * rows * width * width, 2 * width * width + 10 * rows * width),
        name="finish",
    )(me, candidates, gate, w_out, *parts)


def stages(count, inner_first):
    outer = []
    bit = count // 2
    while bit >= 2:
        outer.append(2 * bit - 2)
        bit //= 2
    inner = [1] if count > 1 else []
    held, plan = [0], []

    def step(mask, codes):
        plan.append((mask, tuple(codes)))
        held.extend(c ^ mask for c in codes)

    if inner_first:
        for mask in inner + outer:
            step(mask, list(held))
        return plan
    for mask in outer[:-1]:
        step(mask, list(held))
    early = list(held)
    if outer:
        if inner:
            plan.append((1, tuple(early)))
        step(outer[-1], early)
    late = [c for c in held if c not in early] or early
    if inner:
        plan.append((1, tuple(late)))
    return plan


def joined(pieces):
    return pieces[0] if len(pieces) == 1 else jnp.concatenate(pieces, axis=0)


def gather_plan(count, head):
    return stages(count, head % 2 == 1)


def scatter_plan(count, head):
    if head % 2 == 1:
        return stages(count, False)
    outer = [mask for mask, codes in stages(count, True) if mask != 1]
    plan, main, side = [], [0], [1]
    for mask in outer[:-1]:
        plan.append((mask, tuple(main)))
        main += [c ^ mask for c in main]
    plan.append((1, (0,)))
    for mask in outer[:-1]:
        plan.append((mask, tuple(side)))
        side += [c ^ mask for c in side]
    for mask in outer[-1:]:
        plan.append((mask, tuple(main)))
        plan.append((1, tuple(c ^ mask for c in main)))
    return plan


def gather_queries(own, plan):
    cands = own.shape[0]
    arrays, where = [own], {0: (0, 0)}
    for mask, codes in plan:
        pieces = [arrays[where[c][0]][where[c][1] : where[c][1] + cands] for c in codes]
        arrays.append(swap(joined(pieces), "req", mask))
        for j, c in enumerate(codes):
            where[c ^ mask] = (len(arrays) - 1, j * cands)
    return arrays, where


def scatter_sums(plan, groups, arrays, cands):
    whole = {tuple(g): a for g, a in zip(groups, arrays)}
    held = {}
    for group, array in zip(groups, arrays):
        for j, c in enumerate(group):
            held[c] = [(array, j * cands)]
    for number in reversed(range(len(plan))):
        mask, codes = plan[number]
        away = tuple(c ^ mask for c in codes)
        if away in whole:
            sent = whole[away]
        else:
            sums = [sum(a[at : at + cands].astype(F32) for a, at in held[c]) for c in away]
            sent = joined([part.astype(BF16) for part in sums])
        got = swap(sent, "req", mask)
        whole = {g: a for g, a in whole.items() if not set(g) & set(codes)}
        for j, c in enumerate(codes):
            held[c].append((got, j * cands))
    return held[0]


def total_kernel(starts, *refs):
    arrays, outs = refs[: len(starts)], refs[len(starts) :]
    mine = outs[0].shape[0]
    for k, out in enumerate(outs):
        rows = [slice(at + k * mine, at + (k + 1) * mine) for at in starts]
        total = sum(ref[r, :].astype(F32) for ref, r in zip(arrays, rows))
        out[...] = total.astype(out.dtype)


def add_up(terms, cands, count):
    vmem = pl.BlockSpec(memory_space=pltpu.VMEM)
    mine = cands // count
    kinds = [F32] + [BF16] * (count - 1)
    return pl.pallas_call(
        functools.partial(total_kernel, [at for _, at in terms]),
        in_specs=[vmem] * len(terms),
        out_specs=[vmem] * count,
        out_shape=[jax.ShapeDtypeStruct((mine, HEAD), kind) for kind in kinds],
        compiler_params=room_for(*[(a.shape, a.dtype) for a, _ in terms], ((cands, HEAD), F32)),
        cost_estimate=cost(len(terms) * cands * HEAD, 4 * len(terms) * cands * HEAD),
    )(*[a for a, _ in terms])


def on_device(history, block_owner, candidates, w_kv, w_qu, w_out):
    n_req, n_ctx = lax.axis_size("req"), lax.axis_size("ctx")
    rows, width = history.shape
    blocks = block_owner.shape[0]
    events = rows // blocks
    mine = candidates.shape[0]
    cands = mine * n_ctx
    each = width // HEAD // n_ctx
    room = -(-n_ctx * (2 * blocks // n_req) * events // TILE) * TILE
    me_ctx = lax.axis_index("ctx").astype(jnp.int32).reshape(1)
    me_req = lax.axis_index("req").astype(jnp.int32)

    made = project_queries(me_ctx, candidates, w_qu, block_owner, n_ctx)
    arrived = [made[0]] + [swap(made[k], "ctx", k) for k in range(1, n_ctx)]

    far = list(range(n_ctx // 2, n_ctx))
    near = list(range(0, n_ctx // 2))
    made_far = project_keys_values(me_ctx, history, w_kv, n_ctx, far)
    made_near = project_keys_values(me_ctx, history, w_kv, n_ctx, near)
    kvs = []
    for h in range(each):
        kvs.append(
            [
                heads[h] if k == 0 else swap(heads[h], "ctx", k)
                for k, heads in zip(near + far, made_near + made_far)
            ]
        )

    asked, owners = assemble(arrived, mine, each, blocks)
    owners = owners.reshape(-1)
    code = owners ^ me_req
    total_blocks = n_ctx * blocks
    order = jnp.arange(total_blocks, dtype=jnp.int32)
    same = code[:, None] == code[None, :]
    rank = jnp.sum((same & (order[None, :] < order[:, None])).astype(jnp.int32), axis=1)
    pos = code * (room // events) + rank
    counts = jnp.sum(
        (code[None, :] == jnp.arange(n_req, dtype=jnp.int32)[:, None]).astype(jnp.int32), axis=1
    )

    gate = project_gate(me_ctx, candidates, w_qu, n_ctx)

    parts = [[None] * each for _ in range(n_ctx)]
    for h in range(each):
        arrays, where = gather_queries(asked[h], gather_plan(n_req, h))
        plan = scatter_plan(n_req, h)
        groups = [[c ^ mask for c in codes] for mask, codes in plan] + [[0]]
        sums = {}
        for call in calls_of(n_req, h):
            made = attend(
                pos, counts, kvs[h], arrays, where, [groups[i] for i in call],
                cands, events, room,
            )
            sums.update(zip(call, made))
        terms = scatter_sums(plan, groups, [sums[i] for i in range(len(groups))], cands)
        pieces = add_up(terms, cands, n_ctx)
        for k, piece in enumerate(pieces):
            parts[k][h] = piece if k == 0 else swap(piece, "ctx", k)
    return finish(me_ctx, candidates, gate, w_out, [p for row in parts for p in row])


def calls_of(count, head):
    last = len(scatter_plan(count, head)) - 1
    rest = [i for i in range(last + 2) if i != last]
    return [rest, [last]] if head % 2 == 0 else [[last], rest]


def solution(mesh):
    placed = (
        P(("req", "ctx"), None),
        P(("req", "ctx"), None),
        P(("req", "ctx"), None),
        P(),
        P(),
        P(),
    )
    return jax.shard_map(
        on_device, mesh=mesh, in_specs=placed, out_specs=P(("req", "ctx"), None), check_vma=False
    )
```
